128 devices in a mesh: client: 4 (over x_hi, core), blk: 32 (over z, x_lo, y).
Axes of the slice: x: 4 (x_hi: 2, x_lo: 2; x = x_hi * 2 + x_lo), y: 4, z: 4, core: 2. Of those that a mesh axis runs over, the one named last changes fastest.
Arguments:
- activations: bfloat16 [8, 2, 32, 8, 1280], P('client', None, 'blk'), may hold values from -6 to 6
- sample_count: int32 [8], replicated, may hold values from 1 to 2, as said below
- client_weights: bfloat16 [8, 11520, 1280], P('client', 'blk'), may hold values from -6 to 6
Outputs:
- merged_gram: float32 [11520, 11520], P(('blk', 'client'))
- merged_rhs: float32 [11520, 1280], P(('blk', 'client'))
The draws below stay inside these ranges and needn't reach their ends.
Inputs may be any that keep to these rules, and one draw needn't show every extreme that they name: `sample_count`: some client has all 2 slots live in every draw.
All inputs are finite; a program needn't handle non-finite values.
Results may differ from the reference program's by a relative error of at most 0.0029.
Values may be sent and summed in bfloat16 or wider, within the bound.
No kernel may reach another device: no remote copies, remote signals or barrier semaphores. Data moves between devices by JAX's collectives and lax.ppermute only.
A program may use at most 128 MiB of HBM per device.

```python
import jax
import jax.numpy as jnp
from jax import lax

CH = 1280
COUT = 1280
IMG_W = 8
SLOTS = 2
CLIENTS = 8
HH = 32
KK = 11520


def draw_sample_count(key, part):
    first_key, second_key = jax.random.split(jax.random.fold_in(key, 17))
    counts_drawn = jax.random.randint(first_key, (CLIENTS,), 1, SLOTS + 1)
    filled_client = jax.random.randint(second_key, (), 0, CLIENTS)
    positions = jnp.arange(CLIENTS)
    return jnp.where(positions == filled_client, SLOTS, counts_drawn).astype(jnp.int32)


def block_levels(own_key, extent, cuts, low, high):
    def one(dim, shards_of):
        steps = jax.random.uniform(jax.random.fold_in(jax.random.fold_in(own_key, 6), dim), (shards_of,), jnp.float32, low / len(cuts), high / len(cuts))
        return jnp.repeat(jnp.exp(steps), extent[dim] // shards_of).reshape((-1,) + (1,) * (len(extent) - dim - 1))

    loudness = one(*cuts[0])
    for cut in cuts[1:]:
        loudness = loudness * one(*cut)
    return loudness


def normal_values(own_key, dims, deviation, bound, shards=(), kind=jnp.bfloat16):
    entries = jax.random.normal(own_key, dims, jnp.float32) * deviation
    if len(shards) > 0:
        entries = block_levels(own_key, dims, shards, -0.22, 0.18) * entries
    return jnp.clip(entries, min=-bound, max=bound).astype(kind)


def setup_inputs(seed: int = 0) -> dict:
    key_list = jax.random.split(jax.random.key(seed), 4)
    activations = normal_values(key_list[0], (CLIENTS, SLOTS, HH, IMG_W, CH), 1.0, 6.0, ((0, 4), (2, 32)))
    sample_count = draw_sample_count(jax.random.fold_in(key_list[3], 71), 0)
    client_weights = normal_values(key_list[2], (CLIENTS, KK, COUT), 1.0, 6.0, ((0, 4), (1, 32)))
    return {"activations": activations, "sample_count": sample_count, "client_weights": client_weights}


keep_off = 0.9


def patch_rows(images):
    groups, slots, img_height, img_width, channel_count = images.shape
    padded = jnp.pad(images, [(0, 0), (0, 0), (1, 1), (1, 1), (0, 0)])
    shifted = [padded[:, :, row_off:row_off + img_height, col_off:col_off + img_width, :] for row_off in range(3) for col_off in range(3)]
    stacked = jnp.stack(shifted, axis=-1)
    return stacked.reshape(groups, slots * img_height * img_width, channel_count * 9)


def reference(activations, sample_count, client_weights):
    live = lax.broadcasted_iota(jnp.int32, (CLIENTS, SLOTS), 1) < sample_count[:, None]
    masked = jnp.where(live[:, :, None, None, None], activations, jnp.zeros_like(activations))
    patches = patch_rows(masked)
    scales = 1.0 / (CLIENTS * sample_count.astype(jnp.float32) * (HH * IMG_W))

    def accumulate(running, inputs):
        patch_one, scale_one, weight_one = inputs
        gram_part = jnp.dot(patch_one.T, patch_one, preferred_element_type=jnp.float32)
        outputs = jnp.dot(patch_one, weight_one, preferred_element_type=jnp.float32).astype(jnp.bfloat16)
        cross = jnp.dot(patch_one.T, outputs, preferred_element_type=jnp.float32)
        diag_part = jnp.sum(jnp.square(patch_one.astype(jnp.float32)), axis=0)
        rhs_part = keep_off * cross + (1.0 - keep_off) * diag_part[:, None] * weight_one.astype(jnp.float32)
        return (running[0] + scale_one * gram_part, running[1] + scale_one * rhs_part), None

    start_state = (jnp.zeros((KK, KK), jnp.float32), jnp.zeros((KK, COUT), jnp.float32))
    (summed, merged_rhs), _ = lax.scan(accumulate, start_state, (patches, scales, client_weights))
    on_diag = lax.broadcasted_iota(jnp.int32, (KK, KK), 0) == lax.broadcasted_iota(jnp.int32, (KK, KK), 1)
    merged_gram = jnp.where(on_diag, summed, keep_off * summed)
    return merged_gram, merged_rhs
```

```python
import jax
import jax.numpy as jnp
import numpy as np
from jax import lax
from jax.experimental import pallas as pl
from jax.experimental.pallas import tpu as pltpu
from jax.sharding import PartitionSpec as P

keep_off = 0.9
AXES = ("client", "blk")
CHIPS = 4
ROWS = 32
CH = 1280
LANES = 1024
TAPS = 9
OWN = 10
MPAD = 96


def split_device(index):
    client, blk = divmod(index, 32)
    x_hi, core = divmod(client, 2)
    z, rest = divmod(blk, 8)
    x_lo, y = divmod(rest, 4)
    return x_hi * 2 + x_lo, y, z, core


def join_device(x, y, z, core):
    return ((x // 2) * 2 + core) * 32 + z * 8 + (x % 2) * 4 + y


def take_from(value, offset):
    pairs = []
    for dst in range(128):
        x, y, z, core = split_device(dst)
        src = join_device((x + offset[0]) % 4, (y + offset[1]) % 4, (z + offset[2]) % 4, core)
        pairs.append((src, dst))
    return lax.ppermute(value, AXES, pairs)


def vec_add(*vectors):
    return tuple(sum(parts) % 4 for parts in zip(*vectors))


STEP = (1, 0, 1)
FIRST = [tuple(k * s % 4 for s in STEP) for k in range(4)]
SECOND = [(0, 0, 0), (1, 1, 3), (0, 2, 0), (3, 3, 1)]
HEAD = [vec_add(g, f) for g in SECOND[:2] for f in FIRST]
TAIL = [vec_add(g, f) for g in SECOND[2:] for f in FIRST]
LAST = [((1, 0, 0), 0), ((0, 0, 3), 1), ((3, 0, 0), 0), ((0, 0, 1), 1), ((0, 1, 0), 0), ((0, 3, 0), 0)]
SOURCES = list(HEAD) + list(TAIL)
for away, part in LAST:
    SOURCES += [vec_add(away, o) for o in (TAIL if part else HEAD)]
assert len(set(SOURCES)) == 64


def gather_chips(block):
    level = jnp.concatenate([block] + [take_from(block, o) for o in FIRST[1:]], axis=0)
    level = jnp.concatenate([level] + [take_from(level, o) for o in SECOND[1:]], axis=0)
    halves = (level[:256], level[256:])
    return [level] + [take_from(halves[part], away) for away, part in LAST]


def assemble_kernel(slots, *refs):
    sources, out, sems = refs[:7], refs[7], refs[8]
    copies = []
    for t in range(64):
        if t < 16:
            src = sources[0].at[pl.ds(t * ROWS, ROWS)]
        else:
            piece, row = divmod(t - 16, 8)
            src = sources[1 + piece].at[pl.ds(row * ROWS, ROWS)]
        copies.append(pltpu.make_async_copy(src, out.at[slots[t]], sems.at[t]))
    for copy in copies:
        copy.start()
    for copy in copies:
        copy.wait()


def assemble(slots, pieces):
    return pl.pallas_call(
        assemble_kernel,
        out_shape=jax.ShapeDtypeStruct((64, ROWS, CH), jnp.bfloat16),
        grid_spec=pltpu.PrefetchScalarGridSpec(
            num_scalar_prefetch=1,
            grid=(1,),
            in_specs=[pl.BlockSpec(memory_space=pl.ANY)] * 7,
            out_specs=pl.BlockSpec(memory_space=pl.ANY),
            scratch_shapes=[pltpu.SemaphoreType.DMA((64,))],
        ),
        name="assemble",
    )(slots, *pieces)


def shift_lanes(value, row_off, col_off):
    amount = 32 * row_off + col_off
    moved = pltpu.roll(value, (-amount) % LANES, 1) if amount else value
    lane = lax.broadcasted_iota(jnp.int32, (1, LANES), 1)
    row = lane // 32 + row_off
    col = lane % 8 + col_off
    inside = (row >= 0) & (row < 32) & (col >= 0) & (col < 8)
    return jnp.where(inside, moved, 0.0)


def gram_kernel(first_ref, own_ref, other_ref, pick_ref, order_ref, spread_ref, scale_ref, out_ref, left, acc, high):
    pick = pick_ref[...]
    order = order_ref[...]
    for group in range(4):
        source = own_ref if group < 2 else other_ref
        pixels = source[pl.ds((group % 2) * LANES, LANES), :]
        slab = lax.dot_general(pick, pixels, (((1,), (1,)), ((), ())), preferred_element_type=jnp.float32)
        shifted = [shift_lanes(slab, t // 3 - 1, t % 3 - 1) for t in range(TAPS)]
        stacked = jnp.concatenate(shifted, axis=0).astype(jnp.bfloat16)
        patch = jnp.dot(order, stacked, preferred_element_type=jnp.float32)
        patch = patch * scale_ref[pl.ds(group, 1), :]
        for t in range(TAPS):
            left[pl.ds(t * MPAD, MPAD), pl.ds(group * LANES, LANES)] = shift_lanes(
                patch, 1 - t // 3, 1 - t % 3
            ).astype(jnp.bfloat16)

    @pl.loop(0, 5)
    def _(n):
        lanes = pl.ds(pl.multiple_of(n * 256, 256), 256)
        total = jnp.dot(left[:, pl.ds(0, 2048)], own_ref[:, lanes], preferred_element_type=jnp.float32)
        total += jnp.dot(left[:, pl.ds(2048, 2048)], other_ref[:, lanes], preferred_element_type=jnp.float32)
        acc[:, lanes] = total

    for block in range(10):
        for t in range(TAPS):
            part = acc[pl.ds(t * MPAD, MPAD), pl.ds(block * 128, 128)]
            top = part.astype(jnp.bfloat16)
            high[pl.ds(block * 2 * MPAD, MPAD), pl.ds(t * 128, 128)] = top
            high[pl.ds((block * 2 + 1) * MPAD, MPAD), pl.ds(t * 128, 128)] = (
                part - top.astype(jnp.float32)
            ).astype(jnp.bfloat16)

    first = first_ref[0]

    @pl.loop(0, 6)
    def _(step):
        half = step // 3
        piece = step % 3
        rows = pl.ds(pl.multiple_of(half * 960, 960), 960)
        cols = pl.ds(pl.multiple_of(piece * 384, 128), 384)
        wide = jnp.dot(high[rows, :], spread_ref[:, cols], preferred_element_type=jnp.float32)
        for b in range(5):
            value = wide[b * 192 : b * 192 + 96] + wide[b * 192 + 96 : b * 192 + 192]
            value = value[:90]
            base = half * 5760 + b * 1152 + piece * 384
            row = lax.broadcasted_iota(jnp.int32, value.shape, 0) + first
            col = lax.broadcasted_iota(jnp.int32, value.shape, 1) + base
            out_ref[:, pl.ds(pl.multiple_of(base, 128), 384)] = jnp.where(row == col, value, keep_off * value)


def gram(first, own, other, pick, order, spread, scale):
    whole = pl.BlockSpec(memory_space=pltpu.VMEM)
    return pl.pallas_call(
        gram_kernel,
        out_shape=jax.ShapeDtypeStruct((90, 11520), jnp.float32),
        in_specs=[pl.BlockSpec(memory_space=pltpu.SMEM)] + [whole] * 6,
        out_specs=whole,
        scratch_shapes=[
            pltpu.VMEM((TAPS * MPAD, 4 * LANES), jnp.bfloat16),
            pltpu.VMEM((TAPS * MPAD, CH), jnp.float32),
            pltpu.VMEM((20 * MPAD, TAPS * 128), jnp.bfloat16),
        ],
        compiler_params=pltpu.CompilerParams(vmem_limit_bytes=58 * 1024 * 1024),
        cost_estimate=pl.CostEstimate(flops=20_000_000_000, bytes_accessed=20_000_000, transcendentals=0),
        name="gram",
    )(first, own, other, pick, order, spread, scale)


def body(activations, sample_count, client_weights):
    client_here = lax.axis_index("client")
    blk_here = lax.axis_index("blk")
    x_hi, core = client_here // 2, client_here % 2
    z, x_lo, y = blk_here // 8, (blk_here // 4) % 2, blk_here % 4
    x = x_hi * 2 + x_lo

    counts = sample_count.astype(jnp.float32)
    all_scale = 1.0 / (8 * counts * 256)
    mine = lax.dynamic_slice_in_dim(sample_count, client_here * 2, 2)
    my_scale = lax.dynamic_slice_in_dim(all_scale, client_here * 2, 2)

    packed = client_weights.reshape(2, 40, TAPS, 32, 40).transpose(3, 1, 0, 2, 4).reshape(32, 40, 720)
    tiles = lax.all_to_all(packed, "blk", split_axis=0, concat_axis=0, tiled=True)
    tiles = tiles.reshape(CH, 2, 3, 3, 40)

    live = lax.broadcasted_iota(jnp.int32, (2, 2), 1) < mine[:, None]
    masked = jnp.where(live[:, :, None, None, None], activations, jnp.zeros_like(activations))
    pieces = gather_chips(masked.reshape(ROWS, CH))
    offs = np.array(SOURCES, np.int32)
    src_x, src_y, src_z = (x + offs[:, 0]) % 4, (y + offs[:, 1]) % 4, (z + offs[:, 2]) % 4
    away = (src_x // 2 != x_hi).astype(jnp.int32)
    slots = (away * 32 + src_z * 8 + (src_x % 2) * 4 + src_y).astype(jnp.int32)
    own = assemble(slots, pieces)
    other = lax.ppermute(own, AXES, [(d, d ^ 32) for d in range(128)])

    pixels = own[:32].reshape(32, 2, 2, 8, CH)
    outs = []
    for c in range(2):
        out = lax.conv_general_dilated(
            pixels[:, c], tiles[:, c], (1, 1), ((1, 1), (1, 1)),
            dimension_numbers=("HNWC", "IHWO", "HNWC"), preferred_element_type=jnp.float32,
        ).astype(jnp.bfloat16)
        outs.append(out * my_scale[c].astype(jnp.bfloat16))
    outs = jnp.stack(outs, axis=1).reshape(32, 4, 8, 40)
    cross = lax.conv_general_dilated(
        pixels.reshape(32, 4, 8, CH), outs, (1, 1), ((1, 1), (1, 1)),
        dimension_numbers=("HCWN", "HIWO", "NHWC"), preferred_element_type=jnp.float32,
    )
    square = jnp.square(pixels.astype(jnp.float32))
    by_col = jnp.sum(square, axis=(0, 2))
    top, bottom = jnp.sum(square[0], axis=1), jnp.sum(square[31], axis=1)
    by_row = jnp.stack([by_col - bottom, by_col, by_col - top], axis=1)
    full = jnp.sum(by_row, axis=2)
    diag = jnp.stack([full - by_row[:, :, 7], full, full - by_row[:, :, 0]], axis=2)
    weight = ((1.0 - keep_off) * my_scale)[:, None, None, None] * diag
    weight = weight.transpose(3, 0, 1, 2)
    rhs = keep_off * cross + jnp.sum(weight[..., None] * tiles.astype(jnp.float32), axis=1)
    sent = lax.all_to_all(
        rhs.reshape(128, OWN, TAPS, 40), ("blk", "client"), split_axis=0, concat_axis=0, tiled=True
    )
    rhs_out = jnp.sum(sent.reshape(32, 4, OWN, TAPS, 40), axis=1).transpose(1, 2, 0, 3).reshape(90, CH)

    first_channel = blk_here * 40 + client_here * OWN
    chan = lax.broadcasted_iota(jnp.int32, (16, CH), 1) - first_channel
    lane = lax.broadcasted_iota(jnp.int32, (16, CH), 0)
    pick = ((chan == lane) & (lane < OWN)).astype(jnp.bfloat16)
    row = lax.broadcasted_iota(jnp.int32, (MPAD, TAPS * 16), 0)
    col = lax.broadcasted_iota(jnp.int32, (MPAD, TAPS * 16), 1)
    order = ((row // TAPS == col % 16) & (row % TAPS == col // 16)).astype(jnp.bfloat16)
    row = lax.broadcasted_iota(jnp.int32, (1152, 1152), 0)
    col = lax.broadcasted_iota(jnp.int32, (1152, 1152), 1)
    spread = ((row % 128) * TAPS + row // 128 == col).astype(jnp.bfloat16)
    groups = jnp.stack([client_here, client_here ^ 2, client_here ^ 1, client_here ^ 3])
    group_scale = all_scale.reshape(4, 2)[groups]
    img_scale = jnp.repeat(jnp.repeat(group_scale, 16, axis=1)[:, None, :], 32, axis=1).reshape(4, LANES)
    gram_out = gram(
        jnp.reshape(first_channel * TAPS, (1,)), own.reshape(2048, CH), other.reshape(2048, CH),
        pick, order, spread, img_scale,
    )
    return gram_out, rhs_out


def solution(mesh):
    in_specs = (P("client", None, "blk", None, None), P(), P("client", "blk", None))
    out_specs = (P(("blk", "client"), None), P(("blk", "client"), None))
    return jax.shard_map(body, mesh=mesh, in_specs=in_specs, out_specs=out_specs, check_vma=False)
```

```python
import jax
import jax.numpy as jnp
import numpy as np
from jax import lax
from jax.experimental import pallas as pl
from jax.experimental.pallas import tpu as pltpu
from jax.sharding import PartitionSpec as P

keep_off = 0.9
AXES = ("client", "blk")
CHIPS = 4
ROWS = 32
CH = 1280
LANES = 1024
TAPS = 9
OWN = 10
MPAD = 96


def split_device(index):
    client, blk = divmod(index, 32)
    x_hi, core = divmod(client, 2)
    z, rest = divmod(blk, 8)
    x_lo, y = divmod(rest, 4)
    return x_hi * 2 + x_lo, y, z, core


def join_device(x, y, z, core):
    return ((x // 2) * 2 + core) * 32 + z * 8 + (x % 2) * 4 + y


def take_from(value, offset):
    pairs = []
    for dst in range(128):
        x, y, z, core = split_device(dst)
        src = join_device((x + offset[0]) % 4, (y + offset[1]) % 4, (z + offset[2]) % 4, core)
        pairs.append((src, dst))
    return lax.ppermute(value, AXES, pairs)


def vec_add(*vectors):
    return tuple(sum(parts) % 4 for parts in zip(*vectors))


STEP = (1, 0, 1)
FIRST = [tuple(k * s % 4 for s in STEP) for k in range(4)]
SECOND = [(0, 0, 0), (1, 1, 3), (0, 2, 0), (3, 3, 1)]
HEAD = [vec_add(g, f) for g in SECOND[:2] for f in FIRST]
TAIL = [vec_add(g, f) for g in SECOND[2:] for f in FIRST]
LAST = [((1, 0, 0), 0), ((0, 0, 3), 1), ((3, 0, 0), 0), ((0, 0, 1), 1), ((0, 1, 0), 0), ((0, 3, 0), 0)]
SOURCES = list(HEAD) + list(TAIL)
for away, part in LAST:
    SOURCES += [vec_add(away, o) for o in (TAIL if part else HEAD)]
assert len(set(SOURCES)) == 64


def gather_chips(block):
    level = jnp.concatenate([block] + [take_from(block, o) for o in FIRST[1:]], axis=0)
    level = jnp.concatenate([level] + [take_from(level, o) for o in SECOND[1:]], axis=0)
    halves = (level[:256], level[256:])
    return [level] + [take_from(halves[part], away) for away, part in LAST]


def assemble_kernel(slots, *refs):
    sources, out, sems = refs[:7], refs[7], refs[8]
    copies = []
    for t in range(64):
        if t < 16:
            src = sources[0].at[pl.ds(t * ROWS, ROWS)]
        else:
            piece, row = divmod(t - 16, 8)
            src = sources[1 + piece].at[pl.ds(row * ROWS, ROWS)]
        copies.append(pltpu.make_async_copy(src, out.at[slots[t]], sems.at[t]))
    for copy in copies:
        copy.start()
    for copy in copies:
        copy.wait()


def assemble(slots, pieces):
    return pl.pallas_call(
        assemble_kernel,
        out_shape=jax.ShapeDtypeStruct((64, ROWS, CH), jnp.bfloat16),
        grid_spec=pltpu.PrefetchScalarGridSpec(
            num_scalar_prefetch=1,
            grid=(1,),
            in_specs=[pl.BlockSpec(memory_space=pl.ANY)] * 7,
            out_specs=pl.BlockSpec((64, ROWS, CH), lambda i, s: (0, 0, 0), pipeline_mode=pl.Buffered(1)),
            scratch_shapes=[pltpu.SemaphoreType.DMA((64,))],
        ),
        compiler_params=pltpu.CompilerParams(vmem_limit_bytes=16 * 1024 * 1024),
        name="assemble",
    )(slots, *pieces)


def shift_lanes(value, row_off, col_off):
    amount = 32 * row_off + col_off
    moved = pltpu.roll(value, (-amount) % LANES, 1) if amount else value
    lane = lax.broadcasted_iota(jnp.int32, (1, LANES), 1)
    row = lane // 32 + row_off
    col = lane % 8 + col_off
    inside = (row >= 0) & (row < 32) & (col >= 0) & (col < 8)
    return jnp.where(inside, moved, 0.0)


def gram_kernel(first_ref, own_ref, other_ref, pick_ref, order_ref, spread_ref, scale_ref, out_ref, left, acc, high):
    pick = pick_ref[...]
    order = order_ref[...]
    for group in range(4):
        source = own_ref if group < 2 else other_ref
        pixels = source[pl.ds((group % 2) * LANES, LANES), :]
        slab = lax.dot_general(pick, pixels, (((1,), (1,)), ((), ())), preferred_element_type=jnp.float32)
        shifted = [shift_lanes(slab, t // 3 - 1, t % 3 - 1) for t in range(TAPS)]
        stacked = jnp.concatenate(shifted, axis=0).astype(jnp.bfloat16)
        patch = jnp.dot(order, stacked, preferred_element_type=jnp.float32)
        patch = patch * scale_ref[pl.ds(group, 1), :]
        for t in range(TAPS):
            left[pl.ds(t * MPAD, MPAD), pl.ds(group * LANES, LANES)] = shift_lanes(
                patch, 1 - t // 3, 1 - t % 3
            ).astype(jnp.bfloat16)

    @pl.loop(0, 5)
    def _(n):
        lanes = pl.ds(pl.multiple_of(n * 256, 256), 256)
        total = jnp.dot(left[:, pl.ds(0, 2048)], own_ref[:, lanes], preferred_element_type=jnp.float32)
        total += jnp.dot(left[:, pl.ds(2048, 2048)], other_ref[:, lanes], preferred_element_type=jnp.float32)
        acc[:, lanes] = total

    for block in range(10):
        for t in range(TAPS):
            part = acc[pl.ds(t * MPAD, MPAD), pl.ds(block * 128, 128)]
            top = part.astype(jnp.bfloat16)
            high[pl.ds(block * 2 * MPAD, MPAD), pl.ds(t * 128, 128)] = top
            high[pl.ds((block * 2 + 1) * MPAD, MPAD), pl.ds(t * 128, 128)] = (
                part - top.astype(jnp.float32)
            ).astype(jnp.bfloat16)

    first = first_ref[0]

    @pl.loop(0, 6)
    def _(step):
        half = step // 3
        piece = step % 3
        rows = pl.ds(pl.multiple_of(half * 960, 960), 960)
        cols = pl.ds(pl.multiple_of(piece * 384, 128), 384)
        wide = jnp.dot(high[rows, :], spread_ref[:, cols], preferred_element_type=jnp.float32)
        for b in range(5):
            value = wide[b * 192 : b * 192 + 96] + wide[b * 192 + 96 : b * 192 + 192]
            value = value[:90]
            base = half * 5760 + b * 1152 + piece * 384
            row = lax.broadcasted_iota(jnp.int32, value.shape, 0) + first
            col = lax.broadcasted_iota(jnp.int32, value.shape, 1) + base
            out_ref[:, pl.ds(pl.multiple_of(base, 128), 384)] = jnp.where(row == col, value, keep_off * value)


def gram(first, own, other, pick, order, spread, scale):
    whole = pl.BlockSpec(memory_space=pltpu.VMEM)
    return pl.pallas_call(
        gram_kernel,
        out_shape=jax.ShapeDtypeStruct((90, 11520), jnp.float32),
        in_specs=[pl.BlockSpec(memory_space=pltpu.SMEM)] + [whole] * 6,
        out_specs=whole,
        scratch_shapes=[
            pltpu.VMEM((TAPS * MPAD, 4 * LANES), jnp.bfloat16),
            pltpu.VMEM((TAPS * MPAD, CH), jnp.float32),
            pltpu.VMEM((20 * MPAD, TAPS * 128), jnp.bfloat16),
        ],
        compiler_params=pltpu.CompilerParams(vmem_limit_bytes=58 * 1024 * 1024),
        cost_estimate=pl.CostEstimate(flops=20_000_000_000, bytes_accessed=20_000_000, transcendentals=0),
        name="gram",
    )(first, own, other, pick, order, spread, scale)


def pack_kernel(weights_ref, order_ref, out_ref, ordered):
    lane = lax.broadcasted_iota(jnp.int32, (1, 128), 1)
    for c in range(2):
        ordered[...] = jnp.dot(order_ref[...], weights_ref[c], preferred_element_type=jnp.float32)
        for dest in range(32):
            tile, off = divmod(dest * 40, 128)
            total = jnp.zeros((120, 128), jnp.float32)
            for b in range(3):
                rows = pl.ds(b * 120, 120)
                amount = (b * 40 - off) % 128
                value = ordered[rows, pl.ds(tile * 128, 128)]
                value = pltpu.roll(value, amount, 1) if amount else value
                if off + 40 > 128:
                    nxt = ordered[rows, pl.ds(tile * 128 + 128, 128)]
                    nxt = pltpu.roll(nxt, amount, 1) if amount else nxt
                    value = jnp.where(lane < b * 40 + 128 - off, value, nxt)
                total = jnp.where((lane >= b * 40) & (lane < b * 40 + 40), value, total)
            out_ref[dest, pl.ds(c * 120, 120), :] = total.astype(jnp.bfloat16)


def pack(weights, order):
    whole = pl.BlockSpec(memory_space=pltpu.VMEM)
    return pl.pallas_call(
        pack_kernel,
        out_shape=jax.ShapeDtypeStruct((32, 240, 128), jnp.bfloat16),
        in_specs=[whole] * 2,
        out_specs=whole,
        scratch_shapes=[pltpu.VMEM((360, CH), jnp.float32)],
        compiler_params=pltpu.CompilerParams(vmem_limit_bytes=24 * 1024 * 1024),
        cost_estimate=pl.CostEstimate(flops=1_000_000_000, bytes_accessed=6_000_000, transcendentals=0),
        name="pack",
    )(weights, order)


def shift_rows(value, amount):
    if amount == 0:
        return value
    pad = jnp.zeros((abs(amount), value.shape[1]), value.dtype)
    if amount > 0:
        return jnp.concatenate([value[amount:], pad], axis=0)
    return jnp.concatenate([pad, value[:amount]], axis=0)


def shift_cols(value, amount):
    if amount == 0:
        return value
    moved = pltpu.roll(value, (-amount) % value.shape[0], 0)
    col = lax.broadcasted_iota(jnp.int32, (value.shape[0], 1), 0) % 8 + amount
    return jnp.where((col >= 0) & (col < 8), moved, 0.0)


def rhs_kernel(scale_ref, pixels_ref, tiles_ref, out_ref, rhs):
    lane = lax.broadcasted_iota(jnp.int32, (1, 128), 1)
    tap_row = lax.broadcasted_iota(jnp.int32, (16, 384), 0)
    tap_lane = lax.broadcasted_iota(jnp.int32, (16, 384), 1)
    spread = (tap_row == (tap_lane // 128) * 3 + (tap_lane % 128) // 40).astype(jnp.bfloat16)
    for c in range(2):
        scale = scale_ref[c]
        pixels = pixels_ref[...].reshape(32, 2, 16, CH)[:, c].reshape(512, CH)
        tiles = jnp.concatenate([tiles_ref[c * 3 + a] for a in range(3)], axis=1)
        taps = jnp.dot(pixels, tiles, preferred_element_type=jnp.float32)
        by_col = shift_rows(taps[:, :128], -16) + taps[:, 128:256] + shift_rows(taps[:, 256:], 16)
        out = shift_cols(by_col, -1)
        out += pltpu.roll(by_col, 88, 1)
        out += shift_cols(pltpu.roll(by_col, 48, 1), 1)
        out = jnp.where(lane < 40, out, 0.0).astype(jnp.bfloat16).astype(jnp.float32) * scale
        moved = shift_cols(out, 1)
        moved += pltpu.roll(out, 40, 1)
        moved += pltpu.roll(shift_cols(out, -1), 80, 1)
        moved = jnp.concatenate([shift_rows(moved, 16), moved, shift_rows(moved, -16)], axis=1)
        cross = lax.dot_general(
            pixels, moved.astype(jnp.bfloat16), (((0,), (0,)), ((), ())), preferred_element_type=jnp.float32
        )
        top = bottom = total = None
        for h in range(32):
            part = jnp.zeros((8, CH), jnp.float32)
            for slot in range(2):
                value = pixels[h * 16 + slot * 8 : h * 16 + slot * 8 + 8].astype(jnp.float32)
                part += value * value
            total = part if total is None else total + part
            if h == 0:
                top = part
            if h == 31:
                bottom = part
        col = lax.broadcasted_iota(jnp.int32, (8, 1), 0)
        diag = []
        for kept in (total - bottom, total, total - top):
            diag.append(jnp.sum(jnp.where(col < 7, kept, 0.0), axis=0, keepdims=True))
            diag.append(jnp.sum(kept, axis=0, keepdims=True))
            diag.append(jnp.sum(jnp.where(col > 0, kept, 0.0), axis=0, keepdims=True))
        diag = jnp.concatenate(diag + [jnp.zeros((7, CH), jnp.float32)], axis=0)
        diag = diag * (scale * (1.0 - keep_off))
        wide = None
        for _ in range(3):
            head = diag.astype(jnp.bfloat16)
            part = lax.dot_general(head, spread, (((0,), (0,)), ((), ())), preferred_element_type=jnp.float32)
            wide = part if wide is None else wide + part
            diag = diag - head.astype(jnp.float32)
        value = keep_off * cross + wide * tiles.astype(jnp.float32)
        rhs[...] = value if c == 0 else rhs[...] + value
    for dest in range(128):
        for a in range(3):
            out_ref[dest, pl.ds(a * OWN, OWN), :] = rhs[pl.ds(dest * OWN, OWN), pl.ds(a * 128, 128)]
        out_ref[dest, pl.ds(30, 2), :] = jnp.zeros((2, 128), jnp.float32)


def rhs_part(scale, pixels, tiles):
    whole = pl.BlockSpec(memory_space=pltpu.VMEM)
    return pl.pallas_call(
        rhs_kernel,
        out_shape=jax.ShapeDtypeStruct((128, 32, 128), jnp.float32),
        in_specs=[pl.BlockSpec(memory_space=pltpu.SMEM), pl.BlockSpec((1024, CH), lambda i: (0, 0)), pl.BlockSpec((6, CH, 128), lambda i: (0, 0, 0))],
        grid=(1,),
        out_specs=pl.BlockSpec((128, 32, 128), lambda i: (0, 0, 0)),
        scratch_shapes=[pltpu.VMEM((CH, 384), jnp.float32)],
        compiler_params=pltpu.CompilerParams(vmem_limit_bytes=48 * 1024 * 1024),
        cost_estimate=pl.CostEstimate(flops=4_000_000_000, bytes_accessed=8_000_000, transcendentals=0),
        name="rhs_part",
    )(scale, pixels, tiles)


def finish_kernel(sent_ref, after_ref, out_ref, rows):
    del after_ref
    lane = lax.broadcasted_iota(jnp.int32, (1, 128), 1)
    for tile in range(10):
        first = tile * 128 // 40
        last = (tile * 128 + 127) // 40
        values = [jnp.zeros((32, 128), jnp.float32)] * 3
        for b in range(first, last + 1):
            total = sent_ref[b * 4] + sent_ref[b * 4 + 1] + sent_ref[b * 4 + 2] + sent_ref[b * 4 + 3]
            start = b * 40 - tile * 128
            keep = (lane >= start) & (lane < start + 40)
            for t in range(3):
                amount = (start - t * 40) % 128
                moved = pltpu.roll(total, amount, 1) if amount else total
                values[t] = jnp.where(keep, moved, values[t])
        for t in range(3):
            rows[pl.ds(t * 32, 32), pl.ds(tile * 128, 128)] = values[t]
    dst = lax.broadcasted_iota(jnp.int32, (MPAD, 96), 0)
    src = lax.broadcasted_iota(jnp.int32, (MPAD, 96), 1)
    inner = src % 32
    pick = (dst == (inner % OWN) * TAPS + (inner // OWN) * 3 + src // 32) & (inner < 30)
    pick = pick.astype(jnp.bfloat16)
    value = rows[...]
    result = None
    for _ in range(3):
        head = value.astype(jnp.bfloat16)
        part = jnp.dot(pick, head, preferred_element_type=jnp.float32)
        result = part if result is None else result + part
        value = value - head.astype(jnp.float32)
    out_ref[...] = result[:90]


def finish(sent, after):
    whole = pl.BlockSpec(memory_space=pltpu.VMEM)
    return pl.pallas_call(
        finish_kernel,
        out_shape=jax.ShapeDtypeStruct((90, CH), jnp.float32),
        in_specs=[whole, pl.BlockSpec(memory_space=pl.ANY)],
        out_specs=whole,
        scratch_shapes=[pltpu.VMEM((96, CH), jnp.float32)],
        compiler_params=pltpu.CompilerParams(vmem_limit_bytes=16 * 1024 * 1024),
        name="finish",
    )(sent, after)


def body(activations, sample_count, client_weights):
    client_here = lax.axis_index("client")
    blk_here = lax.axis_index("blk")
    x_hi, core = client_here // 2, client_here % 2
    z, x_lo, y = blk_here // 8, (blk_here // 4) % 2, blk_here % 4
    x = x_hi * 2 + x_lo

    counts = sample_count.astype(jnp.float32)
    all_scale = 1.0 / (8 * counts * 256)
    mine = lax.dynamic_slice_in_dim(sample_count, client_here * 2, 2)
    my_scale = lax.dynamic_slice_in_dim(all_scale, client_here * 2, 2)

    row = lax.broadcasted_iota(jnp.int32, (360, 360), 0)
    col = lax.broadcasted_iota(jnp.int32, (360, 360), 1)
    tap_order = (col == (row % 40) * TAPS + (row // 40) % 3 * 3 + row // 120).astype(jnp.bfloat16)
    packed = pack(client_weights, tap_order)
    tiles = lax.all_to_all(packed, "blk", split_axis=0, concat_axis=0, tiled=True)
    tiles = tiles.reshape(32, 6, 40, 128).transpose(1, 0, 2, 3).reshape(6, CH, 128)

    live = lax.broadcasted_iota(jnp.int32, (2, 2), 1) < mine[:, None]
    masked = jnp.where(live[:, :, None, None, None], activations, jnp.zeros_like(activations))
    pieces = gather_chips(masked.reshape(ROWS, CH))
    offs = np.array(SOURCES, np.int32)
    src_x, src_y, src_z = (x + offs[:, 0]) % 4, (y + offs[:, 1]) % 4, (z + offs[:, 2]) % 4
    away = (src_x // 2 != x_hi).astype(jnp.int32)
    slots = (away * 32 + src_z * 8 + (src_x % 2) * 4 + src_y).astype(jnp.int32)
    own = assemble(slots, pieces)
    other = lax.ppermute(own, AXES, [(d, d ^ 32) for d in range(128)])

    own_rows = own.reshape(2048, CH)
    part = rhs_part(my_scale, own_rows, tiles)
    sent = lax.all_to_all(part, ("blk", "client"), split_axis=0, concat_axis=0, tiled=True)

    first_channel = blk_here * 40 + client_here * OWN
    chan = lax.broadcasted_iota(jnp.int32, (16, CH), 1) - first_channel
    lane = lax.broadcasted_iota(jnp.int32, (16, CH), 0)
    pick = ((chan == lane) & (lane < OWN)).astype(jnp.bfloat16)
    row = lax.broadcasted_iota(jnp.int32, (MPAD, TAPS * 16), 0)
    col = lax.broadcasted_iota(jnp.int32, (MPAD, TAPS * 16), 1)
    order = ((row // TAPS == col % 16) & (row % TAPS == col // 16)).astype(jnp.bfloat16)
    row = lax.broadcasted_iota(jnp.int32, (1152, 1152), 0)
    col = lax.broadcasted_iota(jnp.int32, (1152, 1152), 1)
    spread = ((row % 128) * TAPS + row // 128 == col).astype(jnp.bfloat16)
    groups = jnp.stack([client_here, client_here ^ 2, client_here ^ 1, client_here ^ 3])
    group_scale = all_scale.reshape(4, 2)[groups]
    img_scale = jnp.repeat(jnp.repeat(group_scale, 16, axis=1)[:, None, :], 32, axis=1).reshape(4, LANES)
    gram_out = gram(
        jnp.reshape(first_channel * TAPS, (1,)), own_rows, other.reshape(2048, CH),
        pick, order, spread, img_scale,
    )
    return gram_out, finish(sent, gram_out)


def solution(mesh):
    in_specs = (P("client", None, "blk", None, None), P(), P("client", "blk", None))
    out_specs = (P(("blk", "client"), None), P(("blk", "client"), None))
    return jax.shard_map(body, mesh=mesh, in_specs=in_specs, out_specs=out_specs, check_vma=False)
```

```python
import jax
import jax.numpy as jnp
import numpy as np
from jax import lax
from jax.experimental import pallas as pl
from jax.experimental.pallas import tpu as pltpu
from jax.sharding import PartitionSpec as P

keep_off = 0.9
AXES = ("client", "blk")
CHIPS = 4
ROWS = 32
CH = 1280
LANES = 1024
TAPS = 9
OWN = 10
MPAD = 96


def split_device(index):
    client, blk = divmod(index, 32)
    x_hi, core = divmod(client, 2)
    z, rest = divmod(blk, 8)
    x_lo, y = divmod(rest, 4)
    return x_hi * 2 + x_lo, y, z, core


def join_device(x, y, z, core):
    return ((x // 2) * 2 + core) * 32 + z * 8 + (x % 2) * 4 + y


def take_from(value, offset):
    pairs = []
    for dst in range(128):
        x, y, z, core = split_device(dst)
        src = join_device((x + offset[0]) % 4, (y + offset[1]) % 4, (z + offset[2]) % 4, core)
        pairs.append((src, dst))
    return lax.ppermute(value, AXES, pairs)


def vec_add(*vectors):
    return tuple(sum(parts) % 4 for parts in zip(*vectors))


STEP = (1, 0, 1)
FIRST = [tuple(k * s % 4 for s in STEP) for k in range(4)]
SECOND = [(0, 0, 0), (1, 1, 3), (0, 2, 0), (3, 3, 1)]
LEVEL = [vec_add(g, f) for g in SECOND for f in FIRST]
LAST = [((1, 0, 0), 0, 8), ((0, 0, 3), 8, 16), ((3, 0, 0), 0, 8), ((0, 0, 1), 8, 16), ((0, 1, 0), 0, 12), ((0, 3, 0), 4, 8)]
SOURCES = list(LEVEL)
for away, low, high in LAST:
    SOURCES += [vec_add(away, o) for o in LEVEL[low:high]]
assert len(SOURCES) == 64 and len(set(SOURCES)) == 64


def gather_chips(block, tiles):
    level = jnp.concatenate([block] + [take_from(block, o) for o in FIRST[1:]], axis=0)
    level = jnp.concatenate([level] + [take_from(level, o) for o in SECOND[1:]], axis=0)
    level, tiles = lax.optimization_barrier((level, tiles))
    parts = [level[low * ROWS : high * ROWS] for _, low, high in LAST]
    small = take_from(parts[5], LAST[5][0])
    parts[2], small = lax.optimization_barrier((parts[2], small))
    return [level] + [take_from(part, last[0]) for part, last in zip(parts[:5], LAST)] + [small], tiles


def assemble_kernel(slots, *refs):
    out = refs[-1]
    spot = 0
    for ref in refs[:-1]:
        for row in range(ref.shape[0] // ROWS):
            out[slots[spot]] = ref[pl.ds(row * ROWS, ROWS), :]
            spot += 1


def assemble(slots, pieces):
    return pl.pallas_call(
        assemble_kernel,
        out_shape=jax.ShapeDtypeStruct((64, ROWS, CH), jnp.bfloat16),
        in_specs=[pl.BlockSpec(memory_space=pltpu.SMEM)] + [pl.BlockSpec(memory_space=pltpu.VMEM)] * 7,
        out_specs=pl.BlockSpec(memory_space=pltpu.VMEM),
        compiler_params=pltpu.CompilerParams(vmem_limit_bytes=16 * 1024 * 1024),
        name="assemble",
    )(slots, *pieces)


def shift_lanes(value, row_off, col_off):
    amount = 32 * row_off + col_off
    moved = pltpu.roll(value, (-amount) % LANES, 1) if amount else value
    lane = lax.broadcasted_iota(jnp.int32, (1, LANES), 1)
    row = lane // 32 + row_off
    col = lane % 8 + col_off
    inside = (row >= 0) & (row < 32) & (col >= 0) & (col < 8)
    return jnp.where(inside, moved, 0.0)


def gram_kernel(first_ref, own_ref, other_ref, pick_ref, order_ref, scale_ref, out_ref, left, acc, staged, sems):
    pick = pick_ref[...]
    order = order_ref[...]
    for group in range(4):
        source = own_ref if group < 2 else other_ref
        pixels = source[pl.ds((group % 2) * LANES, LANES), :]
        slab = lax.dot_general(pick, pixels, (((1,), (1,)), ((), ())), preferred_element_type=jnp.float32)
        shifted = [shift_lanes(slab, t // 3 - 1, t % 3 - 1) for t in range(TAPS)]
        stacked = jnp.concatenate(shifted, axis=0).astype(jnp.bfloat16)
        patch = jnp.dot(order, stacked, preferred_element_type=jnp.float32)
        patch = patch * scale_ref[pl.ds(group, 1), :]
        for t in range(TAPS):
            left[pl.ds(t * MPAD, MPAD), pl.ds(group * LANES, LANES)] = shift_lanes(
                patch, 1 - t // 3, 1 - t % 3
            ).astype(jnp.bfloat16)

    @pl.loop(0, 5)
    def _(n):
        lanes = pl.ds(pl.multiple_of(n * 256, 256), 256)
        total = jnp.dot(left[:, pl.ds(0, 2048)], own_ref[:, lanes], preferred_element_type=jnp.float32)
        total += jnp.dot(left[:, pl.ds(2048, 2048)], other_ref[:, lanes], preferred_element_type=jnp.float32)
        acc[:, lanes] = total

    first = first_ref[0]
    lane = lax.broadcasted_iota(jnp.int32, (MPAD, 128), 1)
    row = lax.broadcasted_iota(jnp.int32, (MPAD, 128), 0)

    def weave(values, part):
        spot = lane + 128 * part
        index = spot // 3
        result = None
        for k in range(3):
            moved = jnp.take_along_axis(values[k], index, axis=1)
            result = moved if result is None else jnp.where(spot % 3 == k, moved, result)
        return result

    @pl.loop(0, 10)
    def _(block):
        lanes = pl.ds(pl.multiple_of(block * 128, 128), 128)
        inner = [
            [weave([acc[pl.ds((3 * a + b) * MPAD, MPAD), lanes] for a in range(3)], part) for part in range(3)]
            for b in range(3)
        ]
        for tile in range(9):
            value = weave([inner[b][tile // 3] for b in range(3)], tile % 3)
            base = block * 1152 + tile * 128
            value = jnp.where(row + first == lane + base, value, keep_off * value)
            staged[:, pl.ds(pl.multiple_of(base, 128), 128)] = value[:90]
        wide = pl.ds(pl.multiple_of(block * 1152, 128), 1152)
        pltpu.make_async_copy(staged.at[:, wide], out_ref.at[:, wide], sems.at[block]).start()

    for block in range(10):
        wide = pl.ds(block * 1152, 1152)
        pltpu.make_async_copy(staged.at[:, wide], out_ref.at[:, wide], sems.at[block]).wait()


def gram(first, own, other, pick, order, scale):
    whole = pl.BlockSpec(memory_space=pltpu.VMEM)
    return pl.pallas_call(
        gram_kernel,
        out_shape=jax.ShapeDtypeStruct((90, 11520), jnp.float32),
        in_specs=[pl.BlockSpec(memory_space=pltpu.SMEM)] + [whole] * 5,
        out_specs=pl.BlockSpec(memory_space=pl.ANY),
        scratch_shapes=[
            pltpu.VMEM((TAPS * MPAD, 4 * LANES), jnp.bfloat16),
            pltpu.VMEM((TAPS * MPAD, CH), jnp.float32),
            pltpu.VMEM((90, 11520), jnp.float32),
            pltpu.SemaphoreType.DMA((10,)),
        ],
        compiler_params=pltpu.CompilerParams(vmem_limit_bytes=58 * 1024 * 1024),
        cost_estimate=pl.CostEstimate(flops=20_000_000_000, bytes_accessed=20_000_000, transcendentals=0),
        name="gram",
    )(first, own, other, pick, order, scale)


def pack_kernel(weights_ref, order_ref, out_ref, ordered):
    lane = lax.broadcasted_iota(jnp.int32, (1, 128), 1)
    for c in range(2):
        ordered[...] = jnp.dot(order_ref[...], weights_ref[c], preferred_element_type=jnp.float32)
        for dest in range(32):
            tile, off = divmod(dest * 40, 128)
            total = jnp.zeros((120, 128), jnp.float32)
            for b in range(3):
                rows = pl.ds(b * 120, 120)
                amount = (b * 40 - off) % 128
                value = ordered[rows, pl.ds(tile * 128, 128)]
                value = pltpu.roll(value, amount, 1) if amount else value
                if off + 40 > 128:
                    nxt = ordered[rows, pl.ds(tile * 128 + 128, 128)]
                    nxt = pltpu.roll(nxt, amount, 1) if amount else nxt
                    value = jnp.where(lane < b * 40 + 128 - off, value, nxt)
                total = jnp.where((lane >= b * 40) & (lane < b * 40 + 40), value, total)
            out_ref[dest, pl.ds(c * 120, 120), :] = total.astype(jnp.bfloat16)


def pack(weights, order):
    whole = pl.BlockSpec(memory_space=pltpu.VMEM)
    return pl.pallas_call(
        pack_kernel,
        out_shape=jax.ShapeDtypeStruct((32, 240, 128), jnp.bfloat16),
        in_specs=[whole] * 2,
        out_specs=whole,
        scratch_shapes=[pltpu.VMEM((360, CH), jnp.float32)],
        compiler_params=pltpu.CompilerParams(vmem_limit_bytes=24 * 1024 * 1024),
        cost_estimate=pl.CostEstimate(flops=1_000_000_000, bytes_accessed=6_000_000, transcendentals=0),
        name="pack",
    )(weights, order)


def shift_rows(value, amount):
    if amount == 0:
        return value
    pad = jnp.zeros((abs(amount), value.shape[1]), value.dtype)
    if amount > 0:
        return jnp.concatenate([value[amount:], pad], axis=0)
    return jnp.concatenate([pad, value[:amount]], axis=0)


def shift_cols(value, amount):
    if amount == 0:
        return value
    moved = pltpu.roll(value, (-amount) % value.shape[0], 0)
    col = lax.broadcasted_iota(jnp.int32, (value.shape[0], 1), 0) % 8 + amount
    return jnp.where((col >= 0) & (col < 8), moved, 0.0)


def rhs_kernel(scale_ref, pixels_ref, tiles_ref, out_ref, rhs):
    lane = lax.broadcasted_iota(jnp.int32, (1, 128), 1)
    tap_row = lax.broadcasted_iota(jnp.int32, (16, 384), 0)
    tap_lane = lax.broadcasted_iota(jnp.int32, (16, 384), 1)
    spread = (tap_row == (tap_lane // 128) * 3 + (tap_lane % 128) // 40).astype(jnp.bfloat16)
    for c in range(2):
        scale = scale_ref[c]
        pixels = pixels_ref[...].reshape(32, 2, 16, CH)[:, c].reshape(512, CH)
        tiles = jnp.concatenate([tiles_ref[c * 3 + a] for a in range(3)], axis=1)
        taps = jnp.dot(pixels, tiles, preferred_element_type=jnp.float32)
        by_col = shift_rows(taps[:, :128], -16) + taps[:, 128:256] + shift_rows(taps[:, 256:], 16)
        out = shift_cols(by_col, -1)
        out += pltpu.roll(by_col, 88, 1)
        out += shift_cols(pltpu.roll(by_col, 48, 1), 1)
        out = jnp.where(lane < 40, out, 0.0).astype(jnp.bfloat16).astype(jnp.float32) * scale
        moved = shift_cols(out, 1)
        moved += pltpu.roll(out, 40, 1)
        moved += pltpu.roll(shift_cols(out, -1), 80, 1)
        moved = jnp.concatenate([shift_rows(moved, 16), moved, shift_rows(moved, -16)], axis=1)
        cross = lax.dot_general(
            pixels, moved.astype(jnp.bfloat16), (((0,), (0,)), ((), ())), preferred_element_type=jnp.float32
        )
        top = bottom = total = None
        for h in range(32):
            part = jnp.zeros((8, CH), jnp.float32)
            for slot in range(2):
                value = pixels[h * 16 + slot * 8 : h * 16 + slot * 8 + 8].astype(jnp.float32)
                part += value * value
            total = part if total is None else total + part
            if h == 0:
                top = part
            if h == 31:
                bottom = part
        col = lax.broadcasted_iota(jnp.int32, (8, 1), 0)
        diag = []
        for kept in (total - bottom, total, total - top):
            diag.append(jnp.sum(jnp.where(col < 7, kept, 0.0), axis=0, keepdims=True))
            diag.append(jnp.sum(kept, axis=0, keepdims=True))
            diag.append(jnp.sum(jnp.where(col > 0, kept, 0.0), axis=0, keepdims=True))
        diag = jnp.concatenate(diag + [jnp.zeros((7, CH), jnp.float32)], axis=0)
        diag = diag * (scale * (1.0 - keep_off))
        wide = None
        for _ in range(3):
            head = diag.astype(jnp.bfloat16)
            part = lax.dot_general(head, spread, (((0,), (0,)), ((), ())), preferred_element_type=jnp.float32)
            wide = part if wide is None else wide + part
            diag = diag - head.astype(jnp.float32)
        value = keep_off * cross + wide * tiles.astype(jnp.float32)
        rhs[...] = value if c == 0 else rhs[...] + value
    for dest in range(128):
        for a in range(3):
            out_ref[dest, pl.ds(a * OWN, OWN), :] = rhs[pl.ds(dest * OWN, OWN), pl.ds(a * 128, 128)]
        out_ref[dest, pl.ds(30, 2), :] = jnp.zeros((2, 128), jnp.float32)


def rhs_part(scale, pixels, tiles):
    whole = pl.BlockSpec(memory_space=pltpu.VMEM)
    return pl.pallas_call(
        rhs_kernel,
        out_shape=jax.ShapeDtypeStruct((128, 32, 128), jnp.float32),
        in_specs=[pl.BlockSpec(memory_space=pltpu.SMEM), pl.BlockSpec((1024, CH), lambda i: (0, 0)), pl.BlockSpec((6, CH, 128), lambda i: (0, 0, 0))],
        grid=(1,),
        out_specs=pl.BlockSpec((128, 32, 128), lambda i: (0, 0, 0)),
        scratch_shapes=[pltpu.VMEM((CH, 384), jnp.float32)],
        compiler_params=pltpu.CompilerParams(vmem_limit_bytes=48 * 1024 * 1024),
        cost_estimate=pl.CostEstimate(flops=4_000_000_000, bytes_accessed=8_000_000, transcendentals=0),
        name="rhs_part",
    )(scale, pixels, tiles)


def finish_kernel(sent_ref, after_ref, out_ref, rows):
    del after_ref
    lane = lax.broadcasted_iota(jnp.int32, (1, 128), 1)
    for tile in range(10):
        first = tile * 128 // 40
        last = (tile * 128 + 127) // 40
        values = [jnp.zeros((32, 128), jnp.float32)] * 3
        for b in range(first, last + 1):
            total = sent_ref[b * 4] + sent_ref[b * 4 + 1] + sent_ref[b * 4 + 2] + sent_ref[b * 4 + 3]
            start = b * 40 - tile * 128
            keep = (lane >= start) & (lane < start + 40)
            for t in range(3):
                amount = (start - t * 40) % 128
                moved = pltpu.roll(total, amount, 1) if amount else total
                values[t] = jnp.where(keep, moved, values[t])
        for t in range(3):
            rows[pl.ds(t * 32, 32), pl.ds(tile * 128, 128)] = values[t]
    dst = lax.broadcasted_iota(jnp.int32, (MPAD, 96), 0)
    src = lax.broadcasted_iota(jnp.int32, (MPAD, 96), 1)
    inner = src % 32
    pick = (dst == (inner % OWN) * TAPS + (inner // OWN) * 3 + src // 32) & (inner < 30)
    pick = pick.astype(jnp.bfloat16)
    value = rows[...]
    result = None
    for _ in range(3):
        head = value.astype(jnp.bfloat16)
        part = jnp.dot(pick, head, preferred_element_type=jnp.float32)
        result = part if result is None else result + part
        value = value - head.astype(jnp.float32)
    out_ref[...] = result[:90]


def finish(sent, after):
    whole = pl.BlockSpec(memory_space=pltpu.VMEM)
    return pl.pallas_call(
        finish_kernel,
        out_shape=jax.ShapeDtypeStruct((90, CH), jnp.float32),
        in_specs=[whole, pl.BlockSpec(memory_space=pl.ANY)],
        out_specs=whole,
        scratch_shapes=[pltpu.VMEM((96, CH), jnp.float32)],
        compiler_params=pltpu.CompilerParams(vmem_limit_bytes=16 * 1024 * 1024),
        name="finish",
    )(sent, after)


def body(activations, sample_count, client_weights):
    client_here = lax.axis_index("client")
    blk_here = lax.axis_index("blk")
    x_hi, core = client_here // 2, client_here % 2
    z, x_lo, y = blk_here // 8, (blk_here // 4) % 2, blk_here % 4
    x = x_hi * 2 + x_lo

    counts = sample_count.astype(jnp.float32)
    all_scale = 1.0 / (8 * counts * 256)
    mine = lax.dynamic_slice_in_dim(sample_count, client_here * 2, 2)
    my_scale = lax.dynamic_slice_in_dim(all_scale, client_here * 2, 2)

    row = lax.broadcasted_iota(jnp.int32, (360, 360), 0)
    col = lax.broadcasted_iota(jnp.int32, (360, 360), 1)
    tap_order = (col == (row % 40) * TAPS + (row // 40) % 3 * 3 + row // 120).astype(jnp.bfloat16)
    packed = pack(client_weights, tap_order)

    live = lax.broadcasted_iota(jnp.int32, (2, 2), 1) < mine[:, None]
    masked = jnp.where(live[:, :, None, None, None], activations, jnp.zeros_like(activations))
    masked, packed = lax.optimization_barrier((masked, packed))
    tiles = lax.all_to_all(packed, "blk", split_axis=0, concat_axis=0, tiled=True)
    pieces, tiles = gather_chips(masked.reshape(ROWS, CH), tiles)
    tiles = tiles.reshape(32, 6, 40, 128).transpose(1, 0, 2, 3).reshape(6, CH, 128)
    offs = np.array(SOURCES, np.int32)
    src_x, src_y, src_z = (x + offs[:, 0]) % 4, (y + offs[:, 1]) % 4, (z + offs[:, 2]) % 4
    away = (src_x // 2 != x_hi).astype(jnp.int32)
    slots = (away * 32 + src_z * 8 + (src_x % 2) * 4 + src_y).astype(jnp.int32)
    own = assemble(slots, pieces)
    other = lax.ppermute(own, AXES, [(d, d ^ 32) for d in range(128)])

    own_rows = own.reshape(2048, CH)
    part = rhs_part(my_scale, own_rows, tiles)
    sent = lax.all_to_all(part, ("blk", "client"), split_axis=0, concat_axis=0, tiled=True)

    first_channel = blk_here * 40 + client_here * OWN
    chan = lax.broadcasted_iota(jnp.int32, (16, CH), 1) - first_channel
    lane = lax.broadcasted_iota(jnp.int32, (16, CH), 0)
    pick = ((chan == lane) & (lane < OWN)).astype(jnp.bfloat16)
    row = lax.broadcasted_iota(jnp.int32, (MPAD, TAPS * 16), 0)
    col = lax.broadcasted_iota(jnp.int32, (MPAD, TAPS * 16), 1)
    order = ((row // TAPS == col % 16) & (row % TAPS == col // 16)).astype(jnp.bfloat16)
    groups = jnp.stack([client_here, client_here ^ 2, client_here ^ 1, client_here ^ 3])
    group_scale = all_scale.reshape(4, 2)[groups]
    img_scale = jnp.repeat(jnp.repeat(group_scale, 16, axis=1)[:, None, :], 32, axis=1).reshape(4, LANES)
    gram_out = gram(
        jnp.reshape(first_channel * TAPS, (1,)), own_rows, other.reshape(2048, CH),
        pick, order, img_scale,
    )
    return gram_out, finish(sent, gram_out)


def solution(mesh):
    in_specs = (P("client", None, "blk", None, None), P(), P("client", "blk", None))
    out_specs = (P(("blk", "client"), None), P(("blk", "client"), None))
    return jax.shard_map(body, mesh=mesh, in_specs=in_specs, out_specs=out_specs, check_vma=False)
```

```python
import jax
import jax.numpy as jnp
import numpy as np
from jax import lax
from jax.experimental import pallas as pl
from jax.experimental.pallas import tpu as pltpu
from jax.sharding import PartitionSpec as P

keep_off = 0.9
AXES = ("client", "blk")
CHIPS = 4
ROWS = 32
CH = 1280
LANES = 1024
TAPS = 9
OWN = 10
MPAD = 96


def split_device(index):
    client, blk = divmod(index, 32)
    x_hi, core = divmod(client, 2)
    z, rest = divmod(blk, 8)
    x_lo, y = divmod(rest, 4)
    return x_hi * 2 + x_lo, y, z, core


def join_device(x, y, z, core):
    return ((x // 2) * 2 + core) * 32 + z * 8 + (x % 2) * 4 + y


def take_from(value, offset):
    pairs = []
    for dst in range(128):
        x, y, z, core = split_device(dst)
        src = join_device((x + offset[0]) % 4, (y + offset[1]) % 4, (z + offset[2]) % 4, core)
        pairs.append((src, dst))
    return lax.ppermute(value, AXES, pairs)


def vec_add(*vectors):
    return tuple(sum(parts) % 4 for parts in zip(*vectors))


STEP = (1, 0, 1)
FIRST = [tuple(k * s % 4 for s in STEP) for k in range(4)]
SECOND = [(0, 0, 0), (1, 1, 3), (0, 2, 0), (3, 3, 1)]
LEVEL = [vec_add(g, f) for g in SECOND for f in FIRST]
LAST = [((1, 0, 0), 0, 8), ((0, 0, 3), 8, 16), ((3, 0, 0), 0, 8), ((0, 0, 1), 8, 16), ((0, 1, 0), 0, 12), ((0, 3, 0), 4, 8)]
SOURCES = list(LEVEL)
for away, low, high in LAST:
    SOURCES += [vec_add(away, o) for o in LEVEL[low:high]]
assert len(SOURCES) == 64 and len(set(SOURCES)) == 64


def gather_chips(block, tiles, early):
    level = jnp.concatenate([block] + [take_from(block, o) for o in FIRST[1:]], axis=0)
    level, early = lax.optimization_barrier((level, early))
    level = jnp.concatenate([level] + [take_from(level, o) for o in SECOND[1:]], axis=0)
    level, tiles = lax.optimization_barrier((level, tiles))
    parts = [level[low * ROWS : high * ROWS] for _, low, high in LAST]
    small = take_from(parts[5], LAST[5][0])
    tiles = tiles.reshape(32, 6, 40, 128).transpose(1, 0, 2, 3).reshape(6, CH, 128)
    parts[2], small, tiles = lax.optimization_barrier((parts[2], small, tiles))
    return [level] + [take_from(part, last[0]) for part, last in zip(parts[:5], LAST)] + [small], tiles, early


def assemble_kernel(slots, *refs):
    out = refs[-1]
    spot = 0
    for ref in refs[:-1]:
        for row in range(ref.shape[0] // ROWS):
            out[slots[spot]] = ref[pl.ds(row * ROWS, ROWS), :]
            spot += 1


def assemble(slots, pieces):
    return pl.pallas_call(
        assemble_kernel,
        out_shape=jax.ShapeDtypeStruct((64, ROWS, CH), jnp.bfloat16),
        in_specs=[pl.BlockSpec(memory_space=pltpu.SMEM)] + [pl.BlockSpec(memory_space=pltpu.VMEM)] * 7,
        out_specs=pl.BlockSpec(memory_space=pltpu.VMEM),
        compiler_params=pltpu.CompilerParams(vmem_limit_bytes=16 * 1024 * 1024),
        name="assemble",
    )(slots, *pieces)


def shift_lanes(value, row_off, col_off):
    amount = 32 * row_off + col_off
    moved = pltpu.roll(value, (-amount) % LANES, 1) if amount else value
    lane = lax.broadcasted_iota(jnp.int32, (1, LANES), 1)
    row = lane // 32 + row_off
    col = lane % 8 + col_off
    inside = (row >= 0) & (row < 32) & (col >= 0) & (col < 8)
    return jnp.where(inside, moved, 0.0)


def gram_kernel(first_ref, own_hbm, other_hbm, pick_ref, order_ref, scale_ref, out_ref, token_ref, left, acc, staged, pixels_own, pixels_other, sems, loads):
    own_ref, other_ref = pixels_own, pixels_other
    copies = []
    for group in range(4):
        rows = pl.ds((group % 2) * LANES, LANES)
        source, target = (own_hbm, pixels_own) if group < 2 else (other_hbm, pixels_other)
        copies.append(pltpu.make_async_copy(source.at[rows], target.at[rows], loads.at[group]))
        copies[-1].start()
    token_ref[...] = jnp.zeros_like(token_ref)
    pick = pick_ref[...]
    order = order_ref[...]
    for group in range(4):
        copies[group].wait()
        source = own_ref if group < 2 else other_ref
        pixels = source[pl.ds((group % 2) * LANES, LANES), :]
        slab = lax.dot_general(pick, pixels, (((1,), (1,)), ((), ())), preferred_element_type=jnp.float32)
        shifted = [shift_lanes(slab, t // 3 - 1, t % 3 - 1) for t in range(TAPS)]
        stacked = jnp.concatenate(shifted, axis=0).astype(jnp.bfloat16)
        patch = jnp.dot(order, stacked, preferred_element_type=jnp.float32)
        patch = patch * scale_ref[pl.ds(group, 1), :]
        for t in range(TAPS):
            left[pl.ds(t * MPAD, MPAD), pl.ds(group * LANES, LANES)] = shift_lanes(
                patch, 1 - t // 3, 1 - t % 3
            ).astype(jnp.bfloat16)

    @pl.loop(0, 5)
    def _(n):
        lanes = pl.ds(pl.multiple_of(n * 256, 256), 256)
        total = jnp.dot(left[:, pl.ds(0, 2048)], own_ref[:, lanes], preferred_element_type=jnp.float32)
        total += jnp.dot(left[:, pl.ds(2048, 2048)], other_ref[:, lanes], preferred_element_type=jnp.float32)
        acc[:, lanes] = total

    first = first_ref[0]
    lane = lax.broadcasted_iota(jnp.int32, (MPAD, 128), 1)
    row = lax.broadcasted_iota(jnp.int32, (MPAD, 128), 0)

    def weave(values, part):
        spot = lane + 128 * part
        index = spot // 3
        result = None
        for k in range(3):
            moved = jnp.take_along_axis(values[k], index, axis=1)
            result = moved if result is None else jnp.where(spot % 3 == k, moved, result)
        return result

    @pl.loop(0, 10)
    def _(block):
        lanes = pl.ds(pl.multiple_of(block * 128, 128), 128)
        inner = [
            [weave([acc[pl.ds((3 * a + b) * MPAD, MPAD), lanes] for a in range(3)], part) for part in range(3)]
            for b in range(3)
        ]
        for tile in range(9):
            value = weave([inner[b][tile // 3] for b in range(3)], tile % 3)
            base = block * 1152 + tile * 128
            value = jnp.where(row + first == lane + base, value, keep_off * value)
            staged[:, pl.ds(pl.multiple_of(base, 128), 128)] = value[:90]
        wide = pl.ds(pl.multiple_of(block * 1152, 128), 1152)
        pltpu.make_async_copy(staged.at[:, wide], out_ref.at[:, wide], sems.at[block]).start()

    for block in range(10):
        wide = pl.ds(block * 1152, 1152)
        pltpu.make_async_copy(staged.at[:, wide], out_ref.at[:, wide], sems.at[block]).wait()


def gram(first, own, other, pick, order, scale):
    whole = pl.BlockSpec(memory_space=pltpu.VMEM)
    held = pl.BlockSpec(memory_space=pltpu.HBM)
    return pl.pallas_call(
        gram_kernel,
        out_shape=(jax.ShapeDtypeStruct((90, 11520), jnp.float32), jax.ShapeDtypeStruct((8, 128), jnp.float32)),
        in_specs=[pl.BlockSpec(memory_space=pltpu.SMEM), held, held] + [whole] * 3,
        out_specs=(held, whole),
        scratch_shapes=[
            pltpu.VMEM((TAPS * MPAD, 4 * LANES), jnp.bfloat16),
            pltpu.VMEM((TAPS * MPAD, CH), jnp.float32),
            pltpu.VMEM((90, 11520), jnp.float32),
            pltpu.VMEM((2 * LANES, CH), jnp.bfloat16),
            pltpu.VMEM((2 * LANES, CH), jnp.bfloat16),
            pltpu.SemaphoreType.DMA((10,)),
            pltpu.SemaphoreType.DMA((4,)),
        ],
        compiler_params=pltpu.CompilerParams(vmem_limit_bytes=58 * 1024 * 1024),
        cost_estimate=pl.CostEstimate(flops=20_000_000_000, bytes_accessed=20_000_000, transcendentals=0),
        name="gram",
    )(first, own, other, pick, order, scale)


def pack_kernel(weights_ref, order_ref, out_ref, ordered):
    lane = lax.broadcasted_iota(jnp.int32, (1, 128), 1)
    for c in range(2):
        ordered[...] = jnp.dot(order_ref[...], weights_ref[c], preferred_element_type=jnp.float32)
        for dest in range(32):
            tile, off = divmod(dest * 40, 128)
            total = jnp.zeros((120, 128), jnp.float32)
            for b in range(3):
                rows = pl.ds(b * 120, 120)
                amount = (b * 40 - off) % 128
                value = ordered[rows, pl.ds(tile * 128, 128)]
                value = pltpu.roll(value, amount, 1) if amount else value
                if off + 40 > 128:
                    nxt = ordered[rows, pl.ds(tile * 128 + 128, 128)]
                    nxt = pltpu.roll(nxt, amount, 1) if amount else nxt
                    value = jnp.where(lane < b * 40 + 128 - off, value, nxt)
                total = jnp.where((lane >= b * 40) & (lane < b * 40 + 40), value, total)
            out_ref[dest, pl.ds(c * 120, 120), :] = total.astype(jnp.bfloat16)


def pack(weights, order):
    whole = pl.BlockSpec(memory_space=pltpu.VMEM)
    return pl.pallas_call(
        pack_kernel,
        out_shape=jax.ShapeDtypeStruct((32, 240, 128), jnp.bfloat16),
        in_specs=[whole] * 2,
        out_specs=whole,
        scratch_shapes=[pltpu.VMEM((360, CH), jnp.float32)],
        compiler_params=pltpu.CompilerParams(vmem_limit_bytes=24 * 1024 * 1024),
        cost_estimate=pl.CostEstimate(flops=1_000_000_000, bytes_accessed=6_000_000, transcendentals=0),
        name="pack",
    )(weights, order)


def shift_rows(value, amount):
    if amount == 0:
        return value
    pad = jnp.zeros((abs(amount), value.shape[1]), value.dtype)
    if amount > 0:
        return jnp.concatenate([value[amount:], pad], axis=0)
    return jnp.concatenate([pad, value[:amount]], axis=0)


def shift_cols(value, amount):
    if amount == 0:
        return value
    moved = pltpu.roll(value, (-amount) % value.shape[0], 0)
    col = lax.broadcasted_iota(jnp.int32, (value.shape[0], 1), 0) % 8 + amount
    return jnp.where((col >= 0) & (col < 8), moved, 0.0)


def rhs_kernel(scale_ref, pixels_ref, tiles_ref, out_ref, rhs, staged, sems):
    lane = lax.broadcasted_iota(jnp.int32, (1, 128), 1)
    tap_row = lax.broadcasted_iota(jnp.int32, (16, 384), 0)
    tap_lane = lax.broadcasted_iota(jnp.int32, (16, 384), 1)
    spread = (tap_row == (tap_lane // 128) * 3 + (tap_lane % 128) // 40).astype(jnp.bfloat16)
    for c in range(2):
        scale = scale_ref[c]
        pixels = pixels_ref[...].reshape(32, 2, 16, CH)[:, c].reshape(512, CH)
        tiles = jnp.concatenate([tiles_ref[c * 3 + a] for a in range(3)], axis=1)
        taps = jnp.dot(pixels, tiles, preferred_element_type=jnp.float32)
        by_col = shift_rows(taps[:, :128], -16) + taps[:, 128:256] + shift_rows(taps[:, 256:], 16)
        out = shift_cols(by_col, -1)
        out += pltpu.roll(by_col, 88, 1)
        out += shift_cols(pltpu.roll(by_col, 48, 1), 1)
        out = jnp.where(lane < 40, out, 0.0).astype(jnp.bfloat16).astype(jnp.float32) * scale
        moved = shift_cols(out, 1)
        moved += pltpu.roll(out, 40, 1)
        moved += pltpu.roll(shift_cols(out, -1), 80, 1)
        moved = jnp.concatenate([shift_rows(moved, 16), moved, shift_rows(moved, -16)], axis=1)
        cross = lax.dot_general(
            pixels, moved.astype(jnp.bfloat16), (((0,), (0,)), ((), ())), preferred_element_type=jnp.float32
        )
        top = bottom = total = None
        for h in range(32):
            part = jnp.zeros((8, CH), jnp.float32)
            for slot in range(2):
                value = pixels[h * 16 + slot * 8 : h * 16 + slot * 8 + 8].astype(jnp.float32)
                part += value * value
            total = part if total is None else total + part
            if h == 0:
                top = part
            if h == 31:
                bottom = part
        col = lax.broadcasted_iota(jnp.int32, (8, 1), 0)
        diag = []
        for kept in (total - bottom, total, total - top):
            diag.append(jnp.sum(jnp.where(col < 7, kept, 0.0), axis=0, keepdims=True))
            diag.append(jnp.sum(kept, axis=0, keepdims=True))
            diag.append(jnp.sum(jnp.where(col > 0, kept, 0.0), axis=0, keepdims=True))
        diag = jnp.concatenate(diag + [jnp.zeros((7, CH), jnp.float32)], axis=0)
        diag = diag * (scale * (1.0 - keep_off))
        wide = None
        for _ in range(3):
            head = diag.astype(jnp.bfloat16)
            part = lax.dot_general(head, spread, (((0,), (0,)), ((), ())), preferred_element_type=jnp.float32)
            wide = part if wide is None else wide + part
            diag = diag - head.astype(jnp.float32)
        value = keep_off * cross + wide * tiles.astype(jnp.float32)
        rhs[...] = value if c == 0 else rhs[...] + value
    zeros = jnp.zeros((2, 128), jnp.float32)
    copies = []
    for part in range(8):
        for dest in range(part * 16, part * 16 + 16):
            for a in range(3):
                staged[dest, pl.ds(a * OWN, OWN), :] = rhs[pl.ds(dest * OWN, OWN), pl.ds(a * 128, 128)]
            staged[dest, pl.ds(30, 2), :] = zeros
        some = pl.ds(part * 16, 16)
        copies.append(pltpu.make_async_copy(staged.at[some], out_ref.at[some], sems.at[part]))
        copies[-1].start()
    for copy in copies:
        copy.wait()


def rhs_part(scale, pixels, tiles):
    whole = pl.BlockSpec(memory_space=pltpu.VMEM)
    return pl.pallas_call(
        rhs_kernel,
        out_shape=jax.ShapeDtypeStruct((128, 32, 128), jnp.float32),
        in_specs=[pl.BlockSpec(memory_space=pltpu.SMEM), pl.BlockSpec((1024, CH), lambda i: (0, 0)), pl.BlockSpec((6, CH, 128), lambda i: (0, 0, 0))],
        grid=(1,),
        out_specs=pl.BlockSpec(memory_space=pltpu.HBM),
        scratch_shapes=[
            pltpu.VMEM((CH, 384), jnp.float32),
            pltpu.VMEM((128, 32, 128), jnp.float32),
            pltpu.SemaphoreType.DMA((8,)),
        ],
        compiler_params=pltpu.CompilerParams(vmem_limit_bytes=48 * 1024 * 1024),
        cost_estimate=pl.CostEstimate(flops=4_000_000_000, bytes_accessed=8_000_000, transcendentals=0),
        name="rhs_part",
    )(scale, pixels, tiles)


def finish_kernel(sent_ref, after_ref, out_ref, rows):
    del after_ref
    lane = lax.broadcasted_iota(jnp.int32, (1, 128), 1)
    for tile in range(10):
        first = tile * 128 // 40
        last = (tile * 128 + 127) // 40
        values = [jnp.zeros((32, 128), jnp.float32)] * 3
        for b in range(first, last + 1):
            total = sent_ref[b * 4] + sent_ref[b * 4 + 1] + sent_ref[b * 4 + 2] + sent_ref[b * 4 + 3]
            start = b * 40 - tile * 128
            keep = (lane >= start) & (lane < start + 40)
            for t in range(3):
                amount = (start - t * 40) % 128
                moved = pltpu.roll(total, amount, 1) if amount else total
                values[t] = jnp.where(keep, moved, values[t])
        for t in range(3):
            rows[pl.ds(t * 32, 32), pl.ds(tile * 128, 128)] = values[t]
    dst = lax.broadcasted_iota(jnp.int32, (MPAD, 96), 0)
    src = lax.broadcasted_iota(jnp.int32, (MPAD, 96), 1)
    inner = src % 32
    pick = (dst == (inner % OWN) * TAPS + (inner // OWN) * 3 + src // 32) & (inner < 30)
    pick = pick.astype(jnp.bfloat16)
    value = rows[...]
    result = None
    for _ in range(3):
        head = value.astype(jnp.bfloat16)
        part = jnp.dot(pick, head, preferred_element_type=jnp.float32)
        result = part if result is None else result + part
        value = value - head.astype(jnp.float32)
    out_ref[...] = result[:90]


def finish(sent, after):
    whole = pl.BlockSpec(memory_space=pltpu.VMEM)
    return pl.pallas_call(
        finish_kernel,
        out_shape=jax.ShapeDtypeStruct((90, CH), jnp.float32),
        in_specs=[whole, whole],
        out_specs=whole,
        scratch_shapes=[pltpu.VMEM((96, CH), jnp.float32)],
        compiler_params=pltpu.CompilerParams(vmem_limit_bytes=16 * 1024 * 1024),
        name="finish",
    )(sent, after)


def body(activations, sample_count, client_weights):
    client_here = lax.axis_index("client")
    blk_here = lax.axis_index("blk")
    x_hi, core = client_here // 2, client_here % 2
    z, x_lo, y = blk_here // 8, (blk_here // 4) % 2, blk_here % 4
    x = x_hi * 2 + x_lo

    counts = sample_count.astype(jnp.float32)
    all_scale = 1.0 / (8 * counts * 256)
    mine = lax.dynamic_slice_in_dim(sample_count, client_here * 2, 2)
    my_scale = lax.dynamic_slice_in_dim(all_scale, client_here * 2, 2)

    row = lax.broadcasted_iota(jnp.int32, (360, 360), 0)
    col = lax.broadcasted_iota(jnp.int32, (360, 360), 1)
    tap_order = (col == (row % 40) * TAPS + (row // 40) % 3 * 3 + row // 120).astype(jnp.bfloat16)
    packed = pack(client_weights, tap_order)

    live = lax.broadcasted_iota(jnp.int32, (2, 2), 1) < mine[:, None]
    first_channel = blk_here * 40 + client_here * OWN
    chan = lax.broadcasted_iota(jnp.int32, (16, CH), 1) - first_channel
    lane = lax.broadcasted_iota(jnp.int32, (16, CH), 0)
    pick = ((chan == lane) & (lane < OWN)).astype(jnp.bfloat16)
    row = lax.broadcasted_iota(jnp.int32, (MPAD, TAPS * 16), 0)
    col = lax.broadcasted_iota(jnp.int32, (MPAD, TAPS * 16), 1)
    order = ((row // TAPS == col % 16) & (row % TAPS == col // 16)).astype(jnp.bfloat16)
    groups = jnp.stack([client_here, client_here ^ 2, client_here ^ 1, client_here ^ 3])
    group_scale = all_scale.reshape(4, 2)[groups]
    img_scale = jnp.repeat(jnp.repeat(group_scale, 16, axis=1)[:, None, :], 32, axis=1).reshape(4, LANES)

    masked = jnp.where(live[:, :, None, None, None], activations, jnp.zeros_like(activations))
    tiles = lax.all_to_all(packed, "blk", split_axis=0, concat_axis=0, tiled=True)
    offs = np.array(SOURCES, np.int32)
    src_x, src_y, src_z = (x + offs[:, 0]) % 4, (y + offs[:, 1]) % 4, (z + offs[:, 2]) % 4
    away = (src_x // 2 != x_hi).astype(jnp.int32)
    slots = (away * 32 + src_z * 8 + (src_x % 2) * 4 + src_y).astype(jnp.int32)
    pieces, tiles, early = gather_chips(masked.reshape(ROWS, CH), tiles, (pick, order, img_scale, slots))
    pick, order, img_scale, slots = early
    own = assemble(slots, pieces)
    other = lax.ppermute(own, AXES, [(d, d ^ 32) for d in range(128)])

    own_rows = own.reshape(2048, CH)
    part = rhs_part(my_scale, own_rows, tiles)
    sent = lax.all_to_all(part, ("blk", "client"), split_axis=0, concat_axis=0, tiled=True)

    gram_out, token = gram(
        jnp.reshape(first_channel * TAPS, (1,)), own_rows, other.reshape(2048, CH),
        pick, order, img_scale,
    )
    return gram_out, finish(sent, token)


def solution(mesh):
    in_specs = (P("client", None, "blk", None, None), P(), P("client", "blk", None))
    out_specs = (P(("blk", "client"), None), P(("blk", "client"), None))
    return jax.shard_map(body, mesh=mesh, in_specs=in_specs, out_specs=out_specs, check_vma=False)
```

```python
import jax
import jax.numpy as jnp
import numpy as np
from jax import lax
from jax.experimental import pallas as pl
from jax.experimental.pallas import tpu as pltpu
from jax.sharding import PartitionSpec as P

keep_off = 0.9
AXES = ("client", "blk")
CHIPS = 4
ROWS = 32
CH = 1280
LANES = 1024
TAPS = 9
OWN = 10
MPAD = 96


def split_device(index):
    client, blk = divmod(index, 32)
    x_hi, core = divmod(client, 2)
    z, rest = divmod(blk, 8)
    x_lo, y = divmod(rest, 4)
    return x_hi * 2 + x_lo, y, z, core


def join_device(x, y, z, core):
    return ((x // 2) * 2 + core) * 32 + z * 8 + (x % 2) * 4 + y


def take_from(value, offset):
    pairs = []
    for dst in range(128):
        x, y, z, core = split_device(dst)
        src = join_device((x + offset[0]) % 4, (y + offset[1]) % 4, (z + offset[2]) % 4, core)
        pairs.append((src, dst))
    return lax.ppermute(value, AXES, pairs)


def vec_add(*vectors):
    return tuple(sum(parts) % 4 for parts in zip(*vectors))


STEP = (1, 0, 1)
FIRST = [tuple(k * s % 4 for s in STEP) for k in range(4)]
SECOND = [(0, 0, 0), (1, 1, 3), (0, 2, 0), (3, 3, 1)]
LEVEL = [vec_add(g, f) for g in SECOND for f in FIRST]
LAST = [((1, 0, 0), 0, 8), ((0, 0, 3), 8, 16), ((3, 0, 0), 0, 8), ((0, 0, 1), 8, 16), ((0, 1, 0), 0, 12), ((0, 3, 0), 4, 8)]
SOURCES = list(LEVEL)
for away, low, high in LAST:
    SOURCES += [vec_add(away, o) for o in LEVEL[low:high]]
assert len(SOURCES) == 64 and len(set(SOURCES)) == 64


def gather_chips(block, packed, early):
    level = jnp.concatenate([block] + [take_from(block, o) for o in FIRST[1:]], axis=0)
    level, packed = lax.optimization_barrier((level, packed))
    tiles = lax.all_to_all(packed, "blk", split_axis=0, concat_axis=0, tiled=True)
    level = jnp.concatenate([level] + [take_from(level, o) for o in SECOND[1:]], axis=0)
    parts = [level[low * ROWS : high * ROWS] for _, low, high in LAST]
    small = take_from(parts[5], LAST[5][0])
    parts[2], small, tiles, early = lax.optimization_barrier((parts[2], small, tiles, early))
    tiles = tiles.reshape(32, 6, 40, 128).transpose(1, 0, 2, 3).reshape(6, CH, 128)
    late = take_from(parts[2], LAST[2][0])
    late, tiles = lax.optimization_barrier((late, tiles))
    pieces = [take_from(parts[i], LAST[i][0]) for i in (0, 1, 3, 4)]
    return [level] + pieces[:2] + [late] + pieces[2:] + [small], tiles, early


def assemble_kernel(slots, *refs):
    out = refs[-1]
    spot = 0
    for ref in refs[:-1]:
        for row in range(ref.shape[0] // ROWS):
            out[slots[spot]] = ref[pl.ds(row * ROWS, ROWS), :]
            spot += 1


def assemble(slots, pieces):
    return pl.pallas_call(
        assemble_kernel,
        out_shape=jax.ShapeDtypeStruct((64, ROWS, CH), jnp.bfloat16),
        in_specs=[pl.BlockSpec(memory_space=pltpu.SMEM)] + [pl.BlockSpec(memory_space=pltpu.VMEM)] * 7,
        out_specs=pl.BlockSpec(memory_space=pltpu.VMEM),
        compiler_params=pltpu.CompilerParams(vmem_limit_bytes=16 * 1024 * 1024),
        name="assemble",
    )(slots, *pieces)


def shift_lanes(value, row_off, col_off):
    amount = 32 * row_off + col_off
    moved = pltpu.roll(value, (-amount) % LANES, 1) if amount else value
    lane = lax.broadcasted_iota(jnp.int32, (1, LANES), 1)
    row = lane // 32 + row_off
    col = lane % 8 + col_off
    inside = (row >= 0) & (row < 32) & (col >= 0) & (col < 8)
    return jnp.where(inside, moved, 0.0)


def gram_kernel(first_ref, own_hbm, other_hbm, pick_ref, order_ref, scale_ref, out_ref, token_ref, left, acc, staged, pixels_own, pixels_other, sems, loads):
    own_ref, other_ref = pixels_own, pixels_other
    copies = []
    for group in range(4):
        rows = pl.ds((group % 2) * LANES, LANES)
        source, target = (own_hbm, pixels_own) if group < 2 else (other_hbm, pixels_other)
        copies.append(pltpu.make_async_copy(source.at[rows], target.at[rows], loads.at[group]))
        copies[-1].start()
    token_ref[...] = jnp.zeros_like(token_ref)
    pick = pick_ref[...]
    order = order_ref[...]
    for group in range(4):
        copies[group].wait()
        source = own_ref if group < 2 else other_ref
        pixels = source[pl.ds((group % 2) * LANES, LANES), :]
        slab = lax.dot_general(pick, pixels, (((1,), (1,)), ((), ())), preferred_element_type=jnp.float32)
        shifted = [shift_lanes(slab, t // 3 - 1, t % 3 - 1) for t in range(TAPS)]
        stacked = jnp.concatenate(shifted, axis=0).astype(jnp.bfloat16)
        patch = jnp.dot(order, stacked, preferred_element_type=jnp.float32)
        patch = patch * scale_ref[pl.ds(group, 1), :]
        for t in range(TAPS):
            left[pl.ds(t * MPAD, MPAD), pl.ds(group * LANES, LANES)] = shift_lanes(
                patch, 1 - t // 3, 1 - t % 3
            ).astype(jnp.bfloat16)

    @pl.loop(0, 5)
    def _(n):
        lanes = pl.ds(pl.multiple_of(n * 256, 256), 256)
        total = jnp.dot(left[:, pl.ds(0, 2048)], own_ref[:, lanes], preferred_element_type=jnp.float32)
        total += jnp.dot(left[:, pl.ds(2048, 2048)], other_ref[:, lanes], preferred_element_type=jnp.float32)
        acc[:, lanes] = total

    first = first_ref[0]
    lane = lax.broadcasted_iota(jnp.int32, (MPAD, 128), 1)
    row = lax.broadcasted_iota(jnp.int32, (MPAD, 128), 0)

    def weave(values, part):
        spot = lane + 128 * part
        index = spot // 3
        result = None
        for k in range(3):
            moved = jnp.take_along_axis(values[k], index, axis=1)
            result = moved if result is None else jnp.where(spot % 3 == k, moved, result)
        return result

    @pl.loop(0, 10)
    def _(block):
        lanes = pl.ds(pl.multiple_of(block * 128, 128), 128)
        inner = [
            [weave([acc[pl.ds((3 * a + b) * MPAD, MPAD), lanes] for a in range(3)], part) for part in range(3)]
            for b in range(3)
        ]
        for tile in range(9):
            value = weave([inner[b][tile // 3] for b in range(3)], tile % 3)
            base = block * 1152 + tile * 128
            value = jnp.where(row + first == lane + base, value, keep_off * value)
            staged[:, pl.ds(pl.multiple_of(base, 128), 128)] = value[:90]
        wide = pl.ds(pl.multiple_of(block * 1152, 128), 1152)
        pltpu.make_async_copy(staged.at[:, wide], out_ref.at[:, wide], sems.at[block]).start()

    for block in range(10):
        wide = pl.ds(block * 1152, 1152)
        pltpu.make_async_copy(staged.at[:, wide], out_ref.at[:, wide], sems.at[block]).wait()


def gram(first, own, other, pick, order, scale):
    whole = pl.BlockSpec(memory_space=pltpu.VMEM)
    held = pl.BlockSpec(memory_space=pltpu.HBM)
    return pl.pallas_call(
        gram_kernel,
        out_shape=(jax.ShapeDtypeStruct((90, 11520), jnp.float32), jax.ShapeDtypeStruct((8, 128), jnp.float32)),
        in_specs=[pl.BlockSpec(memory_space=pltpu.SMEM), held, held] + [whole] * 3,
        out_specs=(held, whole),
        scratch_shapes=[
            pltpu.VMEM((TAPS * MPAD, 4 * LANES), jnp.bfloat16),
            pltpu.VMEM((TAPS * MPAD, CH), jnp.float32),
            pltpu.VMEM((90, 11520), jnp.float32),
            pltpu.VMEM((2 * LANES, CH), jnp.bfloat16),
            pltpu.VMEM((2 * LANES, CH), jnp.bfloat16),
            pltpu.SemaphoreType.DMA((10,)),
            pltpu.SemaphoreType.DMA((4,)),
        ],
        compiler_params=pltpu.CompilerParams(vmem_limit_bytes=58 * 1024 * 1024),
        cost_estimate=pl.CostEstimate(flops=20_000_000_000, bytes_accessed=20_000_000, transcendentals=0),
        name="gram",
    )(first, own, other, pick, order, scale)


def pack_kernel(weights_ref, order_ref, out_ref, ordered):
    lane = lax.broadcasted_iota(jnp.int32, (1, 128), 1)
    for c in range(2):
        ordered[...] = jnp.dot(order_ref[...], weights_ref[c], preferred_element_type=jnp.float32)
        for dest in range(32):
            tile, off = divmod(dest * 40, 128)
            total = jnp.zeros((120, 128), jnp.float32)
            for b in range(3):
                rows = pl.ds(b * 120, 120)
                amount = (b * 40 - off) % 128
                value = ordered[rows, pl.ds(tile * 128, 128)]
                value = pltpu.roll(value, amount, 1) if amount else value
                if off + 40 > 128:
                    nxt = ordered[rows, pl.ds(tile * 128 + 128, 128)]
                    nxt = pltpu.roll(nxt, amount, 1) if amount else nxt
                    value = jnp.where(lane < b * 40 + 128 - off, value, nxt)
                total = jnp.where((lane >= b * 40) & (lane < b * 40 + 40), value, total)
            out_ref[dest, pl.ds(c * 120, 120), :] = total.astype(jnp.bfloat16)


def pack(weights, order):
    whole = pl.BlockSpec(memory_space=pltpu.VMEM)
    return pl.pallas_call(
        pack_kernel,
        out_shape=jax.ShapeDtypeStruct((32, 240, 128), jnp.bfloat16),
        in_specs=[whole] * 2,
        out_specs=whole,
        scratch_shapes=[pltpu.VMEM((360, CH), jnp.float32)],
        compiler_params=pltpu.CompilerParams(vmem_limit_bytes=24 * 1024 * 1024),
        cost_estimate=pl.CostEstimate(flops=1_000_000_000, bytes_accessed=6_000_000, transcendentals=0),
        name="pack",
    )(weights, order)


def shift_rows(value, amount):
    if amount == 0:
        return value
    pad = jnp.zeros((abs(amount), value.shape[1]), value.dtype)
    if amount > 0:
        return jnp.concatenate([value[amount:], pad], axis=0)
    return jnp.concatenate([pad, value[:amount]], axis=0)


def shift_cols(value, amount):
    if amount == 0:
        return value
    moved = pltpu.roll(value, (-amount) % value.shape[0], 0)
    col = lax.broadcasted_iota(jnp.int32, (value.shape[0], 1), 0) % 8 + amount
    return jnp.where((col >= 0) & (col < 8), moved, 0.0)


def rhs_kernel(scale_ref, pixels_ref, tiles_ref, out_ref, rhs, staged):
    lane = lax.broadcasted_iota(jnp.int32, (1, 128), 1)
    tap_row = lax.broadcasted_iota(jnp.int32, (16, 384), 0)
    tap_lane = lax.broadcasted_iota(jnp.int32, (16, 384), 1)
    spread = (tap_row == (tap_lane // 128) * 3 + (tap_lane % 128) // 40).astype(jnp.bfloat16)
    for c in range(2):
        scale = scale_ref[c]
        pixels = pixels_ref[...].reshape(32, 2, 16, CH)[:, c].reshape(512, CH)
        tiles = jnp.concatenate([tiles_ref[c * 3 + a] for a in range(3)], axis=1)
        taps = jnp.dot(pixels, tiles, preferred_element_type=jnp.float32)
        by_col = shift_rows(taps[:, :128], -16) + taps[:, 128:256] + shift_rows(taps[:, 256:], 16)
        out = shift_cols(by_col, -1)
        out += pltpu.roll(by_col, 88, 1)
        out += shift_cols(pltpu.roll(by_col, 48, 1), 1)
        out = jnp.where(lane < 40, out, 0.0).astype(jnp.bfloat16).astype(jnp.float32) * scale
        moved = shift_cols(out, 1)
        moved += pltpu.roll(out, 40, 1)
        moved += pltpu.roll(shift_cols(out, -1), 80, 1)
        moved = jnp.concatenate([shift_rows(moved, 16), moved, shift_rows(moved, -16)], axis=1)
        cross = lax.dot_general(
            pixels, moved.astype(jnp.bfloat16), (((0,), (0,)), ((), ())), preferred_element_type=jnp.float32
        )
        top = bottom = total = None
        for h in range(32):
            part = jnp.zeros((8, CH), jnp.float32)
            for slot in range(2):
                value = pixels[h * 16 + slot * 8 : h * 16 + slot * 8 + 8].astype(jnp.float32)
                part += value * value
            total = part if total is None else total + part
            if h == 0:
                top = part
            if h == 31:
                bottom = part
        col = lax.broadcasted_iota(jnp.int32, (8, 1), 0)
        diag = []
        for kept in (total - bottom, total, total - top):
            diag.append(jnp.sum(jnp.where(col < 7, kept, 0.0), axis=0, keepdims=True))
            diag.append(jnp.sum(kept, axis=0, keepdims=True))
            diag.append(jnp.sum(jnp.where(col > 0, kept, 0.0), axis=0, keepdims=True))
        diag = jnp.concatenate(diag + [jnp.zeros((7, CH), jnp.float32)], axis=0)
        diag = diag * (scale * (1.0 - keep_off))
        wide = None
        for _ in range(3):
            head = diag.astype(jnp.bfloat16)
            part = lax.dot_general(head, spread, (((0,), (0,)), ((), ())), preferred_element_type=jnp.float32)
            wide = part if wide is None else wide + part
            diag = diag - head.astype(jnp.float32)
        value = keep_off * cross + wide * tiles.astype(jnp.float32)
        rhs[...] = value if c == 0 else rhs[...] + value
    zeros = jnp.zeros((2, 128), jnp.float32)
    for part in range(8):
        for dest in range(part * 16, part * 16 + 16):
            for a in range(3):
                staged[dest, pl.ds(a * OWN, OWN), :] = rhs[pl.ds(dest * OWN, OWN), pl.ds(a * 128, 128)]
            staged[dest, pl.ds(30, 2), :] = zeros
        some = pl.ds(part * 16, 16)
        out_ref[some] = staged[some].astype(jnp.bfloat16)


def rhs_part(scale, pixels, tiles):
    whole = pl.BlockSpec(memory_space=pltpu.VMEM)
    return pl.pallas_call(
        rhs_kernel,
        out_shape=jax.ShapeDtypeStruct((128, 32, 128), jnp.bfloat16),
        in_specs=[pl.BlockSpec(memory_space=pltpu.SMEM), pl.BlockSpec((1024, CH), lambda i: (0, 0)), pl.BlockSpec((6, CH, 128), lambda i: (0, 0, 0))],
        grid=(1,),
        out_specs=pl.BlockSpec((128, 32, 128), lambda i: (0, 0, 0)),
        scratch_shapes=[
            pltpu.VMEM((CH, 384), jnp.float32),
            pltpu.VMEM((128, 32, 128), jnp.float32),
        ],
        compiler_params=pltpu.CompilerParams(vmem_limit_bytes=48 * 1024 * 1024),
        cost_estimate=pl.CostEstimate(flops=4_000_000_000, bytes_accessed=8_000_000, transcendentals=0),
        name="rhs_part",
    )(scale, pixels, tiles)


def finish_kernel(sent_ref, after_ref, out_ref, rows):
    del after_ref
    lane = lax.broadcasted_iota(jnp.int32, (1, 128), 1)
    for tile in range(10):
        first = tile * 128 // 40
        last = (tile * 128 + 127) // 40
        values = [jnp.zeros((32, 128), jnp.float32)] * 3
        for b in range(first, last + 1):
            total = jnp.sum(sent_ref[pl.ds(b * 4, 4)].astype(jnp.float32), axis=0)
            start = b * 40 - tile * 128
            keep = (lane >= start) & (lane < start + 40)
            for t in range(3):
                amount = (start - t * 40) % 128
                moved = pltpu.roll(total, amount, 1) if amount else total
                values[t] = jnp.where(keep, moved, values[t])
        for t in range(3):
            rows[pl.ds(t * 32, 32), pl.ds(tile * 128, 128)] = values[t]
    dst = lax.broadcasted_iota(jnp.int32, (MPAD, 96), 0)
    src = lax.broadcasted_iota(jnp.int32, (MPAD, 96), 1)
    inner = src % 32
    pick = (dst == (inner % OWN) * TAPS + (inner // OWN) * 3 + src // 32) & (inner < 30)
    pick = pick.astype(jnp.bfloat16)
    value = rows[...]
    result = None
    for _ in range(3):
        head = value.astype(jnp.bfloat16)
        part = jnp.dot(pick, head, preferred_element_type=jnp.float32)
        result = part if result is None else result + part
        value = value - head.astype(jnp.float32)
    out_ref[...] = result[:90]


def finish(sent, after):
    whole = pl.BlockSpec(memory_space=pltpu.VMEM)
    return pl.pallas_call(
        finish_kernel,
        out_shape=jax.ShapeDtypeStruct((90, CH), jnp.float32),
        in_specs=[whole, whole],
        out_specs=whole,
        scratch_shapes=[pltpu.VMEM((96, CH), jnp.float32)],
        compiler_params=pltpu.CompilerParams(vmem_limit_bytes=16 * 1024 * 1024),
        name="finish",
    )(sent, after)


def body(activations, sample_count, client_weights):
    client_here = lax.axis_index("client")
    blk_here = lax.axis_index("blk")
    x_hi, core = client_here // 2, client_here % 2
    z, x_lo, y = blk_here // 8, (blk_here // 4) % 2, blk_here % 4
    x = x_hi * 2 + x_lo

    counts = sample_count.astype(jnp.float32)
    all_scale = 1.0 / (8 * counts * 256)
    mine = lax.dynamic_slice_in_dim(sample_count, client_here * 2, 2)
    my_scale = lax.dynamic_slice_in_dim(all_scale, client_here * 2, 2)

    row = lax.broadcasted_iota(jnp.int32, (360, 360), 0)
    col = lax.broadcasted_iota(jnp.int32, (360, 360), 1)
    tap_order = (col == (row % 40) * TAPS + (row // 40) % 3 * 3 + row // 120).astype(jnp.bfloat16)
    packed = pack(client_weights, tap_order)

    live = lax.broadcasted_iota(jnp.int32, (2, 2), 1) < mine[:, None]
    first_channel = blk_here * 40 + client_here * OWN
    chan = lax.broadcasted_iota(jnp.int32, (16, CH), 1) - first_channel
    lane = lax.broadcasted_iota(jnp.int32, (16, CH), 0)
    pick = ((chan == lane) & (lane < OWN)).astype(jnp.bfloat16)
    row = lax.broadcasted_iota(jnp.int32, (MPAD, TAPS * 16), 0)
    col = lax.broadcasted_iota(jnp.int32, (MPAD, TAPS * 16), 1)
    order = ((row // TAPS == col % 16) & (row % TAPS == col // 16)).astype(jnp.bfloat16)
    groups = jnp.stack([client_here, client_here ^ 2, client_here ^ 1, client_here ^ 3])
    group_scale = all_scale.reshape(4, 2)[groups]
    img_scale = jnp.repeat(jnp.repeat(group_scale, 16, axis=1)[:, None, :], 32, axis=1).reshape(4, LANES)

    masked = jnp.where(live[:, :, None, None, None], activations, jnp.zeros_like(activations))
    offs = np.array(SOURCES, np.int32)
    src_x, src_y, src_z = (x + offs[:, 0]) % 4, (y + offs[:, 1]) % 4, (z + offs[:, 2]) % 4
    away = (src_x // 2 != x_hi).astype(jnp.int32)
    slots = (away * 32 + src_z * 8 + (src_x % 2) * 4 + src_y).astype(jnp.int32)
    pieces, tiles, early = gather_chips(masked.reshape(ROWS, CH), packed, (pick, order, img_scale, slots))
    pick, order, img_scale, slots = early
    own = assemble(slots, pieces)
    other = lax.ppermute(own, AXES, [(d, d ^ 32) for d in range(128)])

    own_rows = own.reshape(2048, CH)
    part = rhs_part(my_scale, own_rows, tiles)
    sent = lax.all_to_all(part, ("blk", "client"), split_axis=0, concat_axis=0, tiled=True)

    gram_out, token = gram(
        jnp.reshape(first_channel * TAPS, (1,)), own_rows, other.reshape(2048, CH),
        pick, order, img_scale,
    )
    return gram_out, finish(sent, token)


def solution(mesh):
    in_specs = (P("client", None, "blk", None, None), P(), P("client", "blk", None))
    out_specs = (P(("blk", "client"), None), P(("blk", "client"), None))
    return jax.shard_map(body, mesh=mesh, in_specs=in_specs, out_specs=out_specs, check_vma=False)
```

```python
import jax
import jax.numpy as jnp
import numpy as np
from jax import lax
from jax.experimental import pallas as pl
from jax.experimental.pallas import tpu as pltpu
from jax.sharding import PartitionSpec as P

keep_off = 0.9
AXES = ("client", "blk")
CHIPS = 4
ROWS = 32
CH = 1280
LANES = 1024
TAPS = 9
OWN = 10
MPAD = 96


def split_device(index):
    client, blk = divmod(index, 32)
    x_hi, core = divmod(client, 2)
    z, rest = divmod(blk, 8)
    x_lo, y = divmod(rest, 4)
    return x_hi * 2 + x_lo, y, z, core


def join_device(x, y, z, core):
    return ((x // 2) * 2 + core) * 32 + z * 8 + (x % 2) * 4 + y


def take_from(value, offset):
    pairs = []
    for dst in range(128):
        x, y, z, core = split_device(dst)
        src = join_device((x + offset[0]) % 4, (y + offset[1]) % 4, (z + offset[2]) % 4, core)
        pairs.append((src, dst))
    return lax.ppermute(value, AXES, pairs)


def vec_add(*vectors):
    return tuple(sum(parts) % 4 for parts in zip(*vectors))


STEP = (1, 0, 1)
FIRST = [tuple(k * s % 4 for s in STEP) for k in range(4)]
SECOND = [(0, 0, 0), (1, 1, 3), (0, 2, 0), (3, 3, 1)]
LEVEL = [vec_add(g, f) for g in SECOND for f in FIRST]
LAST = [((1, 0, 0), 0, 8), ((0, 0, 3), 8, 16), ((3, 0, 0), 0, 8), ((0, 0, 1), 8, 16), ((0, 1, 0), 0, 12), ((0, 3, 0), 4, 8)]
SOURCES = list(LEVEL)
for away, low, high in LAST:
    SOURCES += [vec_add(away, o) for o in LEVEL[low:high]]
assert len(SOURCES) == 64 and len(set(SOURCES)) == 64


def gather_chips(block, packed, early):
    tiles = lax.all_to_all(packed, "blk", split_axis=0, concat_axis=0, tiled=True)
    level = jnp.concatenate([block] + [take_from(block, o) for o in FIRST[1:]], axis=0)
    level = jnp.concatenate([level] + [take_from(level, o) for o in SECOND[1:]], axis=0)
    level, tiles = lax.optimization_barrier((level, tiles))
    parts = [level[low * ROWS : high * ROWS] for _, low, high in LAST]
    small = take_from(parts[5], LAST[5][0])
    tiles = tiles.reshape(32, 6, 40, 128).transpose(1, 0, 2, 3).reshape(6, CH, 128)
    parts[2], small, tiles, early = lax.optimization_barrier((parts[2], small, tiles, early))
    return [level] + [take_from(part, last[0]) for part, last in zip(parts[:5], LAST)] + [small], tiles, early


def assemble_kernel(slots, *refs):
    out = refs[-1]
    spot = 0
    for ref in refs[:-1]:
        for row in range(ref.shape[0] // ROWS):
            out[slots[spot]] = ref[pl.ds(row * ROWS, ROWS), :]
            spot += 1


def assemble(slots, pieces):
    return pl.pallas_call(
        assemble_kernel,
        out_shape=jax.ShapeDtypeStruct((64, ROWS, CH), jnp.bfloat16),
        in_specs=[pl.BlockSpec(memory_space=pltpu.SMEM)] + [pl.BlockSpec(memory_space=pltpu.VMEM)] * 7,
        out_specs=pl.BlockSpec(memory_space=pltpu.VMEM),
        compiler_params=pltpu.CompilerParams(vmem_limit_bytes=16 * 1024 * 1024),
        name="assemble",
    )(slots, *pieces)


def shift_lanes(value, row_off, col_off):
    amount = 32 * row_off + col_off
    moved = pltpu.roll(value, (-amount) % LANES, 1) if amount else value
    lane = lax.broadcasted_iota(jnp.int32, (1, LANES), 1)
    row = lane // 32 + row_off
    col = lane % 8 + col_off
    inside = (row >= 0) & (row < 32) & (col >= 0) & (col < 8)
    return jnp.where(inside, moved, 0.0)


def gram_kernel(first_ref, own_hbm, other_hbm, pick_ref, order_ref, scale_ref, out_ref, token_ref, left, acc, staged, pixels_own, pixels_other, sems, loads):
    own_ref, other_ref = pixels_own, pixels_other
    copies = []
    for group in range(4):
        rows = pl.ds((group % 2) * LANES, LANES)
        source, target = (own_hbm, pixels_own) if group < 2 else (other_hbm, pixels_other)
        copies.append(pltpu.make_async_copy(source.at[rows], target.at[rows], loads.at[group]))
        copies[-1].start()
    token_ref[...] = jnp.zeros_like(token_ref)
    pick = pick_ref[...]
    order = order_ref[...]
    for group in range(4):
        copies[group].wait()
        source = own_ref if group < 2 else other_ref
        pixels = source[pl.ds((group % 2) * LANES, LANES), :]
        slab = lax.dot_general(pick, pixels, (((1,), (1,)), ((), ())), preferred_element_type=jnp.float32)
        shifted = [shift_lanes(slab, t // 3 - 1, t % 3 - 1) for t in range(TAPS)]
        stacked = jnp.concatenate(shifted, axis=0).astype(jnp.bfloat16)
        patch = jnp.dot(order, stacked, preferred_element_type=jnp.float32)
        patch = patch * scale_ref[pl.ds(group, 1), :]
        for t in range(TAPS):
            left[pl.ds(t * MPAD, MPAD), pl.ds(group * LANES, LANES)] = shift_lanes(
                patch, 1 - t // 3, 1 - t % 3
            ).astype(jnp.bfloat16)

    first = first_ref[0]
    lane = lax.broadcasted_iota(jnp.int32, (MPAD, 128), 1)
    row = lax.broadcasted_iota(jnp.int32, (MPAD, 128), 0)

    def weave(values, part):
        spot = lane + 128 * part
        index = spot // 3
        result = None
        for k in range(3):
            moved = jnp.take_along_axis(values[k], index, axis=1)
            result = moved if result is None else jnp.where(spot % 3 == k, moved, result)
        return result

    def multiply(n):
        lanes = pl.ds(n * 256, 256)
        total = jnp.dot(left[:, pl.ds(0, 2048)], own_ref[:, lanes], preferred_element_type=jnp.float32)
        total += jnp.dot(left[:, pl.ds(2048, 2048)], other_ref[:, lanes], preferred_element_type=jnp.float32)
        acc[:, lanes] = total

    def interleave(block):
        lanes = pl.ds(block * 128, 128)
        inner = [
            [weave([acc[pl.ds((3 * a + b) * MPAD, MPAD), lanes] for a in range(3)], part) for part in range(3)]
            for b in range(3)
        ]
        for tile in range(9):
            value = weave([inner[b][tile // 3] for b in range(3)], tile % 3)
            base = block * 1152 + tile * 128
            value = jnp.where(row + first == lane + base, value, keep_off * value)
            staged[:, pl.ds(base, 128)] = value[:90]

    def send(block):
        wide = pl.ds(block * 1152, 1152)
        pltpu.make_async_copy(staged.at[:, wide], out_ref.at[:, wide], sems.at[block]).start()

    multiply(0)
    for n in range(5):
        if n < 4:
            multiply(n + 1)
        interleave(2 * n)
        interleave(2 * n + 1)
        send(2 * n)
        send(2 * n + 1)

    for block in range(10):
        wide = pl.ds(block * 1152, 1152)
        pltpu.make_async_copy(staged.at[:, wide], out_ref.at[:, wide], sems.at[block]).wait()


def gram(first, own, other, pick, order, scale):
    whole = pl.BlockSpec(memory_space=pltpu.VMEM)
    held = pl.BlockSpec(memory_space=pltpu.HBM)
    return pl.pallas_call(
        gram_kernel,
        out_shape=(jax.ShapeDtypeStruct((90, 11520), jnp.float32), jax.ShapeDtypeStruct((8, 128), jnp.float32)),
        in_specs=[pl.BlockSpec(memory_space=pltpu.SMEM), held, held] + [whole] * 3,
        out_specs=(held, whole),
        scratch_shapes=[
            pltpu.VMEM((TAPS * MPAD, 4 * LANES), jnp.bfloat16),
            pltpu.VMEM((TAPS * MPAD, CH), jnp.float32),
            pltpu.VMEM((90, 11520), jnp.float32),
            pltpu.VMEM((2 * LANES, CH), jnp.bfloat16),
            pltpu.VMEM((2 * LANES, CH), jnp.bfloat16),
            pltpu.SemaphoreType.DMA((10,)),
            pltpu.SemaphoreType.DMA((4,)),
        ],
        compiler_params=pltpu.CompilerParams(vmem_limit_bytes=58 * 1024 * 1024),
        cost_estimate=pl.CostEstimate(flops=20_000_000_000, bytes_accessed=20_000_000, transcendentals=0),
        name="gram",
    )(first, own, other, pick, order, scale)


def pack_kernel(weights_ref, order_ref, out_ref, ordered):
    lane = lax.broadcasted_iota(jnp.int32, (1, 128), 1)
    for c in range(2):
        ordered[...] = jnp.dot(order_ref[...], weights_ref[c], preferred_element_type=jnp.float32)
        for dest in range(32):
            tile, off = divmod(dest * 40, 128)
            total = jnp.zeros((120, 128), jnp.float32)
            for b in range(3):
                rows = pl.ds(b * 120, 120)
                amount = (b * 40 - off) % 128
                value = ordered[rows, pl.ds(tile * 128, 128)]
                value = pltpu.roll(value, amount, 1) if amount else value
                if off + 40 > 128:
                    nxt = ordered[rows, pl.ds(tile * 128 + 128, 128)]
                    nxt = pltpu.roll(nxt, amount, 1) if amount else nxt
                    value = jnp.where(lane < b * 40 + 128 - off, value, nxt)
                total = jnp.where((lane >= b * 40) & (lane < b * 40 + 40), value, total)
            out_ref[dest, pl.ds(c * 120, 120), :] = total.astype(jnp.bfloat16)


def pack(weights, order):
    whole = pl.BlockSpec(memory_space=pltpu.VMEM)
    return pl.pallas_call(
        pack_kernel,
        out_shape=jax.ShapeDtypeStruct((32, 240, 128), jnp.bfloat16),
        in_specs=[whole] * 2,
        out_specs=whole,
        scratch_shapes=[pltpu.VMEM((360, CH), jnp.float32)],
        compiler_params=pltpu.CompilerParams(vmem_limit_bytes=24 * 1024 * 1024),
        cost_estimate=pl.CostEstimate(flops=1_000_000_000, bytes_accessed=6_000_000, transcendentals=0),
        name="pack",
    )(weights, order)


def shift_rows(value, amount):
    if amount == 0:
        return value
    pad = jnp.zeros((abs(amount), value.shape[1]), value.dtype)
    if amount > 0:
        return jnp.concatenate([value[amount:], pad], axis=0)
    return jnp.concatenate([pad, value[:amount]], axis=0)


def shift_cols(value, amount):
    if amount == 0:
        return value
    moved = pltpu.roll(value, (-amount) % value.shape[0], 0)
    col = lax.broadcasted_iota(jnp.int32, (value.shape[0], 1), 0) % 8 + amount
    return jnp.where((col >= 0) & (col < 8), moved, 0.0)


def rhs_kernel(scale_ref, pixels_ref, tiles_ref, out_ref, rhs, staged):
    lane = lax.broadcasted_iota(jnp.int32, (1, 128), 1)
    tap_row = lax.broadcasted_iota(jnp.int32, (16, 384), 0)
    tap_lane = lax.broadcasted_iota(jnp.int32, (16, 384), 1)
    spread = (tap_row == (tap_lane // 128) * 3 + (tap_lane % 128) // 40).astype(jnp.bfloat16)
    for c in range(2):
        scale = scale_ref[c]
        pixels = pixels_ref[...].reshape(32, 2, 16, CH)[:, c].reshape(512, CH)
        tiles = jnp.concatenate([tiles_ref[c * 3 + a] for a in range(3)], axis=1)
        taps = jnp.dot(pixels, tiles, preferred_element_type=jnp.float32)
        by_col = shift_rows(taps[:, :128], -16) + taps[:, 128:256] + shift_rows(taps[:, 256:], 16)
        out = shift_cols(by_col, -1)
        out += pltpu.roll(by_col, 88, 1)
        out += shift_cols(pltpu.roll(by_col, 48, 1), 1)
        out = jnp.where(lane < 40, out, 0.0).astype(jnp.bfloat16).astype(jnp.float32) * scale
        moved = shift_cols(out, 1)
        moved += pltpu.roll(out, 40, 1)
        moved += pltpu.roll(shift_cols(out, -1), 80, 1)
        moved = jnp.concatenate([shift_rows(moved, 16), moved, shift_rows(moved, -16)], axis=1)
        cross = lax.dot_general(
            pixels, moved.astype(jnp.bfloat16), (((0,), (0,)), ((), ())), preferred_element_type=jnp.float32
        )
        top = bottom = total = None
        for h in range(32):
            part = jnp.zeros((8, CH), jnp.float32)
            for slot in range(2):
                value = pixels[h * 16 + slot * 8 : h * 16 + slot * 8 + 8].astype(jnp.float32)
                part += value * value
            total = part if total is None else total + part
            if h == 0:
                top = part
            if h == 31:
                bottom = part
        col = lax.broadcasted_iota(jnp.int32, (8, 1), 0)
        diag = []
        for kept in (total - bottom, total, total - top):
            diag.append(jnp.sum(jnp.where(col < 7, kept, 0.0), axis=0, keepdims=True))
            diag.append(jnp.sum(kept, axis=0, keepdims=True))
            diag.append(jnp.sum(jnp.where(col > 0, kept, 0.0), axis=0, keepdims=True))
        diag = jnp.concatenate(diag + [jnp.zeros((7, CH), jnp.float32)], axis=0)
        diag = diag * (scale * (1.0 - keep_off))
        wide = None
        for _ in range(3):
            head = diag.astype(jnp.bfloat16)
            part = lax.dot_general(head, spread, (((0,), (0,)), ((), ())), preferred_element_type=jnp.float32)
            wide = part if wide is None else wide + part
            diag = diag - head.astype(jnp.float32)
        value = keep_off * cross + wide * tiles.astype(jnp.float32)
        rhs[...] = value if c == 0 else rhs[...] + value
    zeros = jnp.zeros((2, 128), jnp.float32)
    for part in range(8):
        for dest in range(part * 16, part * 16 + 16):
            for a in range(3):
                staged[dest, pl.ds(a * OWN, OWN), :] = rhs[pl.ds(dest * OWN, OWN), pl.ds(a * 128, 128)]
            staged[dest, pl.ds(30, 2), :] = zeros
        some = pl.ds(part * 16, 16)
        out_ref[some] = staged[some].astype(jnp.bfloat16)


def rhs_part(scale, pixels, tiles):
    whole = pl.BlockSpec(memory_space=pltpu.VMEM)
    return pl.pallas_call(
        rhs_kernel,
        out_shape=jax.ShapeDtypeStruct((128, 32, 128), jnp.bfloat16),
        in_specs=[pl.BlockSpec(memory_space=pltpu.SMEM), pl.BlockSpec((1024, CH), lambda i: (0, 0)), pl.BlockSpec((6, CH, 128), lambda i: (0, 0, 0))],
        grid=(1,),
        out_specs=pl.BlockSpec((128, 32, 128), lambda i: (0, 0, 0)),
        scratch_shapes=[
            pltpu.VMEM((CH, 384), jnp.float32),
            pltpu.VMEM((128, 32, 128), jnp.float32),
        ],
        compiler_params=pltpu.CompilerParams(vmem_limit_bytes=48 * 1024 * 1024),
        cost_estimate=pl.CostEstimate(flops=4_000_000_000, bytes_accessed=8_000_000, transcendentals=0),
        name="rhs_part",
    )(scale, pixels, tiles)


def finish_kernel(sent_ref, after_ref, out_ref, rows):
    del after_ref
    lane = lax.broadcasted_iota(jnp.int32, (1, 128), 1)
    for tile in range(10):
        first = tile * 128 // 40
        last = (tile * 128 + 127) // 40
        values = [jnp.zeros((32, 128), jnp.float32)] * 3
        for b in range(first, last + 1):
            total = jnp.sum(sent_ref[pl.ds(b * 4, 4)].astype(jnp.float32), axis=0)
            start = b * 40 - tile * 128
            keep = (lane >= start) & (lane < start + 40)
            for t in range(3):
                amount = (start - t * 40) % 128
                moved = pltpu.roll(total, amount, 1) if amount else total
                values[t] = jnp.where(keep, moved, values[t])
        for t in range(3):
            rows[pl.ds(t * 32, 32), pl.ds(tile * 128, 128)] = values[t]
    dst = lax.broadcasted_iota(jnp.int32, (MPAD, 96), 0)
    src = lax.broadcasted_iota(jnp.int32, (MPAD, 96), 1)
    inner = src % 32
    pick = (dst == (inner % OWN) * TAPS + (inner // OWN) * 3 + src // 32) & (inner < 30)
    pick = pick.astype(jnp.bfloat16)
    value = rows[...]
    result = None
    for _ in range(3):
        head = value.astype(jnp.bfloat16)
        part = jnp.dot(pick, head, preferred_element_type=jnp.float32)
        result = part if result is None else result + part
        value = value - head.astype(jnp.float32)
    out_ref[...] = result[:90]


def finish(sent, after):
    whole = pl.BlockSpec(memory_space=pltpu.VMEM)
    return pl.pallas_call(
        finish_kernel,
        out_shape=jax.ShapeDtypeStruct((90, CH), jnp.float32),
        in_specs=[whole, whole],
        out_specs=whole,
        scratch_shapes=[pltpu.VMEM((96, CH), jnp.float32)],
        compiler_params=pltpu.CompilerParams(vmem_limit_bytes=16 * 1024 * 1024),
        name="finish",
    )(sent, after)


def body(activations, sample_count, client_weights):
    client_here = lax.axis_index("client")
    blk_here = lax.axis_index("blk")
    x_hi, core = client_here // 2, client_here % 2
    z, x_lo, y = blk_here // 8, (blk_here // 4) % 2, blk_here % 4
    x = x_hi * 2 + x_lo

    counts = sample_count.astype(jnp.float32)
    all_scale = 1.0 / (8 * counts * 256)
    mine = lax.dynamic_slice_in_dim(sample_count, client_here * 2, 2)
    my_scale = lax.dynamic_slice_in_dim(all_scale, client_here * 2, 2)

    row = lax.broadcasted_iota(jnp.int32, (360, 360), 0)
    col = lax.broadcasted_iota(jnp.int32, (360, 360), 1)
    tap_order = (col == (row % 40) * TAPS + (row // 40) % 3 * 3 + row // 120).astype(jnp.bfloat16)
    packed = pack(client_weights, tap_order)

    live = lax.broadcasted_iota(jnp.int32, (2, 2), 1) < mine[:, None]
    first_channel = blk_here * 40 + client_here * OWN
    chan = lax.broadcasted_iota(jnp.int32, (16, CH), 1) - first_channel
    lane = lax.broadcasted_iota(jnp.int32, (16, CH), 0)
    pick = ((chan == lane) & (lane < OWN)).astype(jnp.bfloat16)
    row = lax.broadcasted_iota(jnp.int32, (MPAD, TAPS * 16), 0)
    col = lax.broadcasted_iota(jnp.int32, (MPAD, TAPS * 16), 1)
    order = ((row // TAPS == col % 16) & (row % TAPS == col // 16)).astype(jnp.bfloat16)
    groups = jnp.stack([client_here, client_here ^ 2, client_here ^ 1, client_here ^ 3])
    group_scale = all_scale.reshape(4, 2)[groups]
    img_scale = jnp.repeat(jnp.repeat(group_scale, 16, axis=1)[:, None, :], 32, axis=1).reshape(4, LANES)

    masked = jnp.where(live[:, :, None, None, None], activations, jnp.zeros_like(activations))
    offs = np.array(SOURCES, np.int32)
    src_x, src_y, src_z = (x + offs[:, 0]) % 4, (y + offs[:, 1]) % 4, (z + offs[:, 2]) % 4
    away = (src_x // 2 != x_hi).astype(jnp.int32)
    slots = (away * 32 + src_z * 8 + (src_x % 2) * 4 + src_y).astype(jnp.int32)
    pieces, tiles, early = gather_chips(masked.reshape(ROWS, CH), packed, (pick, order, img_scale, slots))
    pick, order, img_scale, slots = early
    own = assemble(slots, pieces)
    other = lax.ppermute(own, AXES, [(d, d ^ 32) for d in range(128)])

    own_rows = own.reshape(2048, CH)
    part = rhs_part(my_scale, own_rows, tiles)
    sent = lax.all_to_all(part, ("blk", "client"), split_axis=0, concat_axis=0, tiled=True)

    gram_out, token = gram(
        jnp.reshape(first_channel * TAPS, (1,)), own_rows, other.reshape(2048, CH),
        pick, order, img_scale,
    )
    return gram_out, finish(sent, token)


def solution(mesh):
    in_specs = (P("client", None, "blk", None, None), P(), P("client", "blk", None))
    out_specs = (P(("blk", "client"), None), P(("blk", "client"), None))
    return jax.shard_map(body, mesh=mesh, in_specs=in_specs, out_specs=out_specs, check_vma=False)
```

```python
import jax
import jax.numpy as jnp
import numpy as np
from jax import lax
from jax.experimental import pallas as pl
from jax.experimental.pallas import tpu as pltpu
from jax.sharding import PartitionSpec as P

keep_off = 0.9
AXES = ("client", "blk")
CHIPS = 4
ROWS = 32
CH = 1280
LANES = 1024
TAPS = 9
OWN = 10
MPAD = 96


def split_device(index):
    client, blk = divmod(index, 32)
    x_hi, core = divmod(client, 2)
    z, rest = divmod(blk, 8)
    x_lo, y = divmod(rest, 4)
    return x_hi * 2 + x_lo, y, z, core


def join_device(x, y, z, core):
    return ((x // 2) * 2 + core) * 32 + z * 8 + (x % 2) * 4 + y


def take_from(value, offset):
    pairs = []
    for dst in range(128):
        x, y, z, core = split_device(dst)
        src = join_device((x + offset[0]) % 4, (y + offset[1]) % 4, (z + offset[2]) % 4, core)
        pairs.append((src, dst))
    return lax.ppermute(value, AXES, pairs)


def vec_add(*vectors):
    return tuple(sum(parts) % 4 for parts in zip(*vectors))


STEP = (1, 0, 1)
FIRST = [tuple(k * s % 4 for s in STEP) for k in range(4)]
SECOND = [(0, 0, 0), (1, 1, 3), (0, 2, 0), (3, 3, 1)]
LEVEL = [vec_add(g, f) for g in SECOND for f in FIRST]
LAST = [((1, 0, 0), 0, 8), ((0, 0, 3), 8, 16), ((3, 0, 0), 0, 8), ((0, 0, 1), 8, 16), ((0, 1, 0), 0, 10), ((0, 3, 0), 2, 8)]
SOURCES = list(LEVEL)
for away, low, high in LAST:
    SOURCES += [vec_add(away, o) for o in LEVEL[low:high]]
assert len(SOURCES) == 64 and len(set(SOURCES)) == 64


def gather_chips(block, packed, early):
    tiles = lax.all_to_all(packed, "blk", split_axis=0, concat_axis=0, tiled=True)
    level = jnp.concatenate([block] + [take_from(block, o) for o in FIRST[1:]], axis=0)
    level = jnp.concatenate([level] + [take_from(level, o) for o in SECOND[1:]], axis=0)
    level, tiles = lax.optimization_barrier((level, tiles))
    parts = [level[low * ROWS : high * ROWS] for _, low, high in LAST]
    small = take_from(parts[5], LAST[5][0])
    parts[2], small, early = lax.optimization_barrier((parts[2], small, early))
    pieces = [take_from(part, last[0]) for part, last in zip(parts[:5], LAST)]
    tiles = tiles.reshape(32, 6, 40, 128).transpose(1, 0, 2, 3).reshape(6, CH, 128)
    pieces[0], tiles = lax.optimization_barrier((pieces[0], tiles))
    return [level] + pieces + [small], tiles, early


def assemble_kernel(slots, *refs):
    out = refs[-1]
    spot = 0
    for ref in refs[:-1]:
        for row in range(ref.shape[0] // ROWS):
            out[slots[spot]] = ref[pl.ds(row * ROWS, ROWS), :]
            spot += 1


def assemble(slots, pieces):
    return pl.pallas_call(
        assemble_kernel,
        out_shape=jax.ShapeDtypeStruct((64, ROWS, CH), jnp.bfloat16),
        in_specs=[pl.BlockSpec(memory_space=pltpu.SMEM)] + [pl.BlockSpec(memory_space=pltpu.VMEM)] * 7,
        out_specs=pl.BlockSpec(memory_space=pltpu.VMEM),
        compiler_params=pltpu.CompilerParams(vmem_limit_bytes=16 * 1024 * 1024),
        name="assemble",
    )(slots, *pieces)


def shift_lanes(value, row_off, col_off):
    amount = 32 * row_off + col_off
    moved = pltpu.roll(value, (-amount) % LANES, 1) if amount else value
    lane = lax.broadcasted_iota(jnp.int32, (1, LANES), 1)
    row = lane // 32 + row_off
    col = lane % 8 + col_off
    inside = (row >= 0) & (row < 32) & (col >= 0) & (col < 8)
    return jnp.where(inside, moved, 0.0)


def gram_kernel(first_ref, own_hbm, other_hbm, pick_ref, order_ref, scale_ref, out_ref, token_ref, left, acc, staged, pixels, sems, loads):
    copies = []
    for group in range(4):
        source = own_hbm if group < 2 else other_hbm
        rows = pl.ds((group % 2) * LANES, LANES)
        target = pixels.at[pl.ds(group * LANES, LANES)]
        copies.append(pltpu.make_async_copy(source.at[rows], target, loads.at[group]))
        copies[-1].start()
    del token_ref
    pick = pick_ref[...]
    order = order_ref[...]
    for group in range(4):
        copies[group].wait()
        rows = pixels[pl.ds(group * LANES, LANES), :]
        slab = lax.dot_general(pick, rows, (((1,), (1,)), ((), ())), preferred_element_type=jnp.float32)
        shifted = [shift_lanes(slab, t // 3 - 1, t % 3 - 1) for t in range(TAPS)]
        stacked = jnp.concatenate(shifted, axis=0).astype(jnp.bfloat16)
        patch = jnp.dot(order, stacked, preferred_element_type=jnp.float32)
        patch = patch * scale_ref[pl.ds(group, 1), :]
        for t in range(TAPS):
            left[pl.ds(t * MPAD, MPAD), pl.ds(group * LANES, LANES)] = shift_lanes(
                patch, 1 - t // 3, 1 - t % 3
            ).astype(jnp.bfloat16)

    first = first_ref[0]
    lane = lax.broadcasted_iota(jnp.int32, (MPAD, 128), 1)
    row = lax.broadcasted_iota(jnp.int32, (MPAD, 128), 0)

    def weave(values, part):
        spot = lane + 128 * part
        index = spot // 3
        result = None
        for k in range(3):
            moved = jnp.take_along_axis(values[k], index, axis=1)
            result = moved if result is None else jnp.where(spot % 3 == k, moved, result)
        return result

    def multiply(n):
        lanes = pl.ds(n * 256, 256)

        for m in range(3):
            acc[pl.ds(m * 288, 288), lanes] = jnp.dot(left[pl.ds(m * 288, 288), :], pixels[:, lanes], preferred_element_type=jnp.float32)

    def interleave(block):
        lanes = pl.ds(block * 128, 128)
        inner = [
            [weave([acc[pl.ds((3 * a + b) * MPAD, MPAD), lanes] for a in range(3)], part) for part in range(3)]
            for b in range(3)
        ]
        for tile in range(9):
            value = weave([inner[b][tile // 3] for b in range(3)], tile % 3)
            base = block * 1152 + tile * 128
            value = jnp.where(row + first == lane + base, value, keep_off * value)
            staged[:, pl.ds(base, 128)] = value[:90]

    def send(block):
        wide = pl.ds(block * 1152, 1152)
        pltpu.make_async_copy(staged.at[:, wide], out_ref.at[:, wide], sems.at[block]).start()

    multiply(0)
    for n in range(5):
        if n < 4:
            multiply(n + 1)
        interleave(2 * n)
        interleave(2 * n + 1)
        send(2 * n)
        send(2 * n + 1)

    for block in range(10):
        wide = pl.ds(block * 1152, 1152)
        pltpu.make_async_copy(staged.at[:, wide], out_ref.at[:, wide], sems.at[block]).wait()


def gram(first, own, other, pick, order, scale):
    whole = pl.BlockSpec(memory_space=pltpu.VMEM)
    held = pl.BlockSpec(memory_space=pltpu.HBM)
    return pl.pallas_call(
        gram_kernel,
        out_shape=(jax.ShapeDtypeStruct((90, 11520), jnp.float32), jax.ShapeDtypeStruct((8, 128), jnp.float32)),
        in_specs=[pl.BlockSpec(memory_space=pltpu.SMEM), held, held] + [whole] * 3,
        out_specs=(held, held),
        scratch_shapes=[
            pltpu.VMEM((TAPS * MPAD, 4 * LANES), jnp.bfloat16),
            pltpu.VMEM((TAPS * MPAD, CH), jnp.float32),
            pltpu.VMEM((90, 11520), jnp.float32),
            pltpu.VMEM((4 * LANES, CH), jnp.bfloat16),
            pltpu.SemaphoreType.DMA((10,)),
            pltpu.SemaphoreType.DMA((4,)),
        ],
        compiler_params=pltpu.CompilerParams(vmem_limit_bytes=58 * 1024 * 1024),
        cost_estimate=pl.CostEstimate(flops=20_000_000_000, bytes_accessed=20_000_000, transcendentals=0),
        name="gram",
    )(first, own, other, pick, order, scale)


def pack_kernel(weights_ref, order_ref, out_ref, ordered):
    lane = lax.broadcasted_iota(jnp.int32, (1, 128), 1)
    for c in range(2):
        ordered[...] = jnp.dot(order_ref[...], weights_ref[c], preferred_element_type=jnp.float32)
        for dest in range(32):
            tile, off = divmod(dest * 40, 128)
            total = jnp.zeros((120, 128), jnp.float32)
            for b in range(3):
                rows = pl.ds(b * 120, 120)
                amount = (b * 40 - off) % 128
                value = ordered[rows, pl.ds(tile * 128, 128)]
                value = pltpu.roll(value, amount, 1) if amount else value
                if off + 40 > 128:
                    nxt = ordered[rows, pl.ds(tile * 128 + 128, 128)]
                    nxt = pltpu.roll(nxt, amount, 1) if amount else nxt
                    value = jnp.where(lane < b * 40 + 128 - off, value, nxt)
                total = jnp.where((lane >= b * 40) & (lane < b * 40 + 40), value, total)
            out_ref[dest, pl.ds(c * 120, 120), :] = total.astype(jnp.bfloat16)


def pack(weights, order):
    whole = pl.BlockSpec(memory_space=pltpu.VMEM)
    return pl.pallas_call(
        pack_kernel,
        out_shape=jax.ShapeDtypeStruct((32, 240, 128), jnp.bfloat16),
        in_specs=[whole] * 2,
        out_specs=whole,
        scratch_shapes=[pltpu.VMEM((360, CH), jnp.float32)],
        compiler_params=pltpu.CompilerParams(vmem_limit_bytes=24 * 1024 * 1024),
        cost_estimate=pl.CostEstimate(flops=1_000_000_000, bytes_accessed=6_000_000, transcendentals=0),
        name="pack",
    )(weights, order)


def shift_rows(value, amount):
    if amount == 0:
        return value
    pad = jnp.zeros((abs(amount), value.shape[1]), value.dtype)
    if amount > 0:
        return jnp.concatenate([value[amount:], pad], axis=0)
    return jnp.concatenate([pad, value[:amount]], axis=0)


def shift_cols(value, amount):
    if amount == 0:
        return value
    moved = pltpu.roll(value, (-amount) % value.shape[0], 0)
    col = lax.broadcasted_iota(jnp.int32, (value.shape[0], 1), 0) % 8 + amount
    return jnp.where((col >= 0) & (col < 8), moved, 0.0)


def rhs_kernel(scale_ref, pixels_ref, tiles_ref, out_ref, rhs, staged):
    lane = lax.broadcasted_iota(jnp.int32, (1, 128), 1)
    tap_row = lax.broadcasted_iota(jnp.int32, (16, 384), 0)
    tap_lane = lax.broadcasted_iota(jnp.int32, (16, 384), 1)
    spread = (tap_row == (tap_lane // 128) * 3 + (tap_lane % 128) // 40).astype(jnp.bfloat16)
    for c in range(2):
        scale = scale_ref[c]
        pixels = pixels_ref[...].reshape(32, 2, 16, CH)[:, c].reshape(512, CH)
        tiles = jnp.concatenate([tiles_ref[c * 3 + a] for a in range(3)], axis=1)
        taps = jnp.dot(pixels, tiles, preferred_element_type=jnp.float32)
        by_col = shift_rows(taps[:, :128], -16) + taps[:, 128:256] + shift_rows(taps[:, 256:], 16)
        out = shift_cols(by_col, -1)
        out += pltpu.roll(by_col, 88, 1)
        out += shift_cols(pltpu.roll(by_col, 48, 1), 1)
        out = jnp.where(lane < 40, out, 0.0).astype(jnp.bfloat16).astype(jnp.float32) * scale
        moved = shift_cols(out, 1)
        moved += pltpu.roll(out, 40, 1)
        moved += pltpu.roll(shift_cols(out, -1), 80, 1)
        moved = jnp.concatenate([shift_rows(moved, 16), moved, shift_rows(moved, -16)], axis=1)
        cross = lax.dot_general(
            pixels, moved.astype(jnp.bfloat16), (((0,), (0,)), ((), ())), preferred_element_type=jnp.float32
        )
        top = bottom = total = None
        for h in range(32):
            part = jnp.zeros((8, CH), jnp.float32)
            for slot in range(2):
                value = pixels[h * 16 + slot * 8 : h * 16 + slot * 8 + 8].astype(jnp.float32)
                part += value * value
            total = part if total is None else total + part
            if h == 0:
                top = part
            if h == 31:
                bottom = part
        col = lax.broadcasted_iota(jnp.int32, (8, 1), 0)
        diag = []
        for kept in (total - bottom, total, total - top):
            diag.append(jnp.sum(jnp.where(col < 7, kept, 0.0), axis=0, keepdims=True))
            diag.append(jnp.sum(kept, axis=0, keepdims=True))
            diag.append(jnp.sum(jnp.where(col > 0, kept, 0.0), axis=0, keepdims=True))
        diag = jnp.concatenate(diag + [jnp.zeros((7, CH), jnp.float32)], axis=0)
        diag = diag * (scale * (1.0 - keep_off))
        wide = None
        for _ in range(3):
            head = diag.astype(jnp.bfloat16)
            part = lax.dot_general(head, spread, (((0,), (0,)), ((), ())), preferred_element_type=jnp.float32)
            wide = part if wide is None else wide + part
            diag = diag - head.astype(jnp.float32)
        value = keep_off * cross + wide * tiles.astype(jnp.float32)
        rhs[...] = value if c == 0 else rhs[...] + value
    zeros = jnp.zeros((2, 128), jnp.float32)
    for part in range(8):
        for dest in range(part * 16, part * 16 + 16):
            for a in range(3):
                staged[dest, pl.ds(a * OWN, OWN), :] = rhs[pl.ds(dest * OWN, OWN), pl.ds(a * 128, 128)]
            staged[dest, pl.ds(30, 2), :] = zeros
        some = pl.ds(part * 16, 16)
        out_ref[some] = staged[some].astype(jnp.bfloat16)


def rhs_part(scale, pixels, tiles):
    whole = pl.BlockSpec(memory_space=pltpu.VMEM)
    return pl.pallas_call(
        rhs_kernel,
        out_shape=jax.ShapeDtypeStruct((128, 32, 128), jnp.bfloat16),
        in_specs=[pl.BlockSpec(memory_space=pltpu.SMEM), pl.BlockSpec((1024, CH), lambda i: (0, 0)), pl.BlockSpec((6, CH, 128), lambda i: (0, 0, 0))],
        grid=(1,),
        out_specs=pl.BlockSpec((128, 32, 128), lambda i: (0, 0, 0)),
        scratch_shapes=[
            pltpu.VMEM((CH, 384), jnp.float32),
            pltpu.VMEM((128, 32, 128), jnp.float32),
        ],
        compiler_params=pltpu.CompilerParams(vmem_limit_bytes=48 * 1024 * 1024),
        cost_estimate=pl.CostEstimate(flops=4_000_000_000, bytes_accessed=8_000_000, transcendentals=0),
        name="rhs_part",
    )(scale, pixels, tiles)


def finish_kernel(sent_ref, after_ref, out_ref, rows):
    del after_ref
    lane = lax.broadcasted_iota(jnp.int32, (1, 128), 1)
    for tile in range(10):
        first = tile * 128 // 40
        last = (tile * 128 + 127) // 40
        values = [jnp.zeros((32, 128), jnp.float32)] * 3
        for b in range(first, last + 1):
            total = jnp.sum(sent_ref[pl.ds(b * 4, 4)].astype(jnp.float32), axis=0)
            start = b * 40 - tile * 128
            keep = (lane >= start) & (lane < start + 40)
            for t in range(3):
                amount = (start - t * 40) % 128
                moved = pltpu.roll(total, amount, 1) if amount else total
                values[t] = jnp.where(keep, moved, values[t])
        for t in range(3):
            rows[pl.ds(t * 32, 32), pl.ds(tile * 128, 128)] = values[t]
    dst = lax.broadcasted_iota(jnp.int32, (MPAD, 96), 0)
    src = lax.broadcasted_iota(jnp.int32, (MPAD, 96), 1)
    inner = src % 32
    pick = (dst == (inner % OWN) * TAPS + (inner // OWN) * 3 + src // 32) & (inner < 30)
    pick = pick.astype(jnp.bfloat16)
    value = rows[...]
    result = None
    for _ in range(3):
        head = value.astype(jnp.bfloat16)
        part = jnp.dot(pick, head, preferred_element_type=jnp.float32)
        result = part if result is None else result + part
        value = value - head.astype(jnp.float32)
    out_ref[...] = result[:90]


def finish(sent, after):
    whole = pl.BlockSpec(memory_space=pltpu.VMEM)
    return pl.pallas_call(
        finish_kernel,
        out_shape=jax.ShapeDtypeStruct((90, CH), jnp.float32),
        in_specs=[whole, pl.BlockSpec(memory_space=pltpu.HBM)],
        out_specs=whole,
        scratch_shapes=[pltpu.VMEM((96, CH), jnp.float32)],
        compiler_params=pltpu.CompilerParams(vmem_limit_bytes=16 * 1024 * 1024),
        name="finish",
    )(sent, after)


def body(activations, sample_count, client_weights):
    client_here = lax.axis_index("client")
    blk_here = lax.axis_index("blk")
    x_hi, core = client_here // 2, client_here % 2
    z, x_lo, y = blk_here // 8, (blk_here // 4) % 2, blk_here % 4
    x = x_hi * 2 + x_lo

    counts = sample_count.astype(jnp.float32)
    all_scale = 1.0 / (8 * counts * 256)
    mine = lax.dynamic_slice_in_dim(sample_count, client_here * 2, 2)
    my_scale = lax.dynamic_slice_in_dim(all_scale, client_here * 2, 2)

    row = lax.broadcasted_iota(jnp.int32, (360, 360), 0)
    col = lax.broadcasted_iota(jnp.int32, (360, 360), 1)
    tap_order = (col == (row % 40) * TAPS + (row // 40) % 3 * 3 + row // 120).astype(jnp.bfloat16)
    packed = pack(client_weights, tap_order)

    live = lax.broadcasted_iota(jnp.int32, (2, 2), 1) < mine[:, None]
    first_channel = blk_here * 40 + client_here * OWN
    chan = lax.broadcasted_iota(jnp.int32, (16, CH), 1) - first_channel
    lane = lax.broadcasted_iota(jnp.int32, (16, CH), 0)
    pick = ((chan == lane) & (lane < OWN)).astype(jnp.bfloat16)
    row = lax.broadcasted_iota(jnp.int32, (MPAD, TAPS * 16), 0)
    col = lax.broadcasted_iota(jnp.int32, (MPAD, TAPS * 16), 1)
    order = ((row // TAPS == col % 16) & (row % TAPS == col // 16)).astype(jnp.bfloat16)
    groups = jnp.stack([client_here, client_here ^ 2, client_here ^ 1, client_here ^ 3])
    group_scale = all_scale.reshape(4, 2)[groups]
    img_scale = jnp.repeat(jnp.repeat(group_scale, 16, axis=1)[:, None, :], 32, axis=1).reshape(4, LANES)

    masked = jnp.where(live[:, :, None, None, None], activations, jnp.zeros_like(activations))
    offs = np.array(SOURCES, np.int32)
    src_x, src_y, src_z = (x + offs[:, 0]) % 4, (y + offs[:, 1]) % 4, (z + offs[:, 2]) % 4
    away = (src_x // 2 != x_hi).astype(jnp.int32)
    slots = (away * 32 + src_z * 8 + (src_x % 2) * 4 + src_y).astype(jnp.int32)
    pieces, tiles, early = gather_chips(masked.reshape(ROWS, CH), packed, (pick, order, img_scale, slots))
    pick, order, img_scale, slots = early
    own = assemble(slots, pieces)
    other = lax.ppermute(own, AXES, [(d, d ^ 32) for d in range(128)])

    own_rows = own.reshape(2048, CH)
    part = rhs_part(my_scale, own_rows, tiles)
    sent = lax.all_to_all(part, ("blk", "client"), split_axis=0, concat_axis=0, tiled=True)

    gram_out, token = gram(
        jnp.reshape(first_channel * TAPS, (1,)), own_rows, other.reshape(2048, CH),
        pick, order, img_scale,
    )
    return gram_out, finish(sent, token)


def solution(mesh):
    in_specs = (P("client", None, "blk", None, None), P(), P("client", "blk", None))
    out_specs = (P(("blk", "client"), None), P(("blk", "client"), None))
    return jax.shard_map(body, mesh=mesh, in_specs=in_specs, out_specs=out_specs, check_vma=False)
```

```python
import jax
import jax.numpy as jnp
import numpy as np
from jax import lax
from jax.experimental import pallas as pl
from jax.experimental.pallas import tpu as pltpu
from jax.sharding import PartitionSpec as P

keep_off = 0.9
AXES = ("client", "blk")
CHIPS = 4
ROWS = 32
CH = 1280
LANES = 1024
TAPS = 9
OWN = 10
MPAD = 96


def split_device(index):
    client, blk = divmod(index, 32)
    x_hi, core = divmod(client, 2)
    z, rest = divmod(blk, 8)
    x_lo, y = divmod(rest, 4)
    return x_hi * 2 + x_lo, y, z, core


def join_device(x, y, z, core):
    return ((x // 2) * 2 + core) * 32 + z * 8 + (x % 2) * 4 + y


def take_from(value, offset):
    pairs = []
    for dst in range(128):
        x, y, z, core = split_device(dst)
        src = join_device((x + offset[0]) % 4, (y + offset[1]) % 4, (z + offset[2]) % 4, core)
        pairs.append((src, dst))
    return lax.ppermute(value, AXES, pairs)


LAST = [((1, 0, 0), 1, 0, 16), ((0, 0, 3), 1, 16, 32), ((3, 0, 0), 3, 0, 16), ((0, 0, 1), 3, 16, 32), ((0, 1, 0), 2, 0, 24), ((0, 3, 0), 2, 24, 32)]


def share_kernel(mine_ref, theirs_ref, out_ref):
    for dest in range(32):
        z, rest = divmod(dest, 8)
        x_lo, y = divmod(rest, 4)
        kind = (x_lo - z + 2 * y) % 4
        source = mine_ref if kind < 2 else theirs_ref
        out_ref[dest] = source[pl.ds(kind % 2 * 16, 16), :]


def share(mine, theirs):
    whole = pl.BlockSpec(memory_space=pltpu.VMEM)
    return pl.pallas_call(
        share_kernel,
        out_shape=jax.ShapeDtypeStruct((32, 16, CH), jnp.bfloat16),
        in_specs=[whole] * 2,
        out_specs=whole,
        name="share",
    )(mine, theirs)


def gather_chips(block, packed, early):
    theirs = lax.ppermute(block, AXES, [(d, d ^ 64) for d in range(128)])
    level = lax.all_to_all(share(block, theirs), "blk", split_axis=0, concat_axis=0, tiled=True)
    tiles = lax.all_to_all(packed, "blk", split_axis=0, concat_axis=0, tiled=True)
    parts = [level[low:high] for _, _, low, high in LAST]
    small = take_from(parts[5], LAST[5][0])
    parts[2], small, early, tiles = lax.optimization_barrier((parts[2], small, early, tiles))
    pieces = [take_from(part, last[0]) for part, last in zip(parts[:5], LAST)]
    tiles = tiles.reshape(32, 6, 40, 128).transpose(1, 0, 2, 3).reshape(6, CH, 128)
    pieces[0], tiles = lax.optimization_barrier((pieces[0], tiles))
    return [level] + pieces + [small], tiles, early


def assemble_kernel(slots, *refs):
    out = refs[-1]
    for h in range(32):
        out[slots[0], pl.ds(h * 16, 16), :] = refs[0][h]
    for ref, (_, kind, low, high) in zip(refs[1:-1], LAST):
        for h in range(low, high):
            out[slots[kind], pl.ds(h * 16, 16), :] = ref[h - low]


def assemble(slots, pieces):
    return pl.pallas_call(
        assemble_kernel,
        out_shape=jax.ShapeDtypeStruct((4, 512, CH), jnp.bfloat16),
        in_specs=[pl.BlockSpec(memory_space=pltpu.SMEM)] + [pl.BlockSpec(memory_space=pltpu.VMEM)] * 7,
        out_specs=pl.BlockSpec(memory_space=pltpu.VMEM),
        compiler_params=pltpu.CompilerParams(vmem_limit_bytes=16 * 1024 * 1024),
        name="assemble",
    )(slots, *pieces)


def shift_lanes(value, row_off, col_off):
    amount = 16 * row_off + col_off
    moved = pltpu.roll(value, (-amount) % LANES, 1) if amount else value
    lane = lax.broadcasted_iota(jnp.int32, (1, LANES), 1)
    row = lane // 16 % 32 + row_off
    col = lane % 8 + col_off
    inside = (row >= 0) & (row < 32) & (col >= 0) & (col < 8)
    return jnp.where(inside, moved, 0.0)


def gram_kernel(first_ref, own_hbm, other_hbm, pick_ref, order_ref, scale_ref, out_ref, token_ref, left, acc, staged, pixels, sems, loads):
    copies = []
    for group in range(4):
        source = own_hbm if group < 2 else other_hbm
        rows = pl.ds((group % 2) * LANES, LANES)
        target = pixels.at[pl.ds(group * LANES, LANES)]
        copies.append(pltpu.make_async_copy(source.at[rows], target, loads.at[group]))
        copies[-1].start()
    del token_ref
    pick = pick_ref[...]
    order = order_ref[...]
    for group in range(4):
        copies[group].wait()
        rows = pixels[pl.ds(group * LANES, LANES), :]
        slab = lax.dot_general(pick, rows, (((1,), (1,)), ((), ())), preferred_element_type=jnp.float32)
        shifted = [shift_lanes(slab, t // 3 - 1, t % 3 - 1) for t in range(TAPS)]
        stacked = jnp.concatenate(shifted, axis=0).astype(jnp.bfloat16)
        patch = jnp.dot(order, stacked, preferred_element_type=jnp.float32)
        patch = patch * scale_ref[pl.ds(group, 1), :]
        for t in range(TAPS):
            left[pl.ds(t * MPAD, MPAD), pl.ds(group * LANES, LANES)] = shift_lanes(
                patch, 1 - t // 3, 1 - t % 3
            ).astype(jnp.bfloat16)

    first = first_ref[0]
    lane = lax.broadcasted_iota(jnp.int32, (MPAD, 128), 1)
    row = lax.broadcasted_iota(jnp.int32, (MPAD, 128), 0)

    def weave(values, part):
        spot = lane + 128 * part
        index = spot // 3
        result = None
        for k in range(3):
            moved = jnp.take_along_axis(values[k], index, axis=1)
            result = moved if result is None else jnp.where(spot % 3 == k, moved, result)
        return result

    def multiply(n):
        lanes = pl.ds(n * 256, 256)

        for m in range(3):
            acc[pl.ds(m * 288, 288), lanes] = jnp.dot(left[pl.ds(m * 288, 288), :], pixels[:, lanes], preferred_element_type=jnp.float32)

    def interleave(block):
        lanes = pl.ds(block * 128, 128)
        inner = [
            [weave([acc[pl.ds((3 * a + b) * MPAD, MPAD), lanes] for a in range(3)], part) for part in range(3)]
            for b in range(3)
        ]
        for tile in range(9):
            value = weave([inner[b][tile // 3] for b in range(3)], tile % 3)
            base = block * 1152 + tile * 128
            value = jnp.where(row + first == lane + base, value, keep_off * value)
            staged[:, pl.ds(base, 128)] = value[:90]

    def send(block):
        wide = pl.ds(block * 1152, 1152)
        pltpu.make_async_copy(staged.at[:, wide], out_ref.at[:, wide], sems.at[block]).start()

    multiply(0)
    for n in range(5):
        if n < 4:
            multiply(n + 1)
        interleave(2 * n)
        interleave(2 * n + 1)
        send(2 * n)
        send(2 * n + 1)

    for block in range(10):
        wide = pl.ds(block * 1152, 1152)
        pltpu.make_async_copy(staged.at[:, wide], out_ref.at[:, wide], sems.at[block]).wait()


def gram(first, own, other, pick, order, scale):
    whole = pl.BlockSpec(memory_space=pltpu.VMEM)
    held = pl.BlockSpec(memory_space=pltpu.HBM)
    return pl.pallas_call(
        gram_kernel,
        out_shape=(jax.ShapeDtypeStruct((90, 11520), jnp.float32), jax.ShapeDtypeStruct((8, 128), jnp.float32)),
        in_specs=[pl.BlockSpec(memory_space=pltpu.SMEM), held, held] + [whole] * 3,
        out_specs=(held, held),
        scratch_shapes=[
            pltpu.VMEM((TAPS * MPAD, 4 * LANES), jnp.bfloat16),
            pltpu.VMEM((TAPS * MPAD, CH), jnp.float32),
            pltpu.VMEM((90, 11520), jnp.float32),
            pltpu.VMEM((4 * LANES, CH), jnp.bfloat16),
            pltpu.SemaphoreType.DMA((10,)),
            pltpu.SemaphoreType.DMA((4,)),
        ],
        compiler_params=pltpu.CompilerParams(vmem_limit_bytes=58 * 1024 * 1024),
        cost_estimate=pl.CostEstimate(flops=20_000_000_000, bytes_accessed=20_000_000, transcendentals=0),
        name="gram",
    )(first, own, other, pick, order, scale)


def pack_kernel(weights_ref, order_ref, out_ref, ordered):
    lane = lax.broadcasted_iota(jnp.int32, (1, 128), 1)
    for c in range(2):
        ordered[...] = jnp.dot(order_ref[...], weights_ref[c], preferred_element_type=jnp.float32)
        for dest in range(32):
            tile, off = divmod(dest * 40, 128)
            total = jnp.zeros((120, 128), jnp.float32)
            for b in range(3):
                rows = pl.ds(b * 120, 120)
                amount = (b * 40 - off) % 128
                value = ordered[rows, pl.ds(tile * 128, 128)]
                value = pltpu.roll(value, amount, 1) if amount else value
                if off + 40 > 128:
                    nxt = ordered[rows, pl.ds(tile * 128 + 128, 128)]
                    nxt = pltpu.roll(nxt, amount, 1) if amount else nxt
                    value = jnp.where(lane < b * 40 + 128 - off, value, nxt)
                total = jnp.where((lane >= b * 40) & (lane < b * 40 + 40), value, total)
            out_ref[dest, pl.ds(c * 120, 120), :] = total.astype(jnp.bfloat16)


def pack(weights, order):
    whole = pl.BlockSpec(memory_space=pltpu.VMEM)
    return pl.pallas_call(
        pack_kernel,
        out_shape=jax.ShapeDtypeStruct((32, 240, 128), jnp.bfloat16),
        in_specs=[whole] * 2,
        out_specs=whole,
        scratch_shapes=[pltpu.VMEM((360, CH), jnp.float32)],
        compiler_params=pltpu.CompilerParams(vmem_limit_bytes=24 * 1024 * 1024),
        cost_estimate=pl.CostEstimate(flops=1_000_000_000, bytes_accessed=6_000_000, transcendentals=0),
        name="pack",
    )(weights, order)


def shift_rows(value, amount):
    if amount == 0:
        return value
    pad = jnp.zeros((abs(amount), value.shape[1]), value.dtype)
    if amount > 0:
        return jnp.concatenate([value[amount:], pad], axis=0)
    return jnp.concatenate([pad, value[:amount]], axis=0)


def shift_cols(value, amount):
    if amount == 0:
        return value
    moved = pltpu.roll(value, (-amount) % value.shape[0], 0)
    col = lax.broadcasted_iota(jnp.int32, (value.shape[0], 1), 0) % 8 + amount
    return jnp.where((col >= 0) & (col < 8), moved, 0.0)


def rhs_kernel(scale_ref, pixels_ref, tiles_ref, out_ref, rhs, staged):
    lane = lax.broadcasted_iota(jnp.int32, (1, 128), 1)
    tap_row = lax.broadcasted_iota(jnp.int32, (16, 384), 0)
    tap_lane = lax.broadcasted_iota(jnp.int32, (16, 384), 1)
    spread = (tap_row == (tap_lane // 128) * 3 + (tap_lane % 128) // 40).astype(jnp.bfloat16)
    for c in range(2):
        scale = scale_ref[c]
        pixels = pixels_ref[pl.ds(c * 512, 512), :]
        tiles = jnp.concatenate([tiles_ref[c * 3 + a] for a in range(3)], axis=1)
        taps = jnp.dot(pixels, tiles, preferred_element_type=jnp.float32)
        by_col = shift_rows(taps[:, :128], -16) + taps[:, 128:256] + shift_rows(taps[:, 256:], 16)
        out = shift_cols(by_col, -1)
        out += pltpu.roll(by_col, 88, 1)
        out += shift_cols(pltpu.roll(by_col, 48, 1), 1)
        out = jnp.where(lane < 40, out, 0.0).astype(jnp.bfloat16).astype(jnp.float32) * scale
        moved = shift_cols(out, 1)
        moved += pltpu.roll(out, 40, 1)
        moved += pltpu.roll(shift_cols(out, -1), 80, 1)
        moved = jnp.concatenate([shift_rows(moved, 16), moved, shift_rows(moved, -16)], axis=1)
        cross = lax.dot_general(
            pixels, moved.astype(jnp.bfloat16), (((0,), (0,)), ((), ())), preferred_element_type=jnp.float32
        )
        top = bottom = total = None
        for h in range(32):
            part = jnp.zeros((8, CH), jnp.float32)
            for slot in range(2):
                value = pixels[h * 16 + slot * 8 : h * 16 + slot * 8 + 8].astype(jnp.float32)
                part += value * value
            total = part if total is None else total + part
            if h == 0:
                top = part
            if h == 31:
                bottom = part
        col = lax.broadcasted_iota(jnp.int32, (8, 1), 0)
        diag = []
        for kept in (total - bottom, total, total - top):
            diag.append(jnp.sum(jnp.where(col < 7, kept, 0.0), axis=0, keepdims=True))
            diag.append(jnp.sum(kept, axis=0, keepdims=True))
            diag.append(jnp.sum(jnp.where(col > 0, kept, 0.0), axis=0, keepdims=True))
        diag = jnp.concatenate(diag + [jnp.zeros((7, CH), jnp.float32)], axis=0)
        diag = diag * (scale * (1.0 - keep_off))
        wide = None
        for _ in range(3):
            head = diag.astype(jnp.bfloat16)
            part = lax.dot_general(head, spread, (((0,), (0,)), ((), ())), preferred_element_type=jnp.float32)
            wide = part if wide is None else wide + part
            diag = diag - head.astype(jnp.float32)
        value = keep_off * cross + wide * tiles.astype(jnp.float32)
        rhs[...] = value if c == 0 else rhs[...] + value
    zeros = jnp.zeros((2, 128), jnp.float32)
    for part in range(8):
        for dest in range(part * 16, part * 16 + 16):
            for a in range(3):
                staged[dest, pl.ds(a * OWN, OWN), :] = rhs[pl.ds(dest * OWN, OWN), pl.ds(a * 128, 128)]
            staged[dest, pl.ds(30, 2), :] = zeros
        some = pl.ds(part * 16, 16)
        out_ref[some] = staged[some].astype(jnp.bfloat16)


def rhs_part(scale, pixels, tiles):
    whole = pl.BlockSpec(memory_space=pltpu.VMEM)
    return pl.pallas_call(
        rhs_kernel,
        out_shape=jax.ShapeDtypeStruct((128, 32, 128), jnp.bfloat16),
        in_specs=[pl.BlockSpec(memory_space=pltpu.SMEM), pl.BlockSpec((1024, CH), lambda i: (0, 0)), pl.BlockSpec((6, CH, 128), lambda i: (0, 0, 0))],
        grid=(1,),
        out_specs=pl.BlockSpec((128, 32, 128), lambda i: (0, 0, 0)),
        scratch_shapes=[
            pltpu.VMEM((CH, 384), jnp.float32),
            pltpu.VMEM((128, 32, 128), jnp.float32),
        ],
        compiler_params=pltpu.CompilerParams(vmem_limit_bytes=48 * 1024 * 1024),
        cost_estimate=pl.CostEstimate(flops=4_000_000_000, bytes_accessed=8_000_000, transcendentals=0),
        name="rhs_part",
    )(scale, pixels, tiles)


def finish_kernel(sent_ref, after_ref, out_ref, rows):
    del after_ref
    lane = lax.broadcasted_iota(jnp.int32, (1, 128), 1)
    for tile in range(10):
        first = tile * 128 // 40
        last = (tile * 128 + 127) // 40
        values = [jnp.zeros((32, 128), jnp.float32)] * 3
        for b in range(first, last + 1):
            total = jnp.sum(sent_ref[pl.ds(b * 4, 4)].astype(jnp.float32), axis=0)
            start = b * 40 - tile * 128
            keep = (lane >= start) & (lane < start + 40)
            for t in range(3):
                amount = (start - t * 40) % 128
                moved = pltpu.roll(total, amount, 1) if amount else total
                values[t] = jnp.where(keep, moved, values[t])
        for t in range(3):
            rows[pl.ds(t * 32, 32), pl.ds(tile * 128, 128)] = values[t]
    dst = lax.broadcasted_iota(jnp.int32, (MPAD, 96), 0)
    src = lax.broadcasted_iota(jnp.int32, (MPAD, 96), 1)
    inner = src % 32
    pick = (dst == (inner % OWN) * TAPS + (inner // OWN) * 3 + src // 32) & (inner < 30)
    pick = pick.astype(jnp.bfloat16)
    value = rows[...]
    result = None
    for _ in range(3):
        head = value.astype(jnp.bfloat16)
        part = jnp.dot(pick, head, preferred_element_type=jnp.float32)
        result = part if result is None else result + part
        value = value - head.astype(jnp.float32)
    out_ref[...] = result[:90]


def finish(sent, after):
    whole = pl.BlockSpec(memory_space=pltpu.VMEM)
    return pl.pallas_call(
        finish_kernel,
        out_shape=jax.ShapeDtypeStruct((90, CH), jnp.float32),
        in_specs=[whole, pl.BlockSpec(memory_space=pltpu.HBM)],
        out_specs=whole,
        scratch_shapes=[pltpu.VMEM((96, CH), jnp.float32)],
        compiler_params=pltpu.CompilerParams(vmem_limit_bytes=16 * 1024 * 1024),
        name="finish",
    )(sent, after)


def body(activations, sample_count, client_weights):
    client_here = lax.axis_index("client")
    blk_here = lax.axis_index("blk")
    x_hi, core = client_here // 2, client_here % 2
    z, x_lo, y = blk_here // 8, (blk_here // 4) % 2, blk_here % 4

    counts = sample_count.astype(jnp.float32)
    all_scale = 1.0 / (8 * counts * 256)
    mine = lax.dynamic_slice_in_dim(sample_count, client_here * 2, 2)
    my_scale = lax.dynamic_slice_in_dim(all_scale, client_here * 2, 2)

    row = lax.broadcasted_iota(jnp.int32, (360, 360), 0)
    col = lax.broadcasted_iota(jnp.int32, (360, 360), 1)
    tap_order = (col == (row % 40) * TAPS + (row // 40) % 3 * 3 + row // 120).astype(jnp.bfloat16)
    packed = pack(client_weights, tap_order)

    live = lax.broadcasted_iota(jnp.int32, (2, 2), 1) < mine[:, None]
    first_channel = blk_here * 40 + client_here * OWN
    chan = lax.broadcasted_iota(jnp.int32, (16, CH), 1) - first_channel
    lane = lax.broadcasted_iota(jnp.int32, (16, CH), 0)
    pick = ((chan == lane) & (lane < OWN)).astype(jnp.bfloat16)
    row = lax.broadcasted_iota(jnp.int32, (MPAD, TAPS * 16), 0)
    col = lax.broadcasted_iota(jnp.int32, (MPAD, TAPS * 16), 1)
    order = ((row // TAPS == col % 16) & (row % TAPS == col // 16)).astype(jnp.bfloat16)
    groups = jnp.stack([client_here, client_here ^ 2, client_here ^ 1, client_here ^ 3])
    group_scale = all_scale.reshape(4, 2)[groups]
    img_scale = jnp.repeat(group_scale, 512, axis=1)

    masked = jnp.where(live[:, :, None, None, None], activations, jnp.zeros_like(activations))
    slots = ((x_lo - z + 2 * y) % 4 + jnp.arange(4, dtype=jnp.int32)) % 4
    pieces, tiles, early = gather_chips(masked.reshape(ROWS, CH), packed, (pick, order, img_scale, slots))
    pick, order, img_scale, slots = early
    own = assemble(slots, pieces)
    other = lax.ppermute(own, AXES, [(d, d ^ 32) for d in range(128)])

    own_rows = own.reshape(2048, CH)
    part = rhs_part(my_scale, own_rows, tiles)
    sent = lax.all_to_all(part, ("blk", "client"), split_axis=0, concat_axis=0, tiled=True)

    gram_out, token = gram(
        jnp.reshape(first_channel * TAPS, (1,)), own_rows, other.reshape(2048, CH),
        pick, order, img_scale,
    )
    return gram_out, finish(sent, token)


def solution(mesh):
    in_specs = (P("client", None, "blk", None, None), P(), P("client", "blk", None))
    out_specs = (P(("blk", "client"), None), P(("blk", "client"), None))
    return jax.shard_map(body, mesh=mesh, in_specs=in_specs, out_specs=out_specs, check_vma=False)
```

```python
import jax
import jax.numpy as jnp
import numpy as np
from jax import lax
from jax.experimental import pallas as pl
from jax.experimental.pallas import tpu as pltpu
from jax.sharding import PartitionSpec as P

keep_off = 0.9
AXES = ("client", "blk")
CHIPS = 4
ROWS = 32
CH = 1280
LANES = 1024
TAPS = 9
OWN = 10
MPAD = 96


def split_device(index):
    client, blk = divmod(index, 32)
    x_hi, core = divmod(client, 2)
    z, rest = divmod(blk, 8)
    x_lo, y = divmod(rest, 4)
    return x_hi * 2 + x_lo, y, z, core


def join_device(x, y, z, core):
    return ((x // 2) * 2 + core) * 32 + z * 8 + (x % 2) * 4 + y


def take_from(value, offset):
    pairs = []
    for dst in range(128):
        x, y, z, core = split_device(dst)
        src = join_device((x + offset[0]) % 4, (y + offset[1]) % 4, (z + offset[2]) % 4, core)
        pairs.append((src, dst))
    return lax.ppermute(value, AXES, pairs)


def vec_add(*vectors):
    return tuple(sum(parts) % 4 for parts in zip(*vectors))


STEP = (1, 0, 1)
FIRST = [tuple(k * s % 4 for s in STEP) for k in range(4)]
SECOND = [(0, 0, 0), (1, 1, 3), (0, 2, 0), (3, 3, 1)]
LEVEL = [vec_add(g, f) for g in SECOND for f in FIRST]
LAST = [((1, 0, 0), 0, 8), ((0, 0, 3), 8, 16), ((3, 0, 0), 0, 8), ((0, 0, 1), 8, 16), ((0, 1, 0), 0, 12), ((0, 3, 0), 4, 8)]
SOURCES = list(LEVEL)
for away, low, high in LAST:
    SOURCES += [vec_add(away, o) for o in LEVEL[low:high]]
assert len(SOURCES) == 64 and len(set(SOURCES)) == 64


def gather_chips(block, packed, early):
    tiles = lax.all_to_all(packed, "blk", split_axis=0, concat_axis=0, tiled=True)
    level = jnp.concatenate([block] + [take_from(block, o) for o in FIRST[1:]], axis=0)
    level = jnp.concatenate([level] + [take_from(level, o) for o in SECOND[1:]], axis=0)
    level, tiles = lax.optimization_barrier((level, tiles))
    parts = [level[low * ROWS : high * ROWS] for _, low, high in LAST]
    small = take_from(parts[5], LAST[5][0])
    parts[2], small, early = lax.optimization_barrier((parts[2], small, early))
    pieces = [take_from(part, last[0]) for part, last in zip(parts[:5], LAST)]
    tiles = tiles.reshape(32, 6, 40, 128).transpose(1, 0, 2, 3).reshape(6, CH, 128)
    pieces[0], tiles = lax.optimization_barrier((pieces[0], tiles))
    return [level] + pieces + [small], tiles, early


def assemble_kernel(slots, *refs):
    out = refs[-1]
    spot = 0
    for ref in refs[:-1]:
        for row in range(ref.shape[0] // ROWS):
            out[slots[spot]] = ref[pl.ds(row * ROWS, ROWS), :]
            spot += 1


def assemble(slots, pieces):
    return pl.pallas_call(
        assemble_kernel,
        out_shape=jax.ShapeDtypeStruct((64, ROWS, CH), jnp.bfloat16),
        in_specs=[pl.BlockSpec(memory_space=pltpu.SMEM)] + [pl.BlockSpec(memory_space=pltpu.VMEM)] * 7,
        out_specs=pl.BlockSpec(memory_space=pltpu.VMEM),
        compiler_params=pltpu.CompilerParams(vmem_limit_bytes=16 * 1024 * 1024),
        name="assemble",
    )(slots, *pieces)


def shift_lanes(value, row_off, col_off):
    amount = 32 * row_off + col_off
    moved = pltpu.roll(value, (-amount) % LANES, 1) if amount else value
    lane = lax.broadcasted_iota(jnp.int32, (1, LANES), 1)
    row = lane // 32 + row_off
    col = lane % 8 + col_off
    inside = (row >= 0) & (row < 32) & (col >= 0) & (col < 8)
    return jnp.where(inside, moved, 0.0)


def gram_kernel(first_ref, own_hbm, other_hbm, pick_ref, order_ref, scale_ref, out_ref, left, acc, staged, pixels, sems, loads):
    copies = []
    for group in range(4):
        source = own_hbm if group < 2 else other_hbm
        rows = pl.ds((group % 2) * LANES, LANES)
        target = pixels.at[pl.ds(group * LANES, LANES)]
        copies.append(pltpu.make_async_copy(source.at[rows], target, loads.at[group]))
        copies[-1].start()
    pick = pick_ref[...]
    order = order_ref[...]
    for group in range(4):
        copies[group].wait()
        rows = pixels[pl.ds(group * LANES, LANES), :]
        slab = lax.dot_general(pick, rows, (((1,), (1,)), ((), ())), preferred_element_type=jnp.float32)
        shifted = [shift_lanes(slab, t // 3 - 1, t % 3 - 1) for t in range(TAPS)]
        stacked = jnp.concatenate(shifted, axis=0).astype(jnp.bfloat16)
        patch = jnp.dot(order, stacked, preferred_element_type=jnp.float32)
        patch = patch * scale_ref[pl.ds(group, 1), :]
        for t in range(TAPS):
            left[pl.ds(t * MPAD, MPAD), pl.ds(group * LANES, LANES)] = shift_lanes(
                patch, 1 - t // 3, 1 - t % 3
            ).astype(jnp.bfloat16)

    first = first_ref[0]
    lane = lax.broadcasted_iota(jnp.int32, (MPAD, 128), 1)
    row = lax.broadcasted_iota(jnp.int32, (MPAD, 128), 0)

    def weave(values, part):
        spot = lane + 128 * part
        index = spot // 3
        result = None
        for k in range(3):
            moved = jnp.take_along_axis(values[k], index, axis=1)
            result = moved if result is None else jnp.where(spot % 3 == k, moved, result)
        return result

    def multiply(n):
        lanes = pl.ds(n * 256, 256)

        for m in range(3):
            acc[pl.ds(m * 288, 288), lanes] = jnp.dot(left[pl.ds(m * 288, 288), :], pixels[:, lanes], preferred_element_type=jnp.float32)

    def interleave(block):
        lanes = pl.ds(block * 128, 128)
        inner = [
            [weave([acc[pl.ds((3 * a + b) * MPAD, MPAD), lanes] for a in range(3)], part) for part in range(3)]
            for b in range(3)
        ]
        for tile in range(9):
            value = weave([inner[b][tile // 3] for b in range(3)], tile % 3)
            base = block * 1152 + tile * 128
            value = jnp.where(row + first == lane + base, value, keep_off * value)
            staged[:, pl.ds(base, 128)] = value[:90]

    def send(block):
        wide = pl.ds(block * 1152, 1152)
        pltpu.make_async_copy(staged.at[:, wide], out_ref.at[:, wide], sems.at[block]).start()

    multiply(0)
    for n in range(5):
        if n < 4:
            multiply(n + 1)
        interleave(2 * n)
        interleave(2 * n + 1)
        send(2 * n)
        send(2 * n + 1)

    for block in range(10):
        wide = pl.ds(block * 1152, 1152)
        pltpu.make_async_copy(staged.at[:, wide], out_ref.at[:, wide], sems.at[block]).wait()


def gram(first, own, other, pick, order, scale):
    whole = pl.BlockSpec(memory_space=pltpu.VMEM)
    held = pl.BlockSpec(memory_space=pltpu.HBM)
    return pl.pallas_call(
        gram_kernel,
        out_shape=jax.ShapeDtypeStruct((90, 11520), jnp.float32),
        in_specs=[pl.BlockSpec(memory_space=pltpu.SMEM), held, held] + [whole] * 3,
        out_specs=held,
        scratch_shapes=[
            pltpu.VMEM((TAPS * MPAD, 4 * LANES), jnp.bfloat16),
            pltpu.VMEM((TAPS * MPAD, CH), jnp.float32),
            pltpu.VMEM((90, 11520), jnp.float32),
            pltpu.VMEM((4 * LANES, CH), jnp.bfloat16),
            pltpu.SemaphoreType.DMA((10,)),
            pltpu.SemaphoreType.DMA((4,)),
        ],
        compiler_params=pltpu.CompilerParams(vmem_limit_bytes=58 * 1024 * 1024),
        cost_estimate=pl.CostEstimate(flops=20_000_000_000, bytes_accessed=20_000_000, transcendentals=0),
        name="gram",
    )(first, own, other, pick, order, scale)


def pack_kernel(weights_hbm, out_ref, weights, ordered, loads):
    copies = [pltpu.make_async_copy(weights_hbm.at[c], weights.at[c], loads.at[c]) for c in range(2)]
    for copy in copies:
        copy.start()
    lane = lax.broadcasted_iota(jnp.int32, (1, 128), 1)
    row = lax.broadcasted_iota(jnp.int32, (360, 360), 0)
    col = lax.broadcasted_iota(jnp.int32, (360, 360), 1)
    order = (col == (row % 40) * TAPS + (row // 40) % 3 * 3 + row // 120).astype(jnp.bfloat16)
    for c in range(2):
        copies[c].wait()
        ordered[...] = jnp.dot(order, weights[c], preferred_element_type=jnp.float32)
        for dest in range(32):
            tile, off = divmod(dest * 40, 128)
            total = jnp.zeros((120, 128), jnp.float32)
            for b in range(3):
                rows = pl.ds(b * 120, 120)
                amount = (b * 40 - off) % 128
                value = ordered[rows, pl.ds(tile * 128, 128)]
                value = pltpu.roll(value, amount, 1) if amount else value
                if off + 40 > 128:
                    nxt = ordered[rows, pl.ds(tile * 128 + 128, 128)]
                    nxt = pltpu.roll(nxt, amount, 1) if amount else nxt
                    value = jnp.where(lane < b * 40 + 128 - off, value, nxt)
                total = jnp.where((lane >= b * 40) & (lane < b * 40 + 40), value, total)
            out_ref[dest, pl.ds(c * 120, 120), :] = total.astype(jnp.bfloat16)


def pack(weights):
    return pl.pallas_call(
        pack_kernel,
        out_shape=jax.ShapeDtypeStruct((32, 240, 128), jnp.bfloat16),
        in_specs=[pl.BlockSpec(memory_space=pltpu.HBM)],
        out_specs=pl.BlockSpec(memory_space=pltpu.VMEM),
        scratch_shapes=[
            pltpu.VMEM((2, 360, CH), jnp.bfloat16),
            pltpu.VMEM((360, CH), jnp.float32),
            pltpu.SemaphoreType.DMA((2,)),
        ],
        compiler_params=pltpu.CompilerParams(vmem_limit_bytes=63 * 1024 * 1024),
        cost_estimate=pl.CostEstimate(flops=1_000_000_000, bytes_accessed=6_000_000, transcendentals=0),
        name="pack",
    )(weights)


def shift_rows(value, amount):
    if amount == 0:
        return value
    pad = jnp.zeros((abs(amount), value.shape[1]), value.dtype)
    if amount > 0:
        return jnp.concatenate([value[amount:], pad], axis=0)
    return jnp.concatenate([pad, value[:amount]], axis=0)


def shift_cols(value, amount):
    if amount == 0:
        return value
    moved = pltpu.roll(value, (-amount) % value.shape[0], 0)
    col = lax.broadcasted_iota(jnp.int32, (value.shape[0], 1), 0) % 8 + amount
    return jnp.where((col >= 0) & (col < 8), moved, 0.0)


def rhs_kernel(scale_ref, pixels_ref, tiles_ref, out_ref, rhs, staged):
    lane = lax.broadcasted_iota(jnp.int32, (1, 128), 1)
    tap_row = lax.broadcasted_iota(jnp.int32, (16, 384), 0)
    tap_lane = lax.broadcasted_iota(jnp.int32, (16, 384), 1)
    spread = (tap_row == (tap_lane // 128) * 3 + (tap_lane % 128) // 40).astype(jnp.bfloat16)
    for c in range(2):
        scale = scale_ref[c]
        pixels = pixels_ref[...].reshape(32, 2, 16, CH)[:, c].reshape(512, CH)
        tiles = jnp.concatenate([tiles_ref[c * 3 + a] for a in range(3)], axis=1)
        taps = jnp.dot(pixels, tiles, preferred_element_type=jnp.float32)
        by_col = shift_rows(taps[:, :128], -16) + taps[:, 128:256] + shift_rows(taps[:, 256:], 16)
        out = shift_cols(by_col, -1)
        out += pltpu.roll(by_col, 88, 1)
        out += shift_cols(pltpu.roll(by_col, 48, 1), 1)
        out = jnp.where(lane < 40, out, 0.0).astype(jnp.bfloat16).astype(jnp.float32) * scale
        moved = shift_cols(out, 1)
        moved += pltpu.roll(out, 40, 1)
        moved += pltpu.roll(shift_cols(out, -1), 80, 1)
        moved = jnp.concatenate([shift_rows(moved, 16), moved, shift_rows(moved, -16)], axis=1)
        cross = lax.dot_general(
            pixels, moved.astype(jnp.bfloat16), (((0,), (0,)), ((), ())), preferred_element_type=jnp.float32
        )
        top = bottom = total = None
        for h in range(32):
            part = jnp.zeros((8, CH), jnp.float32)
            for slot in range(2):
                value = pixels[h * 16 + slot * 8 : h * 16 + slot * 8 + 8].astype(jnp.float32)
                part += value * value
            total = part if total is None else total + part
            if h == 0:
                top = part
            if h == 31:
                bottom = part
        col = lax.broadcasted_iota(jnp.int32, (8, 1), 0)
        diag = []
        for kept in (total - bottom, total, total - top):
            diag.append(jnp.sum(jnp.where(col < 7, kept, 0.0), axis=0, keepdims=True))
            diag.append(jnp.sum(kept, axis=0, keepdims=True))
            diag.append(jnp.sum(jnp.where(col > 0, kept, 0.0), axis=0, keepdims=True))
        diag = jnp.concatenate(diag + [jnp.zeros((7, CH), jnp.float32)], axis=0)
        diag = diag * (scale * (1.0 - keep_off))
        heads = []
        for _ in range(3):
            heads.append(diag.astype(jnp.bfloat16))
            diag = diag - heads[-1].astype(jnp.float32)
        wide = lax.dot_general(
            jnp.concatenate(heads, axis=0), jnp.concatenate([spread] * 3, axis=0),
            (((0,), (0,)), ((), ())), preferred_element_type=jnp.float32,
        )
        value = keep_off * cross + wide * tiles.astype(jnp.float32)
        rhs[...] = value if c == 0 else rhs[...] + value
    zeros = jnp.zeros((2, 128), jnp.float32)
    for part in range(8):
        for dest in range(part * 16, part * 16 + 16):
            for a in range(3):
                staged[dest, pl.ds(a * OWN, OWN), :] = rhs[pl.ds(dest * OWN, OWN), pl.ds(a * 128, 128)]
            staged[dest, pl.ds(30, 2), :] = zeros
        some = pl.ds(part * 16, 16)
        out_ref[some] = staged[some].astype(jnp.bfloat16)


def rhs_part(scale, pixels, tiles):
    whole = pl.BlockSpec(memory_space=pltpu.VMEM)
    return pl.pallas_call(
        rhs_kernel,
        out_shape=jax.ShapeDtypeStruct((128, 32, 128), jnp.bfloat16),
        in_specs=[pl.BlockSpec(memory_space=pltpu.SMEM), pl.BlockSpec((1024, CH), lambda i: (0, 0)), pl.BlockSpec((6, CH, 128), lambda i: (0, 0, 0))],
        grid=(1,),
        out_specs=pl.BlockSpec((128, 32, 128), lambda i: (0, 0, 0)),
        scratch_shapes=[
            pltpu.VMEM((CH, 384), jnp.float32),
            pltpu.VMEM((128, 32, 128), jnp.float32),
        ],
        compiler_params=pltpu.CompilerParams(vmem_limit_bytes=62 * 1024 * 1024),
        cost_estimate=pl.CostEstimate(flops=4_000_000_000, bytes_accessed=8_000_000, transcendentals=0),
        name="rhs_part",
    )(scale, pixels, tiles)


def finish_kernel(sent_ref, after_ref, out_ref, rows):
    del after_ref
    lane = lax.broadcasted_iota(jnp.int32, (1, 128), 1)
    for tile in range(10):
        first = tile * 128 // 40
        last = (tile * 128 + 127) // 40
        values = [jnp.zeros((32, 128), jnp.float32)] * 3
        for b in range(first, last + 1):
            total = jnp.sum(sent_ref[pl.ds(b * 4, 4)].astype(jnp.float32), axis=0)
            start = b * 40 - tile * 128
            keep = (lane >= start) & (lane < start + 40)
            for t in range(3):
                amount = (start - t * 40) % 128
                moved = pltpu.roll(total, amount, 1) if amount else total
                values[t] = jnp.where(keep, moved, values[t])
        for t in range(3):
            rows[pl.ds(t * 32, 32), pl.ds(tile * 128, 128)] = values[t]
    dst = lax.broadcasted_iota(jnp.int32, (MPAD, 96), 0)
    src = lax.broadcasted_iota(jnp.int32, (MPAD, 96), 1)
    inner = src % 32
    pick = (dst == (inner % OWN) * TAPS + (inner // OWN) * 3 + src // 32) & (inner < 30)
    pick = pick.astype(jnp.bfloat16)
    value = rows[...]
    result = None
    for _ in range(3):
        head = value.astype(jnp.bfloat16)
        part = jnp.dot(pick, head, preferred_element_type=jnp.float32)
        result = part if result is None else result + part
        value = value - head.astype(jnp.float32)
    out_ref[...] = result[:90]


def finish(sent, after):
    whole = pl.BlockSpec(memory_space=pltpu.VMEM)
    return pl.pallas_call(
        finish_kernel,
        out_shape=jax.ShapeDtypeStruct((90, CH), jnp.float32),
        in_specs=[whole, pl.BlockSpec(memory_space=pltpu.HBM)],
        out_specs=whole,
        scratch_shapes=[pltpu.VMEM((96, CH), jnp.float32)],
        compiler_params=pltpu.CompilerParams(vmem_limit_bytes=62 * 1024 * 1024),
        name="finish",
    )(sent, after)


def body(activations, sample_count, client_weights):
    client_here = lax.axis_index("client")
    blk_here = lax.axis_index("blk")
    x_hi, core = client_here // 2, client_here % 2
    z, x_lo, y = blk_here // 8, (blk_here // 4) % 2, blk_here % 4
    x = x_hi * 2 + x_lo

    counts = sample_count.astype(jnp.float32)
    all_scale = 1.0 / (8 * counts * 256)
    mine = lax.dynamic_slice_in_dim(sample_count, client_here * 2, 2)
    my_scale = lax.dynamic_slice_in_dim(all_scale, client_here * 2, 2)

    packed = pack(client_weights)

    live = lax.broadcasted_iota(jnp.int32, (2, 2), 1) < mine[:, None]
    first_channel = blk_here * 40 + client_here * OWN
    chan = lax.broadcasted_iota(jnp.int32, (16, CH), 1) - first_channel
    lane = lax.broadcasted_iota(jnp.int32, (16, CH), 0)
    pick = ((chan == lane) & (lane < OWN)).astype(jnp.bfloat16)
    row = lax.broadcasted_iota(jnp.int32, (MPAD, TAPS * 16), 0)
    col = lax.broadcasted_iota(jnp.int32, (MPAD, TAPS * 16), 1)
    order = ((row // TAPS == col % 16) & (row % TAPS == col // 16)).astype(jnp.bfloat16)
    groups = jnp.stack([client_here, client_here ^ 2, client_here ^ 1, client_here ^ 3])
    group_scale = all_scale.reshape(4, 2)[groups]
    img_scale = jnp.repeat(jnp.repeat(group_scale, 16, axis=1)[:, None, :], 32, axis=1).reshape(4, LANES)

    masked = jnp.where(live[:, :, None, None, None], activations, jnp.zeros_like(activations))
    offs = np.array(SOURCES, np.int32)
    src_x, src_y, src_z = (x + offs[:, 0]) % 4, (y + offs[:, 1]) % 4, (z + offs[:, 2]) % 4
    away = (src_x // 2 != x_hi).astype(jnp.int32)
    slots = (away * 32 + src_z * 8 + (src_x % 2) * 4 + src_y).astype(jnp.int32)
    pieces, tiles, early = gather_chips(masked.reshape(ROWS, CH), packed, (pick, order, img_scale, slots))
    pick, order, img_scale, slots = early
    own = assemble(slots, pieces)
    other = lax.ppermute(own, AXES, [(d, d ^ 32) for d in range(128)])

    own_rows = own.reshape(2048, CH)
    part = rhs_part(my_scale, own_rows, tiles)
    sent = lax.all_to_all(part, ("blk", "client"), split_axis=0, concat_axis=0, tiled=True)

    gram_out = gram(
        jnp.reshape(first_channel * TAPS, (1,)), own_rows, other.reshape(2048, CH),
        pick, order, img_scale,
    )
    return gram_out, finish(sent, gram_out)


def solution(mesh):
    in_specs = (P("client", None, "blk", None, None), P(), P("client", "blk", None))
    out_specs = (P(("blk", "client"), None), P(("blk", "client"), None))
    return jax.shard_map(body, mesh=mesh, in_specs=in_specs, out_specs=out_specs, check_vma=False)
```

```python
import jax
import jax.numpy as jnp
import numpy as np
from jax import lax
from jax.experimental import pallas as pl
from jax.experimental.pallas import tpu as pltpu
from jax.sharding import PartitionSpec as P

keep_off = 0.9
AXES = ("client", "blk")
CHIPS = 4
ROWS = 32
CH = 1280
LANES = 1024
TAPS = 9
OWN = 10
MPAD = 96


def split_device(index):
    client, blk = divmod(index, 32)
    x_hi, core = divmod(client, 2)
    z, rest = divmod(blk, 8)
    x_lo, y = divmod(rest, 4)
    return x_hi * 2 + x_lo, y, z, core


def join_device(x, y, z, core):
    return ((x // 2) * 2 + core) * 32 + z * 8 + (x % 2) * 4 + y


def take_from(value, offset):
    pairs = []
    for dst in range(128):
        x, y, z, core = split_device(dst)
        src = join_device((x + offset[0]) % 4, (y + offset[1]) % 4, (z + offset[2]) % 4, core)
        pairs.append((src, dst))
    return lax.ppermute(value, AXES, pairs)


def vec_add(*vectors):
    return tuple(sum(parts) % 4 for parts in zip(*vectors))


STEP = (1, 0, 1)
FIRST = [tuple(k * s % 4 for s in STEP) for k in range(4)]
SECOND = [(0, 0, 0), (1, 1, 3), (0, 2, 0), (3, 3, 1)]
LEVEL = [vec_add(g, f) for g in SECOND for f in FIRST]
LAST = [((1, 0, 0), 0, 8), ((0, 0, 3), 8, 16), ((3, 0, 0), 0, 8), ((0, 0, 1), 8, 16), ((0, 1, 0), 0, 12), ((0, 3, 0), 4, 8)]
SOURCES = list(LEVEL)
for away, low, high in LAST:
    SOURCES += [vec_add(away, o) for o in LEVEL[low:high]]
assert len(SOURCES) == 64 and len(set(SOURCES)) == 64


def gather_chips(block, packed, early):
    tiles = lax.all_to_all(packed, "blk", split_axis=0, concat_axis=0, tiled=True)
    level = jnp.concatenate([block] + [take_from(block, o) for o in FIRST[1:]], axis=0)
    level = jnp.concatenate([level] + [take_from(level, o) for o in SECOND[1:]], axis=0)
    level, tiles = lax.optimization_barrier((level, tiles))
    parts = [level[low * ROWS : high * ROWS] for _, low, high in LAST]
    small = take_from(parts[5], LAST[5][0])
    parts[2], small, early = lax.optimization_barrier((parts[2], small, early))
    pieces = [take_from(part, last[0]) for part, last in zip(parts[:5], LAST)]
    tiles = tiles.reshape(32, 6, 40, 128).transpose(1, 0, 2, 3).reshape(6, CH, 128)
    pieces[0], tiles = lax.optimization_barrier((pieces[0], tiles))
    return [level] + pieces + [small], tiles, early


def assemble_kernel(slots, *refs):
    out = refs[-1]
    spot = 0
    for ref in refs[:-1]:
        for row in range(ref.shape[0] // ROWS):
            out[slots[spot]] = ref[pl.ds(row * ROWS, ROWS), :]
            spot += 1


def assemble(slots, pieces):
    return pl.pallas_call(
        assemble_kernel,
        out_shape=jax.ShapeDtypeStruct((64, ROWS, CH), jnp.bfloat16),
        in_specs=[pl.BlockSpec(memory_space=pltpu.SMEM)] + [pl.BlockSpec(memory_space=pltpu.VMEM)] * 7,
        out_specs=pl.BlockSpec(memory_space=pltpu.VMEM),
        compiler_params=pltpu.CompilerParams(vmem_limit_bytes=16 * 1024 * 1024),
        name="assemble",
    )(slots, *pieces)


def shift_lanes(value, row_off, col_off):
    amount = 32 * row_off + col_off
    moved = pltpu.roll(value, (-amount) % LANES, 1) if amount else value
    lane = lax.broadcasted_iota(jnp.int32, (1, LANES), 1)
    row = lane // 32 + row_off
    col = lane % 8 + col_off
    inside = (row >= 0) & (row < 32) & (col >= 0) & (col < 8)
    return jnp.where(inside, moved, 0.0)


def gram_kernel(first_ref, own_hbm, other_hbm, pick_ref, order_ref, scale_ref, out_ref, left, acc, staged, pixels, sems, loads):
    copies = []
    for group in range(4):
        source = own_hbm if group < 2 else other_hbm
        rows = pl.ds((group % 2) * LANES, LANES)
        target = pixels.at[pl.ds(group * LANES, LANES)]
        copies.append(pltpu.make_async_copy(source.at[rows], target, loads.at[group]))
        copies[-1].start()
    pick = pick_ref[...]
    order = order_ref[...]
    for group in range(4):
        copies[group].wait()
        rows = pixels[pl.ds(group * LANES, LANES), :]
        slab = lax.dot_general(pick, rows, (((1,), (1,)), ((), ())), preferred_element_type=jnp.float32)
        shifted = [shift_lanes(slab, t // 3 - 1, t % 3 - 1) for t in range(TAPS)]
        stacked = jnp.concatenate(shifted, axis=0).astype(jnp.bfloat16)
        patch = jnp.dot(order, stacked, preferred_element_type=jnp.float32)
        patch = patch * scale_ref[pl.ds(group, 1), :]
        for t in range(TAPS):
            left[pl.ds(t * MPAD, MPAD), pl.ds(group * LANES, LANES)] = shift_lanes(
                patch, 1 - t // 3, 1 - t % 3
            ).astype(jnp.bfloat16)

    first = first_ref[0]
    lane = lax.broadcasted_iota(jnp.int32, (MPAD, 128), 1)
    row = lax.broadcasted_iota(jnp.int32, (MPAD, 128), 0)

    def weave(values, part):
        spot = lane + 128 * part
        index = spot // 3
        result = None
        for k in range(3):
            moved = jnp.take_along_axis(values[k], index, axis=1)
            result = moved if result is None else jnp.where(spot % 3 == k, moved, result)
        return result

    def multiply(n):
        lanes = pl.ds(n * 256, 256)

        for m in range(3):
            acc[pl.ds(m * 288, 288), lanes] = jnp.dot(left[pl.ds(m * 288, 288), :], pixels[:, lanes], preferred_element_type=jnp.float32)

    def interleave(block):
        lanes = pl.ds(block * 128, 128)
        inner = [
            [weave([acc[pl.ds((3 * a + b) * MPAD, MPAD), lanes] for a in range(3)], part) for part in range(3)]
            for b in range(3)
        ]
        for tile in range(9):
            value = weave([inner[b][tile // 3] for b in range(3)], tile % 3)
            base = block * 1152 + tile * 128
            value = jnp.where(row + first == lane + base, value, keep_off * value)
            staged[:, pl.ds(base, 128)] = value[:90]

    def send(block):
        wide = pl.ds(block * 1152, 1152)
        pltpu.make_async_copy(staged.at[:, wide], out_ref.at[:, wide], sems.at[block]).start()

    multiply(0)
    for n in range(5):
        if n < 4:
            multiply(n + 1)
        interleave(2 * n)
        interleave(2 * n + 1)
        send(2 * n)
        send(2 * n + 1)

    for block in range(10):
        wide = pl.ds(block * 1152, 1152)
        pltpu.make_async_copy(staged.at[:, wide], out_ref.at[:, wide], sems.at[block]).wait()


def gram(first, own, other, pick, order, scale):
    whole = pl.BlockSpec(memory_space=pltpu.VMEM)
    held = pl.BlockSpec(memory_space=pltpu.HBM)
    return pl.pallas_call(
        gram_kernel,
        out_shape=jax.ShapeDtypeStruct((90, 11520), jnp.float32),
        in_specs=[pl.BlockSpec(memory_space=pltpu.SMEM), held, held] + [whole] * 3,
        out_specs=held,
        scratch_shapes=[
            pltpu.VMEM((TAPS * MPAD, 4 * LANES), jnp.bfloat16),
            pltpu.VMEM((TAPS * MPAD, CH), jnp.float32),
            pltpu.VMEM((90, 11520), jnp.float32),
            pltpu.VMEM((4 * LANES, CH), jnp.bfloat16),
            pltpu.SemaphoreType.DMA((10,)),
            pltpu.SemaphoreType.DMA((4,)),
        ],
        compiler_params=pltpu.CompilerParams(vmem_limit_bytes=58 * 1024 * 1024),
        cost_estimate=pl.CostEstimate(flops=20_000_000_000, bytes_accessed=20_000_000, transcendentals=0),
        name="gram",
    )(first, own, other, pick, order, scale)


def pack_kernel(weights_hbm, out_ref, weights, ordered, loads):
    copies = [pltpu.make_async_copy(weights_hbm.at[c], weights.at[c], loads.at[c]) for c in range(2)]
    for copy in copies:
        copy.start()
    lane = lax.broadcasted_iota(jnp.int32, (1, 128), 1)
    row = lax.broadcasted_iota(jnp.int32, (360, 360), 0)
    col = lax.broadcasted_iota(jnp.int32, (360, 360), 1)
    order = (col == (row % 40) * TAPS + (row // 40) % 3 * 3 + row // 120).astype(jnp.bfloat16)
    for c in range(2):
        copies[c].wait()
        ordered[...] = jnp.dot(order, weights[c], preferred_element_type=jnp.float32)
        for dest in range(32):
            tile, off = divmod(dest * 40, 128)
            total = jnp.zeros((120, 128), jnp.float32)
            for b in range(3):
                rows = pl.ds(b * 120, 120)
                amount = (b * 40 - off) % 128
                value = ordered[rows, pl.ds(tile * 128, 128)]
                value = pltpu.roll(value, amount, 1) if amount else value
                if off + 40 > 128:
                    nxt = ordered[rows, pl.ds(tile * 128 + 128, 128)]
                    nxt = pltpu.roll(nxt, amount, 1) if amount else nxt
                    value = jnp.where(lane < b * 40 + 128 - off, value, nxt)
                total = jnp.where((lane >= b * 40) & (lane < b * 40 + 40), value, total)
            out_ref[dest, pl.ds(c * 120, 120), :] = total.astype(jnp.bfloat16)


def pack(weights):
    return pl.pallas_call(
        pack_kernel,
        out_shape=jax.ShapeDtypeStruct((32, 240, 128), jnp.bfloat16),
        in_specs=[pl.BlockSpec(memory_space=pltpu.HBM)],
        out_specs=pl.BlockSpec(memory_space=pltpu.VMEM),
        scratch_shapes=[
            pltpu.VMEM((2, 360, CH), jnp.bfloat16),
            pltpu.VMEM((360, CH), jnp.float32),
            pltpu.SemaphoreType.DMA((2,)),
        ],
        compiler_params=pltpu.CompilerParams(vmem_limit_bytes=63 * 1024 * 1024),
        cost_estimate=pl.CostEstimate(flops=1_000_000_000, bytes_accessed=6_000_000, transcendentals=0),
        name="pack",
    )(weights)


def shift_rows(value, amount):
    if amount == 0:
        return value
    pad = jnp.zeros((abs(amount), value.shape[1]), value.dtype)
    if amount > 0:
        return jnp.concatenate([value[amount:], pad], axis=0)
    return jnp.concatenate([pad, value[:amount]], axis=0)


def shift_cols(value, amount):
    if amount == 0:
        return value
    moved = pltpu.roll(value, (-amount) % value.shape[0], 0)
    col = lax.broadcasted_iota(jnp.int32, (value.shape[0], 1), 0) % 8 + amount
    return jnp.where((col >= 0) & (col < 8), moved, 0.0)


def rhs_kernel(scale_ref, pixels_ref, tiles_ref, out_ref, rhs, staged):
    lane = lax.broadcasted_iota(jnp.int32, (1, 128), 1)
    tap_row = lax.broadcasted_iota(jnp.int32, (16, 384), 0)
    tap_lane = lax.broadcasted_iota(jnp.int32, (16, 384), 1)
    spread = (tap_row == (tap_lane // 128) * 3 + (tap_lane % 128) // 40).astype(jnp.bfloat16)
    for c in range(2):
        scale = scale_ref[c]
        pixels = pixels_ref[...].reshape(32, 2, 16, CH)[:, c].reshape(512, CH)
        tiles = jnp.concatenate([tiles_ref[c * 3 + a] for a in range(3)], axis=1)
        taps = jnp.dot(pixels, tiles, preferred_element_type=jnp.float32)
        by_col = shift_rows(taps[:, :128], -16) + taps[:, 128:256] + shift_rows(taps[:, 256:], 16)
        out = shift_cols(by_col, -1)
        out += pltpu.roll(by_col, 88, 1)
        out += shift_cols(pltpu.roll(by_col, 48, 1), 1)
        out = jnp.where(lane < 40, out, 0.0).astype(jnp.bfloat16).astype(jnp.float32) * scale
        moved = shift_cols(out, 1)
        moved += pltpu.roll(out, 40, 1)
        moved += pltpu.roll(shift_cols(out, -1), 80, 1)
        moved = jnp.concatenate([shift_rows(moved, 16), moved, shift_rows(moved, -16)], axis=1)
        cross = lax.dot_general(
            pixels, moved.astype(jnp.bfloat16), (((0,), (0,)), ((), ())), preferred_element_type=jnp.float32
        )
        top = bottom = total = None
        for h in range(32):
            part = jnp.zeros((8, CH), jnp.float32)
            for slot in range(2):
                value = pixels[h * 16 + slot * 8 : h * 16 + slot * 8 + 8].astype(jnp.float32)
                part += value * value
            total = part if total is None else total + part
            if h == 0:
                top = part
            if h == 31:
                bottom = part
        col = lax.broadcasted_iota(jnp.int32, (8, 1), 0)
        diag = []
        for kept in (total - bottom, total, total - top):
            diag.append(jnp.sum(jnp.where(col < 7, kept, 0.0), axis=0, keepdims=True))
            diag.append(jnp.sum(kept, axis=0, keepdims=True))
            diag.append(jnp.sum(jnp.where(col > 0, kept, 0.0), axis=0, keepdims=True))
        diag = jnp.concatenate(diag + [jnp.zeros((7, CH), jnp.float32)], axis=0)
        diag = diag * (scale * (1.0 - keep_off))
        heads = []
        for _ in range(3):
            heads.append(diag.astype(jnp.bfloat16))
            diag = diag - heads[-1].astype(jnp.float32)
        wide = lax.dot_general(
            jnp.concatenate(heads, axis=0), jnp.concatenate([spread] * 3, axis=0),
            (((0,), (0,)), ((), ())), preferred_element_type=jnp.float32,
        )
        value = keep_off * cross + wide * tiles.astype(jnp.float32)
        rhs[...] = value if c == 0 else rhs[...] + value
    zeros = jnp.zeros((2, 128), jnp.float32)
    for part in range(8):
        for dest in range(part * 16, part * 16 + 16):
            for a in range(3):
                staged[dest, pl.ds(a * OWN, OWN), :] = rhs[pl.ds(dest * OWN, OWN), pl.ds(a * 128, 128)]
            staged[dest, pl.ds(30, 2), :] = zeros
        some = pl.ds(part * 16, 16)
        out_ref[some] = staged[some].astype(jnp.bfloat16)


def rhs_part(scale, pixels, tiles):
    whole = pl.BlockSpec(memory_space=pltpu.VMEM)
    return pl.pallas_call(
        rhs_kernel,
        out_shape=jax.ShapeDtypeStruct((128, 32, 128), jnp.bfloat16),
        in_specs=[pl.BlockSpec(memory_space=pltpu.SMEM), pl.BlockSpec((1024, CH), lambda i: (0, 0)), pl.BlockSpec((6, CH, 128), lambda i: (0, 0, 0))],
        grid=(1,),
        out_specs=pl.BlockSpec((128, 32, 128), lambda i: (0, 0, 0)),
        scratch_shapes=[
            pltpu.VMEM((CH, 384), jnp.float32),
            pltpu.VMEM((128, 32, 128), jnp.float32),
        ],
        compiler_params=pltpu.CompilerParams(vmem_limit_bytes=62 * 1024 * 1024),
        cost_estimate=pl.CostEstimate(flops=4_000_000_000, bytes_accessed=8_000_000, transcendentals=0),
        name="rhs_part",
    )(scale, pixels, tiles)


def finish_kernel(sent_ref, after_ref, out_ref, rows):
    del after_ref
    lane = lax.broadcasted_iota(jnp.int32, (1, 128), 1)
    for tile in range(10):
        first = tile * 128 // 40
        last = (tile * 128 + 127) // 40
        values = [jnp.zeros((32, 128), jnp.float32)] * 3
        for b in range(first, last + 1):
            total = jnp.sum(sent_ref[pl.ds(b * 4, 4)].astype(jnp.float32), axis=0)
            start = b * 40 - tile * 128
            keep = (lane >= start) & (lane < start + 40)
            for t in range(3):
                amount = (start - t * 40) % 128
                moved = pltpu.roll(total, amount, 1) if amount else total
                values[t] = jnp.where(keep, moved, values[t])
        for t in range(3):
            rows[pl.ds(t * 32, 32), pl.ds(tile * 128, 128)] = values[t]
    dst = lax.broadcasted_iota(jnp.int32, (MPAD, 96), 0)
    src = lax.broadcasted_iota(jnp.int32, (MPAD, 96), 1)
    inner = src % 32
    pick = (dst == (inner % OWN) * TAPS + (inner // OWN) * 3 + src // 32) & (inner < 30)
    pick = pick.astype(jnp.bfloat16)
    value = rows[...]
    result = None
    for _ in range(3):
        head = value.astype(jnp.bfloat16)
        part = jnp.dot(pick, head, preferred_element_type=jnp.float32)
        result = part if result is None else result + part
        value = value - head.astype(jnp.float32)
    out_ref[...] = result[:90]


def finish(sent, after):
    whole = pl.BlockSpec(memory_space=pltpu.VMEM)
    return pl.pallas_call(
        finish_kernel,
        out_shape=jax.ShapeDtypeStruct((90, CH), jnp.float32),
        in_specs=[whole, pl.BlockSpec(memory_space=pltpu.HBM)],
        out_specs=whole,
        scratch_shapes=[pltpu.VMEM((96, CH), jnp.float32)],
        compiler_params=pltpu.CompilerParams(vmem_limit_bytes=57 * 1024 * 1024),
        name="finish",
    )(sent, after)


def body(activations, sample_count, client_weights):
    client_here = lax.axis_index("client")
    blk_here = lax.axis_index("blk")
    x_hi, core = client_here // 2, client_here % 2
    z, x_lo, y = blk_here // 8, (blk_here // 4) % 2, blk_here % 4
    x = x_hi * 2 + x_lo

    counts = sample_count.astype(jnp.float32)
    all_scale = 1.0 / (8 * counts * 256)
    mine = lax.dynamic_slice_in_dim(sample_count, client_here * 2, 2)
    my_scale = lax.dynamic_slice_in_dim(all_scale, client_here * 2, 2)

    packed = pack(client_weights)

    live = lax.broadcasted_iota(jnp.int32, (2, 2), 1) < mine[:, None]
    first_channel = blk_here * 40 + client_here * OWN
    chan = lax.broadcasted_iota(jnp.int32, (16, CH), 1) - first_channel
    lane = lax.broadcasted_iota(jnp.int32, (16, CH), 0)
    pick = ((chan == lane) & (lane < OWN)).astype(jnp.bfloat16)
    row = lax.broadcasted_iota(jnp.int32, (MPAD, TAPS * 16), 0)
    col = lax.broadcasted_iota(jnp.int32, (MPAD, TAPS * 16), 1)
    order = ((row // TAPS == col % 16) & (row % TAPS == col // 16)).astype(jnp.bfloat16)
    groups = jnp.stack([client_here, client_here ^ 2, client_here ^ 1, client_here ^ 3])
    group_scale = all_scale.reshape(4, 2)[groups]
    img_scale = jnp.repeat(jnp.repeat(group_scale, 16, axis=1)[:, None, :], 32, axis=1).reshape(4, LANES)

    masked = jnp.where(live[:, :, None, None, None], activations, jnp.zeros_like(activations))
    offs = np.array(SOURCES, np.int32)
    src_x, src_y, src_z = (x + offs[:, 0]) % 4, (y + offs[:, 1]) % 4, (z + offs[:, 2]) % 4
    away = (src_x // 2 != x_hi).astype(jnp.int32)
    slots = (away * 32 + src_z * 8 + (src_x % 2) * 4 + src_y).astype(jnp.int32)
    pieces, tiles, early = gather_chips(masked.reshape(ROWS, CH), packed, (pick, order, img_scale, slots, my_scale))
    pick, order, img_scale, slots, my_scale = early
    own = assemble(slots, pieces)
    other = lax.ppermute(own, AXES, [(d, d ^ 32) for d in range(128)])

    own_rows = own.reshape(2048, CH)
    part = rhs_part(my_scale, own_rows, tiles)
    sent = lax.all_to_all(part, ("blk", "client"), split_axis=0, concat_axis=0, tiled=True)

    gram_out = gram(
        jnp.reshape(first_channel * TAPS, (1,)), own_rows, other.reshape(2048, CH),
        pick, order, img_scale,
    )
    return gram_out, finish(sent, gram_out)


def solution(mesh):
    in_specs = (P("client", None, "blk", None, None), P(), P("client", "blk", None))
    out_specs = (P(("blk", "client"), None), P(("blk", "client"), None))
    return jax.shard_map(body, mesh=mesh, in_specs=in_specs, out_specs=out_specs, check_vma=False)
```

```python
import jax
import jax.numpy as jnp
import numpy as np
from jax import lax
from jax.experimental import pallas as pl
from jax.experimental.pallas import tpu as pltpu
from jax.sharding import PartitionSpec as P

keep_off = 0.9
AXES = ("client", "blk")
CHIPS = 4
ROWS = 32
CH = 1280
LANES = 1024
TAPS = 9
OWN = 10
MPAD = 96


def split_device(index):
    client, blk = divmod(index, 32)
    x_hi, core = divmod(client, 2)
    z, rest = divmod(blk, 8)
    x_lo, y = divmod(rest, 4)
    return x_hi * 2 + x_lo, y, z, core


def join_device(x, y, z, core):
    return ((x // 2) * 2 + core) * 32 + z * 8 + (x % 2) * 4 + y


def take_from(value, offset):
    pairs = []
    for dst in range(128):
        x, y, z, core = split_device(dst)
        src = join_device((x + offset[0]) % 4, (y + offset[1]) % 4, (z + offset[2]) % 4, core)
        pairs.append((src, dst))
    return lax.ppermute(value, AXES, pairs)


def vec_add(*vectors):
    return tuple(sum(parts) % 4 for parts in zip(*vectors))


STEP = (1, 0, 1)
FIRST = [tuple(k * s % 4 for s in STEP) for k in range(4)]
SECOND = [(0, 0, 0), (1, 1, 3), (0, 2, 0), (3, 3, 1)]
LEVEL = [vec_add(g, f) for g in SECOND for f in FIRST]
LAST = [((1, 0, 0), 0, 8), ((0, 0, 3), 8, 16), ((3, 0, 0), 0, 8), ((0, 0, 1), 8, 16), ((0, 1, 0), 0, 12), ((0, 3, 0), 4, 8)]
SOURCES = list(LEVEL)
for away, low, high in LAST:
    SOURCES += [vec_add(away, o) for o in LEVEL[low:high]]
assert len(SOURCES) == 64 and len(set(SOURCES)) == 64


def gather_chips(block, packed, early):
    tiles = lax.all_to_all(packed, "blk", split_axis=0, concat_axis=0, tiled=True)
    level = jnp.concatenate([block] + [take_from(block, o) for o in FIRST[1:]], axis=0)
    level = jnp.concatenate([level] + [take_from(level, o) for o in SECOND[1:]], axis=0)
    level, tiles = lax.optimization_barrier((level, tiles))
    parts = [level[low * ROWS : high * ROWS] for _, low, high in LAST]
    small = take_from(parts[5], LAST[5][0])
    parts[2], small, early = lax.optimization_barrier((parts[2], small, early))
    pieces = [take_from(part, last[0]) for part, last in zip(parts[:5], LAST)]
    tiles = tiles.reshape(32, 6, 40, 128).transpose(1, 0, 2, 3).reshape(6, CH, 128)
    pieces[0], tiles = lax.optimization_barrier((pieces[0], tiles))
    return [level] + pieces + [small], tiles, early


def assemble_kernel(slots, *refs):
    out = refs[-1]
    spot = 0
    for ref in refs[:-1]:
        for row in range(ref.shape[0] // ROWS):
            out[slots[spot]] = ref[pl.ds(row * ROWS, ROWS), :]
            spot += 1


def assemble(slots, pieces):
    return pl.pallas_call(
        assemble_kernel,
        out_shape=jax.ShapeDtypeStruct((64, ROWS, CH), jnp.bfloat16),
        in_specs=[pl.BlockSpec(memory_space=pltpu.SMEM)] + [pl.BlockSpec(memory_space=pltpu.VMEM)] * 7,
        out_specs=pl.BlockSpec(memory_space=pltpu.VMEM),
        compiler_params=pltpu.CompilerParams(vmem_limit_bytes=16 * 1024 * 1024),
        name="assemble",
    )(slots, *pieces)


def shift_lanes(value, row_off, col_off):
    amount = 32 * row_off + col_off
    moved = pltpu.roll(value, (-amount) % LANES, 1) if amount else value
    lane = lax.broadcasted_iota(jnp.int32, (1, LANES), 1)
    row = lane // 32 + row_off
    col = lane % 8 + col_off
    inside = (row >= 0) & (row < 32) & (col >= 0) & (col < 8)
    return jnp.where(inside, moved, 0.0)


def gram_kernel(first_ref, own_hbm, other_hbm, pick_ref, order_ref, scale_ref, out_ref, left, acc, staged, pixels, sems, loads):
    copies = []
    for group in range(4):
        source = own_hbm if group < 2 else other_hbm
        rows = pl.ds((group % 2) * LANES, LANES)
        target = pixels.at[pl.ds(group * LANES, LANES)]
        copies.append(pltpu.make_async_copy(source.at[rows], target, loads.at[group]))
        copies[-1].start()
    pick = pick_ref[...]
    order = order_ref[...]
    for group in range(4):
        copies[group].wait()
        rows = pixels[pl.ds(group * LANES, LANES), :]
        slab = lax.dot_general(pick, rows, (((1,), (1,)), ((), ())), preferred_element_type=jnp.float32)
        shifted = [shift_lanes(slab, t // 3 - 1, t % 3 - 1) for t in range(TAPS)]
        stacked = jnp.concatenate(shifted, axis=0).astype(jnp.bfloat16)
        patch = jnp.dot(order, stacked, preferred_element_type=jnp.float32)
        patch = patch * scale_ref[pl.ds(group, 1), :]
        for t in range(TAPS):
            left[pl.ds(t * MPAD, MPAD), pl.ds(group * LANES, LANES)] = shift_lanes(
                patch, 1 - t // 3, 1 - t % 3
            ).astype(jnp.bfloat16)

    first = first_ref[0]
    lane = lax.broadcasted_iota(jnp.int32, (MPAD, 128), 1)
    row = lax.broadcasted_iota(jnp.int32, (MPAD, 128), 0)

    def weave(values, part):
        spot = lane + 128 * part
        index = spot // 3
        result = None
        for k in range(3):
            moved = jnp.take_along_axis(values[k], index, axis=1)
            result = moved if result is None else jnp.where(spot % 3 == k, moved, result)
        return result

    def multiply(n):
        lanes = pl.ds(n * 256, 256)

        for m in range(3):
            acc[pl.ds(m * 288, 288), lanes] = jnp.dot(left[pl.ds(m * 288, 288), :], pixels[:, lanes], preferred_element_type=jnp.float32)

    def interleave(block):
        lanes = pl.ds(block * 128, 128)
        inner = [
            [weave([acc[pl.ds((3 * a + b) * MPAD, MPAD), lanes] for a in range(3)], part) for part in range(3)]
            for b in range(3)
        ]
        for tile in range(9):
            value = weave([inner[b][tile // 3] for b in range(3)], tile % 3)
            base = block * 1152 + tile * 128
            value = jnp.where(row + first == lane + base, value, keep_off * value)
            staged[:, pl.ds(base, 128)] = value[:90]

    def send(block):
        wide = pl.ds(block * 1152, 1152)
        pltpu.make_async_copy(staged.at[:, wide], out_ref.at[:, wide], sems.at[block]).start()

    multiply(0)
    for n in range(5):
        if n < 4:
            multiply(n + 1)
        interleave(2 * n)
        interleave(2 * n + 1)
        send(2 * n)
        send(2 * n + 1)

    for block in range(10):
        wide = pl.ds(block * 1152, 1152)
        pltpu.make_async_copy(staged.at[:, wide], out_ref.at[:, wide], sems.at[block]).wait()


def gram(first, own, other, pick, order, scale):
    whole = pl.BlockSpec(memory_space=pltpu.VMEM)
    held = pl.BlockSpec(memory_space=pltpu.HBM)
    return pl.pallas_call(
        gram_kernel,
        out_shape=jax.ShapeDtypeStruct((90, 11520), jnp.float32),
        in_specs=[pl.BlockSpec(memory_space=pltpu.SMEM), held, held] + [whole] * 3,
        out_specs=held,
        scratch_shapes=[
            pltpu.VMEM((TAPS * MPAD, 4 * LANES), jnp.bfloat16),
            pltpu.VMEM((TAPS * MPAD, CH), jnp.float32),
            pltpu.VMEM((90, 11520), jnp.float32),
            pltpu.VMEM((4 * LANES, CH), jnp.bfloat16),
            pltpu.SemaphoreType.DMA((10,)),
            pltpu.SemaphoreType.DMA((4,)),
        ],
        compiler_params=pltpu.CompilerParams(vmem_limit_bytes=58 * 1024 * 1024),
        cost_estimate=pl.CostEstimate(flops=20_000_000_000, bytes_accessed=20_000_000, transcendentals=0),
        name="gram",
    )(first, own, other, pick, order, scale)


def pack_kernel(weights_hbm, out_ref, weights, ordered, loads):
    copies = [pltpu.make_async_copy(weights_hbm.at[c], weights.at[c], loads.at[c]) for c in range(2)]
    for copy in copies:
        copy.start()
    lane = lax.broadcasted_iota(jnp.int32, (1, 128), 1)
    row = lax.broadcasted_iota(jnp.int32, (360, 360), 0)
    col = lax.broadcasted_iota(jnp.int32, (360, 360), 1)
    order = (col == (row % 40) * TAPS + (row // 40) % 3 * 3 + row // 120).astype(jnp.bfloat16)
    for c in range(2):
        copies[c].wait()
        ordered[...] = jnp.dot(order, weights[c], preferred_element_type=jnp.float32)
        for dest in range(32):
            tile, off = divmod(dest * 40, 128)
            total = jnp.zeros((120, 128), jnp.float32)
            for b in range(3):
                rows = pl.ds(b * 120, 120)
                amount = (b * 40 - off) % 128
                value = ordered[rows, pl.ds(tile * 128, 128)]
                value = pltpu.roll(value, amount, 1) if amount else value
                if off + 40 > 128:
                    nxt = ordered[rows, pl.ds(tile * 128 + 128, 128)]
                    nxt = pltpu.roll(nxt, amount, 1) if amount else nxt
                    value = jnp.where(lane < b * 40 + 128 - off, value, nxt)
                total = jnp.where((lane >= b * 40) & (lane < b * 40 + 40), value, total)
            out_ref[dest, pl.ds(c * 120, 120), :] = total.astype(jnp.bfloat16)


def pack(weights):
    return pl.pallas_call(
        pack_kernel,
        out_shape=jax.ShapeDtypeStruct((32, 240, 128), jnp.bfloat16),
        in_specs=[pl.BlockSpec(memory_space=pltpu.HBM)],
        out_specs=pl.BlockSpec(memory_space=pltpu.VMEM),
        scratch_shapes=[
            pltpu.VMEM((2, 360, CH), jnp.bfloat16),
            pltpu.VMEM((360, CH), jnp.float32),
            pltpu.SemaphoreType.DMA((2,)),
        ],
        compiler_params=pltpu.CompilerParams(vmem_limit_bytes=63 * 1024 * 1024),
        cost_estimate=pl.CostEstimate(flops=1_000_000_000, bytes_accessed=6_000_000, transcendentals=0),
        name="pack",
    )(weights)


def shift_rows(value, amount):
    if amount == 0:
        return value
    pad = jnp.zeros((abs(amount), value.shape[1]), value.dtype)
    if amount > 0:
        return jnp.concatenate([value[amount:], pad], axis=0)
    return jnp.concatenate([pad, value[:amount]], axis=0)


def shift_cols(value, amount):
    if amount == 0:
        return value
    moved = pltpu.roll(value, (-amount) % value.shape[0], 0)
    col = lax.broadcasted_iota(jnp.int32, (value.shape[0], 1), 0) % 8 + amount
    return jnp.where((col >= 0) & (col < 8), moved, 0.0)


def rhs_kernel(scale_ref, pixels_ref, tiles_ref, out_ref, rhs, staged):
    lane = lax.broadcasted_iota(jnp.int32, (1, 128), 1)
    tap_row = lax.broadcasted_iota(jnp.int32, (16, 384), 0)
    tap_lane = lax.broadcasted_iota(jnp.int32, (16, 384), 1)
    spread = (tap_row == (tap_lane // 128) * 3 + (tap_lane % 128) // 40).astype(jnp.bfloat16)
    for c in range(2):
        scale = scale_ref[c]
        pixels = pixels_ref[...].reshape(32, 2, 16, CH)[:, c].reshape(512, CH)
        tiles = jnp.concatenate([tiles_ref[c * 3 + a] for a in range(3)], axis=1)
        taps = jnp.dot(pixels, tiles, preferred_element_type=jnp.float32)
        by_col = shift_rows(taps[:, :128], -16) + taps[:, 128:256] + shift_rows(taps[:, 256:], 16)
        out = shift_cols(by_col, -1)
        out += pltpu.roll(by_col, 88, 1)
        out += shift_cols(pltpu.roll(by_col, 48, 1), 1)
        out = jnp.where(lane < 40, out, 0.0).astype(jnp.bfloat16).astype(jnp.float32) * scale
        moved = shift_cols(out, 1)
        moved += pltpu.roll(out, 40, 1)
        moved += pltpu.roll(shift_cols(out, -1), 80, 1)
        moved = jnp.concatenate([shift_rows(moved, 16), moved, shift_rows(moved, -16)], axis=1)
        cross = lax.dot_general(
            pixels, moved.astype(jnp.bfloat16), (((0,), (0,)), ((), ())), preferred_element_type=jnp.float32
        )
        top = bottom = total = None
        for h in range(32):
            part = jnp.zeros((8, CH), jnp.float32)
            for slot in range(2):
                value = pixels[h * 16 + slot * 8 : h * 16 + slot * 8 + 8].astype(jnp.float32)
                part += value * value
            total = part if total is None else total + part
            if h == 0:
                top = part
            if h == 31:
                bottom = part
        col = lax.broadcasted_iota(jnp.int32, (8, 1), 0)
        diag = []
        for kept in (total - bottom, total, total - top):
            diag.append(jnp.sum(jnp.where(col < 7, kept, 0.0), axis=0, keepdims=True))
            diag.append(jnp.sum(kept, axis=0, keepdims=True))
            diag.append(jnp.sum(jnp.where(col > 0, kept, 0.0), axis=0, keepdims=True))
        diag = jnp.concatenate(diag + [jnp.zeros((7, CH), jnp.float32)], axis=0)
        diag = diag * (scale * (1.0 - keep_off))
        heads = []
        for _ in range(3):
            heads.append(diag.astype(jnp.bfloat16))
            diag = diag - heads[-1].astype(jnp.float32)
        wide = lax.dot_general(
            jnp.concatenate(heads, axis=0), jnp.concatenate([spread] * 3, axis=0),
            (((0,), (0,)), ((), ())), preferred_element_type=jnp.float32,
        )
        value = keep_off * cross + wide * tiles.astype(jnp.float32)
        rhs[...] = value if c == 0 else rhs[...] + value
    zeros = jnp.zeros((2, 128), jnp.float32)
    for part in range(8):
        for dest in range(part * 16, part * 16 + 16):
            for a in range(3):
                staged[dest, pl.ds(a * OWN, OWN), :] = rhs[pl.ds(dest * OWN, OWN), pl.ds(a * 128, 128)]
            staged[dest, pl.ds(30, 2), :] = zeros
        some = pl.ds(part * 16, 16)
        out_ref[some] = staged[some].astype(jnp.bfloat16)


def rhs_part(scale, pixels, tiles):
    whole = pl.BlockSpec(memory_space=pltpu.VMEM)
    return pl.pallas_call(
        rhs_kernel,
        out_shape=jax.ShapeDtypeStruct((128, 32, 128), jnp.bfloat16),
        in_specs=[pl.BlockSpec(memory_space=pltpu.SMEM), pl.BlockSpec((1024, CH), lambda i: (0, 0)), pl.BlockSpec((6, CH, 128), lambda i: (0, 0, 0))],
        grid=(1,),
        out_specs=pl.BlockSpec((128, 32, 128), lambda i: (0, 0, 0)),
        scratch_shapes=[
            pltpu.VMEM((CH, 384), jnp.float32),
            pltpu.VMEM((128, 32, 128), jnp.float32),
        ],
        compiler_params=pltpu.CompilerParams(vmem_limit_bytes=62 * 1024 * 1024),
        cost_estimate=pl.CostEstimate(flops=4_000_000_000, bytes_accessed=8_000_000, transcendentals=0),
        name="rhs_part",
    )(scale, pixels, tiles)


def finish_kernel(sent_ref, after_ref, out_ref, rows):
    del after_ref
    lane = lax.broadcasted_iota(jnp.int32, (1, 128), 1)
    for tile in range(10):
        first = tile * 128 // 40
        last = (tile * 128 + 127) // 40
        values = [jnp.zeros((32, 128), jnp.float32)] * 3
        for b in range(first, last + 1):
            total = jnp.sum(sent_ref[pl.ds(b * 4, 4)].astype(jnp.float32), axis=0)
            start = b * 40 - tile * 128
            keep = (lane >= start) & (lane < start + 40)
            for t in range(3):
                amount = (start - t * 40) % 128
                moved = pltpu.roll(total, amount, 1) if amount else total
                values[t] = jnp.where(keep, moved, values[t])
        for t in range(3):
            rows[pl.ds(t * 32, 32), pl.ds(tile * 128, 128)] = values[t]
    dst = lax.broadcasted_iota(jnp.int32, (MPAD, 96), 0)
    src = lax.broadcasted_iota(jnp.int32, (MPAD, 96), 1)
    inner = src % 32
    pick = (dst == (inner % OWN) * TAPS + (inner // OWN) * 3 + src // 32) & (inner < 30)
    pick = pick.astype(jnp.bfloat16)
    value = rows[...]
    result = None
    for _ in range(3):
        head = value.astype(jnp.bfloat16)
        part = jnp.dot(pick, head, preferred_element_type=jnp.float32)
        result = part if result is None else result + part
        value = value - head.astype(jnp.float32)
    out_ref[...] = result[:90]


def finish(sent, after):
    whole = pl.BlockSpec(memory_space=pltpu.VMEM)
    return pl.pallas_call(
        finish_kernel,
        out_shape=jax.ShapeDtypeStruct((90, CH), jnp.float32),
        in_specs=[whole, pl.BlockSpec(memory_space=pltpu.HBM)],
        out_specs=whole,
        scratch_shapes=[pltpu.VMEM((96, CH), jnp.float32)],
        compiler_params=pltpu.CompilerParams(vmem_limit_bytes=50 * 1024 * 1024),
        name="finish",
    )(sent, after)


def body(activations, sample_count, client_weights):
    client_here = lax.axis_index("client")
    blk_here = lax.axis_index("blk")
    x_hi, core = client_here // 2, client_here % 2
    z, x_lo, y = blk_here // 8, (blk_here // 4) % 2, blk_here % 4
    x = x_hi * 2 + x_lo

    counts = sample_count.astype(jnp.float32)
    all_scale = 1.0 / (8 * counts * 256)
    mine = lax.dynamic_slice_in_dim(sample_count, client_here * 2, 2)
    my_scale = lax.dynamic_slice_in_dim(all_scale, client_here * 2, 2)

    packed = pack(client_weights)

    live = lax.broadcasted_iota(jnp.int32, (2, 2), 1) < mine[:, None]
    first_channel = blk_here * 40 + client_here * OWN
    chan = lax.broadcasted_iota(jnp.int32, (16, CH), 1) - first_channel
    lane = lax.broadcasted_iota(jnp.int32, (16, CH), 0)
    pick = ((chan == lane) & (lane < OWN)).astype(jnp.bfloat16)
    row = lax.broadcasted_iota(jnp.int32, (MPAD, TAPS * 16), 0)
    col = lax.broadcasted_iota(jnp.int32, (MPAD, TAPS * 16), 1)
    order = ((row // TAPS == col % 16) & (row % TAPS == col // 16)).astype(jnp.bfloat16)
    groups = jnp.stack([client_here, client_here ^ 2, client_here ^ 1, client_here ^ 3])
    group_scale = all_scale.reshape(4, 2)[groups]
    img_scale = jnp.repeat(jnp.repeat(group_scale, 16, axis=1)[:, None, :], 32, axis=1).reshape(4, LANES)

    masked = jnp.where(live[:, :, None, None, None], activations, jnp.zeros_like(activations))
    offs = np.array(SOURCES, np.int32)
    src_x, src_y, src_z = (x + offs[:, 0]) % 4, (y + offs[:, 1]) % 4, (z + offs[:, 2]) % 4
    away = (src_x // 2 != x_hi).astype(jnp.int32)
    slots = (away * 32 + src_z * 8 + (src_x % 2) * 4 + src_y).astype(jnp.int32)
    pieces, tiles, early = gather_chips(masked.reshape(ROWS, CH), packed, (pick, order, img_scale, slots, my_scale))
    pick, order, img_scale, slots, my_scale = early
    own = assemble(slots, pieces)
    other = lax.ppermute(own, AXES, [(d, d ^ 32) for d in range(128)])

    own_rows = own.reshape(2048, CH)
    part = rhs_part(my_scale, own_rows, tiles)
    sent = lax.all_to_all(part, ("blk", "client"), split_axis=0, concat_axis=0, tiled=True)

    gram_out = gram(
        jnp.reshape(first_channel * TAPS, (1,)), own_rows, other.reshape(2048, CH),
        pick, order, img_scale,
    )
    return gram_out, finish(sent, gram_out)


def solution(mesh):
    in_specs = (P("client", None, "blk", None, None), P(), P("client", "blk", None))
    out_specs = (P(("blk", "client"), None), P(("blk", "client"), None))
    return jax.shard_map(body, mesh=mesh, in_specs=in_specs, out_specs=out_specs, check_vma=False)
```

```python
import jax
import jax.numpy as jnp
import numpy as np
from jax import lax
from jax.experimental import pallas as pl
from jax.experimental.pallas import tpu as pltpu
from jax.sharding import PartitionSpec as P

keep_off = 0.9
AXES = ("client", "blk")
CHIPS = 4
ROWS = 32
CH = 1280
LANES = 1024
TAPS = 9
OWN = 10
MPAD = 96


def split_device(index):
    client, blk = divmod(index, 32)
    x_hi, core = divmod(client, 2)
    z, rest = divmod(blk, 8)
    x_lo, y = divmod(rest, 4)
    return x_hi * 2 + x_lo, y, z, core


def join_device(x, y, z, core):
    return ((x // 2) * 2 + core) * 32 + z * 8 + (x % 2) * 4 + y


def take_from(value, offset):
    pairs = []
    for dst in range(128):
        x, y, z, core = split_device(dst)
        src = join_device((x + offset[0]) % 4, (y + offset[1]) % 4, (z + offset[2]) % 4, core)
        pairs.append((src, dst))
    return lax.ppermute(value, AXES, pairs)


def vec_add(*vectors):
    return tuple(sum(parts) % 4 for parts in zip(*vectors))


STEP = (1, 0, 1)
FIRST = [tuple(k * s % 4 for s in STEP) for k in range(4)]
SECOND = [(0, 0, 0), (1, 1, 3), (0, 2, 0), (3, 3, 1)]
LEVEL = [vec_add(g, f) for g in SECOND for f in FIRST]
LAST = [((1, 0, 0), 0, 8), ((0, 0, 3), 8, 16), ((3, 0, 0), 0, 8), ((0, 0, 1), 8, 16), ((0, 1, 0), 0, 11), ((0, 3, 0), 3, 8)]
SOURCES = list(LEVEL)
for away, low, high in LAST:
    SOURCES += [vec_add(away, o) for o in LEVEL[low:high]]
assert len(SOURCES) == 64 and len(set(SOURCES)) == 64


def gather_chips(block, packed, early):
    tiles = lax.all_to_all(packed, "blk", split_axis=0, concat_axis=0, tiled=True)
    level = jnp.concatenate([block] + [take_from(block, o) for o in FIRST[1:]], axis=0)
    level = jnp.concatenate([level] + [take_from(level, o) for o in SECOND[1:]], axis=0)
    level, tiles = lax.optimization_barrier((level, tiles))
    parts = [level[low * ROWS : high * ROWS] for _, low, high in LAST]
    small = take_from(parts[5], LAST[5][0])
    parts[2], small, early = lax.optimization_barrier((parts[2], small, early))
    pieces = [take_from(part, last[0]) for part, last in zip(parts[:5], LAST)]
    tiles = tiles.reshape(32, 6, 40, 128).transpose(1, 0, 2, 3).reshape(6, CH, 128)
    pieces[0], tiles = lax.optimization_barrier((pieces[0], tiles))
    return [level] + pieces + [small], tiles, early


def assemble_kernel(slots, *refs):
    out = refs[-1]
    spot = 0
    for ref in refs[:-1]:
        for row in range(ref.shape[0] // ROWS):
            out[slots[spot]] = ref[pl.ds(row * ROWS, ROWS), :]
            spot += 1


def assemble(slots, pieces):
    return pl.pallas_call(
        assemble_kernel,
        out_shape=jax.ShapeDtypeStruct((64, ROWS, CH), jnp.bfloat16),
        in_specs=[pl.BlockSpec(memory_space=pltpu.SMEM)] + [pl.BlockSpec(memory_space=pltpu.VMEM)] * 7,
        out_specs=pl.BlockSpec(memory_space=pltpu.VMEM),
        compiler_params=pltpu.CompilerParams(vmem_limit_bytes=16 * 1024 * 1024),
        name="assemble",
    )(slots, *pieces)


def shift_lanes(value, row_off, col_off):
    amount = 32 * row_off + col_off
    moved = pltpu.roll(value, (-amount) % LANES, 1) if amount else value
    lane = lax.broadcasted_iota(jnp.int32, (1, LANES), 1)
    row = lane // 32 + row_off
    col = lane % 8 + col_off
    inside = (row >= 0) & (row < 32) & (col >= 0) & (col < 8)
    return jnp.where(inside, moved, 0.0)


def gram_kernel(first_ref, own_hbm, other_hbm, pick_ref, order_ref, scale_ref, out_ref, left, acc, staged, pixels, sems, loads):
    copies = []
    for group in range(4):
        source = own_hbm if group < 2 else other_hbm
        rows = pl.ds((group % 2) * LANES, LANES)
        target = pixels.at[pl.ds(group * LANES, LANES)]
        copies.append(pltpu.make_async_copy(source.at[rows], target, loads.at[group]))
        copies[-1].start()
    pick = pick_ref[...]
    order = order_ref[...]
    for group in range(4):
        copies[group].wait()
        rows = pixels[pl.ds(group * LANES, LANES), :]
        slab = lax.dot_general(pick, rows, (((1,), (1,)), ((), ())), preferred_element_type=jnp.float32)
        shifted = [shift_lanes(slab, t // 3 - 1, t % 3 - 1) for t in range(TAPS)]
        stacked = jnp.concatenate(shifted, axis=0).astype(jnp.bfloat16)
        patch = jnp.dot(order, stacked, preferred_element_type=jnp.float32)
        patch = patch * scale_ref[pl.ds(group, 1), :]
        for t in range(TAPS):
            left[pl.ds(t * MPAD, MPAD), pl.ds(group * LANES, LANES)] = shift_lanes(
                patch, 1 - t // 3, 1 - t % 3
            ).astype(jnp.bfloat16)

    first = first_ref[0]
    lane = lax.broadcasted_iota(jnp.int32, (MPAD, 128), 1)
    row = lax.broadcasted_iota(jnp.int32, (MPAD, 128), 0)

    def weave(values, part):
        spot = lane + 128 * part
        index = spot // 3
        result = None
        for k in range(3):
            moved = jnp.take_along_axis(values[k], index, axis=1)
            result = moved if result is None else jnp.where(spot % 3 == k, moved, result)
        return result

    def multiply(n):
        lanes = pl.ds(n * 256, 256)

        for m in range(6):
            acc[pl.ds(m * 144, 144), lanes] = jnp.dot(left[pl.ds(m * 144, 144), :], pixels[:, lanes], preferred_element_type=jnp.float32)

    def interleave(block):
        lanes = pl.ds(block * 128, 128)
        inner = [
            [weave([acc[pl.ds((3 * a + b) * MPAD, MPAD), lanes] for a in range(3)], part) for part in range(3)]
            for b in range(3)
        ]
        for tile in range(9):
            value = weave([inner[b][tile // 3] for b in range(3)], tile % 3)
            base = block * 1152 + tile * 128
            value = jnp.where(row + first == lane + base, value, keep_off * value)
            staged[:, pl.ds(base, 128)] = value[:90]

    def send(block):
        wide = pl.ds(block * 1152, 1152)
        pltpu.make_async_copy(staged.at[:, wide], out_ref.at[:, wide], sems.at[block]).start()

    multiply(0)
    for n in range(5):
        if n < 4:
            multiply(n + 1)
        interleave(2 * n)
        interleave(2 * n + 1)
        send(2 * n)
        send(2 * n + 1)

    for block in range(10):
        wide = pl.ds(block * 1152, 1152)
        pltpu.make_async_copy(staged.at[:, wide], out_ref.at[:, wide], sems.at[block]).wait()


def gram(first, own, other, pick, order, scale):
    whole = pl.BlockSpec(memory_space=pltpu.VMEM)
    held = pl.BlockSpec(memory_space=pltpu.HBM)
    return pl.pallas_call(
        gram_kernel,
        out_shape=jax.ShapeDtypeStruct((90, 11520), jnp.float32),
        in_specs=[pl.BlockSpec(memory_space=pltpu.SMEM), held, held] + [whole] * 3,
        out_specs=held,
        scratch_shapes=[
            pltpu.VMEM((TAPS * MPAD, 4 * LANES), jnp.bfloat16),
            pltpu.VMEM((TAPS * MPAD, CH), jnp.float32),
            pltpu.VMEM((90, 11520), jnp.float32),
            pltpu.VMEM((4 * LANES, CH), jnp.bfloat16),
            pltpu.SemaphoreType.DMA((10,)),
            pltpu.SemaphoreType.DMA((4,)),
        ],
        compiler_params=pltpu.CompilerParams(vmem_limit_bytes=58 * 1024 * 1024),
        cost_estimate=pl.CostEstimate(flops=20_000_000_000, bytes_accessed=20_000_000, transcendentals=0),
        name="gram",
    )(first, own, other, pick, order, scale)


def pack_kernel(weights_hbm, out_ref, weights, ordered, loads):
    copies = [pltpu.make_async_copy(weights_hbm.at[c], weights.at[c], loads.at[c]) for c in range(2)]
    for copy in copies:
        copy.start()
    lane = lax.broadcasted_iota(jnp.int32, (1, 128), 1)
    row = lax.broadcasted_iota(jnp.int32, (360, 360), 0)
    col = lax.broadcasted_iota(jnp.int32, (360, 360), 1)
    order = (col == (row % 40) * TAPS + (row // 40) % 3 * 3 + row // 120).astype(jnp.bfloat16)
    for c in range(2):
        copies[c].wait()
        ordered[...] = jnp.dot(order, weights[c], preferred_element_type=jnp.float32)
        for dest in range(32):
            tile, off = divmod(dest * 40, 128)
            total = jnp.zeros((120, 128), jnp.float32)
            for b in range(3):
                rows = pl.ds(b * 120, 120)
                amount = (b * 40 - off) % 128
                value = ordered[rows, pl.ds(tile * 128, 128)]
                value = pltpu.roll(value, amount, 1) if amount else value
                if off + 40 > 128:
                    nxt = ordered[rows, pl.ds(tile * 128 + 128, 128)]
                    nxt = pltpu.roll(nxt, amount, 1) if amount else nxt
                    value = jnp.where(lane < b * 40 + 128 - off, value, nxt)
                total = jnp.where((lane >= b * 40) & (lane < b * 40 + 40), value, total)
            out_ref[dest, pl.ds(c * 120, 120), :] = total.astype(jnp.bfloat16)


def pack(weights):
    return pl.pallas_call(
        pack_kernel,
        out_shape=jax.ShapeDtypeStruct((32, 240, 128), jnp.bfloat16),
        in_specs=[pl.BlockSpec(memory_space=pltpu.HBM)],
        out_specs=pl.BlockSpec(memory_space=pltpu.VMEM),
        scratch_shapes=[
            pltpu.VMEM((2, 360, CH), jnp.bfloat16),
            pltpu.VMEM((360, CH), jnp.float32),
            pltpu.SemaphoreType.DMA((2,)),
        ],
        compiler_params=pltpu.CompilerParams(vmem_limit_bytes=63 * 1024 * 1024),
        cost_estimate=pl.CostEstimate(flops=1_000_000_000, bytes_accessed=6_000_000, transcendentals=0),
        name="pack",
    )(weights)


def shift_rows(value, amount):
    if amount == 0:
        return value
    pad = jnp.zeros((abs(amount), value.shape[1]), value.dtype)
    if amount > 0:
        return jnp.concatenate([value[amount:], pad], axis=0)
    return jnp.concatenate([pad, value[:amount]], axis=0)


def shift_cols(value, amount):
    if amount == 0:
        return value
    moved = pltpu.roll(value, (-amount) % value.shape[0], 0)
    col = lax.broadcasted_iota(jnp.int32, (value.shape[0], 1), 0) % 8 + amount
    return jnp.where((col >= 0) & (col < 8), moved, 0.0)


def rhs_kernel(scale_ref, pixels_ref, tiles_ref, out_ref, rhs, staged):
    lane = lax.broadcasted_iota(jnp.int32, (1, 128), 1)
    tap_row = lax.broadcasted_iota(jnp.int32, (16, 384), 0)
    tap_lane = lax.broadcasted_iota(jnp.int32, (16, 384), 1)
    spread = (tap_row == (tap_lane // 128) * 3 + (tap_lane % 128) // 40).astype(jnp.bfloat16)
    for c in range(2):
        scale = scale_ref[c]
        pixels = pixels_ref[...].reshape(32, 2, 16, CH)[:, c].reshape(512, CH)
        tiles = jnp.concatenate([tiles_ref[c * 3 + a] for a in range(3)], axis=1)
        taps = jnp.dot(pixels, tiles, preferred_element_type=jnp.float32)
        by_col = shift_rows(taps[:, :128], -16) + taps[:, 128:256] + shift_rows(taps[:, 256:], 16)
        out = shift_cols(by_col, -1)
        out += pltpu.roll(by_col, 88, 1)
        out += shift_cols(pltpu.roll(by_col, 48, 1), 1)
        out = jnp.where(lane < 40, out, 0.0).astype(jnp.bfloat16).astype(jnp.float32) * scale
        moved = shift_cols(out, 1)
        moved += pltpu.roll(out, 40, 1)
        moved += pltpu.roll(shift_cols(out, -1), 80, 1)
        moved = jnp.concatenate([shift_rows(moved, 16), moved, shift_rows(moved, -16)], axis=1)
        cross = lax.dot_general(
            pixels, moved.astype(jnp.bfloat16), (((0,), (0,)), ((), ())), preferred_element_type=jnp.float32
        )
        top = bottom = total = None
        for h in range(32):
            part = jnp.zeros((8, CH), jnp.float32)
            for slot in range(2):
                value = pixels[h * 16 + slot * 8 : h * 16 + slot * 8 + 8].astype(jnp.float32)
                part += value * value
            total = part if total is None else total + part
            if h == 0:
                top = part
            if h == 31:
                bottom = part
        col = lax.broadcasted_iota(jnp.int32, (8, 1), 0)
        diag = []
        for kept in (total - bottom, total, total - top):
            diag.append(jnp.sum(jnp.where(col < 7, kept, 0.0), axis=0, keepdims=True))
            diag.append(jnp.sum(kept, axis=0, keepdims=True))
            diag.append(jnp.sum(jnp.where(col > 0, kept, 0.0), axis=0, keepdims=True))
        diag = jnp.concatenate(diag + [jnp.zeros((7, CH), jnp.float32)], axis=0)
        diag = diag * (scale * (1.0 - keep_off))
        heads = []
        for _ in range(3):
            heads.append(diag.astype(jnp.bfloat16))
            diag = diag - heads[-1].astype(jnp.float32)
        wide = lax.dot_general(
            jnp.concatenate(heads, axis=0), jnp.concatenate([spread] * 3, axis=0),
            (((0,), (0,)), ((), ())), preferred_element_type=jnp.float32,
        )
        value = keep_off * cross + wide * tiles.astype(jnp.float32)
        rhs[...] = value if c == 0 else rhs[...] + value
    zeros = jnp.zeros((2, 128), jnp.float32)
    for part in range(8):
        for dest in range(part * 16, part * 16 + 16):
            for a in range(3):
                staged[dest, pl.ds(a * OWN, OWN), :] = rhs[pl.ds(dest * OWN, OWN), pl.ds(a * 128, 128)]
            staged[dest, pl.ds(30, 2), :] = zeros
        some = pl.ds(part * 16, 16)
        out_ref[some] = staged[some].astype(jnp.bfloat16)


def rhs_part(scale, pixels, tiles):
    whole = pl.BlockSpec(memory_space=pltpu.VMEM)
    return pl.pallas_call(
        rhs_kernel,
        out_shape=jax.ShapeDtypeStruct((128, 32, 128), jnp.bfloat16),
        in_specs=[pl.BlockSpec(memory_space=pltpu.SMEM), pl.BlockSpec((1024, CH), lambda i: (0, 0)), pl.BlockSpec((6, CH, 128), lambda i: (0, 0, 0))],
        grid=(1,),
        out_specs=pl.BlockSpec((128, 32, 128), lambda i: (0, 0, 0)),
        scratch_shapes=[
            pltpu.VMEM((CH, 384), jnp.float32),
            pltpu.VMEM((128, 32, 128), jnp.float32),
        ],
        compiler_params=pltpu.CompilerParams(vmem_limit_bytes=62 * 1024 * 1024),
        cost_estimate=pl.CostEstimate(flops=4_000_000_000, bytes_accessed=8_000_000, transcendentals=0),
        name="rhs_part",
    )(scale, pixels, tiles)


def finish_kernel(sent_ref, after_ref, out_ref, rows):
    del after_ref
    lane = lax.broadcasted_iota(jnp.int32, (1, 128), 1)
    for tile in range(10):
        first = tile * 128 // 40
        last = (tile * 128 + 127) // 40
        values = [jnp.zeros((32, 128), jnp.float32)] * 3
        for b in range(first, last + 1):
            total = jnp.sum(sent_ref[pl.ds(b * 4, 4)].astype(jnp.float32), axis=0)
            start = b * 40 - tile * 128
            keep = (lane >= start) & (lane < start + 40)
            for t in range(3):
                amount = (start - t * 40) % 128
                moved = pltpu.roll(total, amount, 1) if amount else total
                values[t] = jnp.where(keep, moved, values[t])
        for t in range(3):
            rows[pl.ds(t * 32, 32), pl.ds(tile * 128, 128)] = values[t]
    dst = lax.broadcasted_iota(jnp.int32, (MPAD, 96), 0)
    src = lax.broadcasted_iota(jnp.int32, (MPAD, 96), 1)
    inner = src % 32
    pick = (dst == (inner % OWN) * TAPS + (inner // OWN) * 3 + src // 32) & (inner < 30)
    pick = pick.astype(jnp.bfloat16)
    value = rows[...]
    result = None
    for _ in range(3):
        head = value.astype(jnp.bfloat16)
        part = jnp.dot(pick, head, preferred_element_type=jnp.float32)
        result = part if result is None else result + part
        value = value - head.astype(jnp.float32)
    out_ref[...] = result[:90]


def finish(sent, after):
    whole = pl.BlockSpec(memory_space=pltpu.VMEM)
    return pl.pallas_call(
        finish_kernel,
        out_shape=jax.ShapeDtypeStruct((90, CH), jnp.float32),
        in_specs=[whole, pl.BlockSpec(memory_space=pltpu.HBM)],
        out_specs=whole,
        scratch_shapes=[pltpu.VMEM((96, CH), jnp.float32)],
        compiler_params=pltpu.CompilerParams(vmem_limit_bytes=50 * 1024 * 1024),
        name="finish",
    )(sent, after)


def body(activations, sample_count, client_weights):
    client_here = lax.axis_index("client")
    blk_here = lax.axis_index("blk")
    x_hi, core = client_here // 2, client_here % 2
    z, x_lo, y = blk_here // 8, (blk_here // 4) % 2, blk_here % 4
    x = x_hi * 2 + x_lo

    counts = sample_count.astype(jnp.float32)
    all_scale = 1.0 / (8 * counts * 256)
    mine = lax.dynamic_slice_in_dim(sample_count, client_here * 2, 2)
    my_scale = lax.dynamic_slice_in_dim(all_scale, client_here * 2, 2)

    packed = pack(client_weights)

    live = lax.broadcasted_iota(jnp.int32, (2, 2), 1) < mine[:, None]
    first_channel = blk_here * 40 + client_here * OWN
    chan = lax.broadcasted_iota(jnp.int32, (16, CH), 1) - first_channel
    lane = lax.broadcasted_iota(jnp.int32, (16, CH), 0)
    pick = ((chan == lane) & (lane < OWN)).astype(jnp.bfloat16)
    row = lax.broadcasted_iota(jnp.int32, (MPAD, TAPS * 16), 0)
    col = lax.broadcasted_iota(jnp.int32, (MPAD, TAPS * 16), 1)
    order = ((row // TAPS == col % 16) & (row % TAPS == col // 16)).astype(jnp.bfloat16)
    groups = jnp.stack([client_here, client_here ^ 2, client_here ^ 1, client_here ^ 3])
    group_scale = all_scale.reshape(4, 2)[groups]
    img_scale = jnp.repeat(jnp.repeat(group_scale, 16, axis=1)[:, None, :], 32, axis=1).reshape(4, LANES)

    masked = jnp.where(live[:, :, None, None, None], activations, jnp.zeros_like(activations))
    offs = np.array(SOURCES, np.int32)
    src_x, src_y, src_z = (x + offs[:, 0]) % 4, (y + offs[:, 1]) % 4, (z + offs[:, 2]) % 4
    away = (src_x // 2 != x_hi).astype(jnp.int32)
    slots = (away * 32 + src_z * 8 + (src_x % 2) * 4 + src_y).astype(jnp.int32)
    pieces, tiles, early = gather_chips(masked.reshape(ROWS, CH), packed, (pick, order, img_scale, slots, my_scale))
    pick, order, img_scale, slots, my_scale = early
    own = assemble(slots, pieces)
    other = lax.ppermute(own, AXES, [(d, d ^ 32) for d in range(128)])

    own_rows = own.reshape(2048, CH)
    part = rhs_part(my_scale, own_rows, tiles)
    sent = lax.all_to_all(part, ("blk", "client"), split_axis=0, concat_axis=0, tiled=True)

    gram_out = gram(
        jnp.reshape(first_channel * TAPS, (1,)), own_rows, other.reshape(2048, CH),
        pick, order, img_scale,
    )
    return gram_out, finish(sent, gram_out)


def solution(mesh):
    in_specs = (P("client", None, "blk", None, None), P(), P("client", "blk", None))
    out_specs = (P(("blk", "client"), None), P(("blk", "client"), None))
    return jax.shard_map(body, mesh=mesh, in_specs=in_specs, out_specs=out_specs, check_vma=False)
```
